32 devices in a mesh: tp: 4 (over y, x), ep: 8 (over z, core).
Axes of the slice: x: 2, y: 2, z: 4, core: 2. Of those that a mesh axis runs over, the one named last changes fastest.
Arguments:
- tokens: bfloat16 [16, 1024, 1024], P('ep', 'tp'), may hold values from -6 to 6
- cotangent: bfloat16 [16, 1024, 1024], P('ep', 'tp'), may hold values from -6 to 6
- norm_gains: float32 [2, 1024], replicated, may hold values from 0.5 to 1.5
- query_key_value_weight: bfloat16 [1024, 8, 256], P('ep', 'tp'), may hold values from -0.625 to 0.625
- output_weight: bfloat16 [8, 128, 1024], P('tp', None, 'ep'), may hold values from -3 to 3
- w_router: bfloat16 [1024, 32], replicated, may hold values from -0.09375 to 0.09375
- w_gate_up: bfloat16 [32, 1024, 1024], P('ep', 'tp'), may hold values from -0.1875 to 0.1875
- w_down: bfloat16 [32, 512, 1024], P('ep', None, 'tp'), may hold values from -3 to 3
- segment_ids: int32 [16, 1024], P('ep'), may hold values from 0 to 3, never falling along the last dimension, each value on 1 to 512 neighbouring positions
- routes: int32 [16, 4, 256, 8], P('ep', 'tp'), may hold values from 0 to 31, all different within a row; in each aligned block of 256 rows (0 to 255, 256 to 511, ..., all dimensions but the last counted through in order) at most 96 rows name the same one
Outputs:
- output: bfloat16 [16, 1024, 1024], P('ep', 'tp')
- input_grad: float32 [16, 1024, 1024], P('ep', 'tp')
- grad_gains: float32 [2, 1024], P(None, ('tp', 'ep'))
- grad_qkv: float32 [1024, 8, 256], P('ep', 'tp')
- grad_out: float32 [8, 128, 1024], P('tp', None, 'ep')
- grad_router: float32 [1024, 32], P(('tp', 'ep'))
- grad_gate_up: float32 [32, 1024, 1024], P('ep', 'tp')
- grad_down: float32 [32, 512, 1024], P('ep', None, 'tp')
The draws below stay inside these ranges and needn't reach their ends.
Inputs may be any that keep to these rules, and one draw needn't show every extreme that they name: `routes`: each row names 8 different experts; in each aligned block of 256 rows (one device's tokens of one micro-batch) no expert is named more than 96 times. `segment_ids`: document numbers never fall along a sequence; every one of the 4 documents has 1 to 512 positions, one exactly that many.
All inputs are finite; a program needn't handle non-finite values.
Results may differ from the reference program's by a relative error of at most 0.023.
Values may be sent and summed in bfloat16 or wider, within the bound.
No kernel may reach another device: no remote copies, remote signals or barrier semaphores. Data moves between devices by JAX's collectives and lax.ppermute only.
A program may use at most 136 MiB of HBM per device.

```python
import math
import jax
import jax.numpy as jnp
import numpy as np
from jax import lax

MODEL_WIDTH = 1024
QUERY_HEADS = 16
KEY_HEADS = 8
HEAD_SIZE = 64
FF = 512
EXPERTS = 32
TOP = 8
DOCS = 4
ROWS = 256
SEQ_LEN = 1024
SEQS = 16
PROJ_GROUP_COLS = 256
QUERY_GROUP_COLS = 128
CAP = 96
N_TP = 4


def shard_levels(own_key, dims, split, least, top_value):
    factor_of = 1.0
    for position, parts in split:
        heights = jax.random.uniform(jax.random.fold_in(jax.random.fold_in(own_key, 6), position), (parts,), jnp.float32, least / len(split), top_value / len(split))
        factor_of = factor_of * jnp.repeat(jnp.exp(heights), dims[position] // parts).reshape((-1,) + (1,) * (len(dims) - 1 - position))
    return factor_of


def length_profile(number_of, total, bound, slope):
    weights = [(1 << 20) // math.isqrt(grade ** slope) + 1 for grade in range(2, number_of + 1)]
    surplus, given = total - bound - (number_of - 1), [1] * (number_of - 1)
    while surplus > 0:
        movable = [i for i in range(number_of - 1) if given[i] < bound]
        pool, left = sum([weights[i] for i in movable]), surplus
        for i in movable:
            more = min(bound - given[i], max(1, left * weights[i] // pool), surplus)
            given[i] = given[i] + more
            surplus = surplus - more
    return np.array([bound] + given)


def uneven(rng, number_of, total, limit, lean):
    if number_of == 2:
        one = jax.random.randint(rng, (), max(1, total - limit), min(limit, total - 1) + 1)
        return jnp.stack([one, total - one])
    lengths = jnp.asarray(length_profile(number_of, total, limit, lean), jnp.int32)
    twos = (number_of - 1) // 2
    donor, receiver = lengths[1:1 + 2 * twos:2], lengths[2:2 + 2 * twos:2]
    room = jnp.minimum(donor - 1, limit - receiver)
    shifted = jax.random.randint(jax.random.fold_in(rng, 1), (twos,), 0, 1 << 20) % (room + 1)
    lengths = lengths.at[1:1 + 2 * twos:2].set(donor - shifted).at[2:2 + 2 * twos:2].set(receiver + shifted)
    return lengths[jax.random.permutation(jax.random.fold_in(rng, 2), number_of)]


def routed_block(own_key, own, number, rows, count, top, most, skew):
    order = jax.random.permutation(own_key, count)
    heavy_load, usual = shares(count, rows * top, most, skew, True), shares(count, rows * top, most, skew, False)
    places = jnp.arange(count)

    def named(tallies, rotation):
        used = int((tallies > 0).sum())
        fixed = max(1, used // 4)
        moved = fixed + (places - fixed + rotation * (used - fixed)) % max(1, count - fixed)
        return jnp.zeros((count,), jnp.int32).at[order[jnp.where(places < fixed, places, moved)]].set(jnp.asarray(tallies, jnp.int32))

    tallies = jnp.where(number % 4 == 0, named(heavy_load, number // 4), named(usual, number - number // 4 - 1))
    mixed = jax.random.permutation(jax.random.fold_in(own, 3), count)
    source_of, sink = mixed[0:count // 2 * 2:2], mixed[1:count // 2 * 2:2]
    slack = jnp.minimum(tallies[source_of] - 1, most - tallies[sink]) // 2
    slack = jnp.where((source_of == order[0]) | (sink == order[0]) | (tallies[sink] == 0), 0, jnp.maximum(slack, 0))
    moved = jax.random.randint(jax.random.fold_in(own, 4), (count // 2,), 0, 1 << 20) % (slack + 1)
    tallies = tallies.at[source_of].add(-moved).at[sink].add(moved)
    members = jnp.searchsorted(jnp.cumsum(tallies), jnp.arange(rows * top), side="right").astype(jnp.int32)
    table = members.reshape(top, rows).T
    table = table[jax.random.permutation(jax.random.fold_in(own, 1), rows)]
    rotation = jax.random.randint(jax.random.fold_in(own, 2), (rows, 1), 0, top)
    return jnp.take_along_axis(table, (jnp.arange(top)[None, :] + rotation) % top, axis=1)


def shares(count, total, most, lean, full):
    loads = [(1 << 20) // math.isqrt(standing ** lean) + 1 for standing in range(1, count + 1)]
    largest = most if full else min(most, max(-(-total // count), total * loads[0] // sum(loads)))
    least = 1 if total - largest >= count - 1 else 0
    holding, rest = [largest] + [least] * (count - 1), total - largest - least * (count - 1)
    while rest > 0:
        movable = [i for i in range(1, count) if holding[i] < largest] or [i for i in range(1, count) if holding[i] < most]
        mass, remaining = sum([loads[i] for i in movable]), rest
        for i in movable:
            extra = min(most - holding[i], max(1, remaining * loads[i] // mass), rest)
            holding[i] = holding[i] + extra
            rest = rest - extra
    return np.array(holding)


def gaussian(stream_key, extent, width, most, split=(), kind=jnp.bfloat16):
    values = width * jax.random.normal(stream_key, extent, jnp.float32)
    if split:
        values = values * shard_levels(stream_key, extent, split, -0.22, 0.18)
    return jnp.clip(values, -most, most).astype(kind)


def setup_inputs(seed: int = 0) -> dict:
    key_list = jax.random.split(jax.random.key(seed), 11)
    tokens = gaussian(key_list[0], (SEQS, SEQ_LEN, MODEL_WIDTH), 1.0, 6.0, ((0, 8), (1, 4)))
    cotangent = gaussian(key_list[1], (SEQS, SEQ_LEN, MODEL_WIDTH), 1.0, 6.0, ((0, 8), (1, 4)))
    norm_gains = jnp.clip(1.0 + 0.1 * jax.random.normal(key_list[2], (2, MODEL_WIDTH), jnp.float32), 0.5, 1.5)
    query_key_value_weight = gaussian(key_list[3], (MODEL_WIDTH, KEY_HEADS, PROJ_GROUP_COLS), (MODEL_WIDTH // 12) ** -0.5, 0.625, ((0, 8), (1, 4)))
    output_weight = gaussian(key_list[4], (KEY_HEADS, QUERY_GROUP_COLS, MODEL_WIDTH), 4 ** -0.5, 3.0, ((0, 4), (2, 8)))
    w_router = gaussian(key_list[5], (MODEL_WIDTH, EXPERTS), (4 * MODEL_WIDTH) ** -0.5, 0.09375)
    w_gate_up = gaussian(key_list[6], (EXPERTS, MODEL_WIDTH, 2 * FF), MODEL_WIDTH ** -0.5, 0.1875, ((0, 8), (1, 4)))
    w_down = gaussian(key_list[7], (EXPERTS, FF, MODEL_WIDTH), 4 ** -0.5, 3.0, ((0, 8), (2, 4)))
    segment_ids = jax.vmap(lambda own: jnp.searchsorted(jnp.cumsum(uneven(own, DOCS, SEQ_LEN, SEQ_LEN // 2, 1)), jnp.arange(SEQ_LEN), side="right"))(jax.random.split(key_list[8], SEQS)).reshape((SEQS, SEQ_LEN)).astype(jnp.int32)
    routes_keys = jax.random.split(jax.random.fold_in(key_list[9], 1), SEQS * N_TP * ROWS // ROWS)
    routes_turns = jax.random.permutation(jax.random.fold_in(key_list[9], 3), SEQS * N_TP * ROWS // ROWS)
    routes = jax.vmap(lambda own, number: routed_block(jax.random.fold_in(key_list[9], 2), own, number, ROWS, EXPERTS, TOP, CAP, 1))(routes_keys, routes_turns).reshape((SEQS, N_TP, ROWS, TOP))
    return {"tokens": tokens, "cotangent": cotangent, "norm_gains": norm_gains, "query_key_value_weight": query_key_value_weight, "output_weight": output_weight, "w_router": w_router, "w_gate_up": w_gate_up, "w_down": w_down, "segment_ids": segment_ids, "routes": routes}


highest_precision = lax.Precision.HIGHEST
epsilon = 1e-06
score_scale = 0.015625
residual_scale = 0.22
rope_base = 10000.0
masked_score = -1000000000.0

@jax.custom_vjp
def low(v):
    return lax.optimization_barrier(v.astype(jnp.bfloat16)).astype(jnp.float32)

@jax.custom_vjp
def lower_backward(v):
    return v

def low_keep(v):
    return (low(v), None)

def low_pass(kept, grad):
    return (grad,)

def back_keep(v):
    return (v, None)

def back_low(kept, grad):
    return (low(grad),)
low.defvjp(low_keep, low_pass)
lower_backward.defvjp(back_keep, back_low)

def positions_of(segment_row):
    onehot = (segment_row[:, None] == jnp.arange(DOCS, dtype=jnp.int32)[None, :]).astype(jnp.int32)
    doc_len = lax.optimization_barrier(jnp.sum(onehot, axis=0))
    starts = jnp.cumsum(doc_len) - doc_len
    return jnp.arange(segment_row.shape[0], dtype=jnp.int32) - lax.optimization_barrier(jnp.sum(onehot * starts[None, :], axis=1))

def rope_tables(positions):
    halves = HEAD_SIZE // 2
    freqs = rope_base ** (-(jnp.arange(halves, dtype=jnp.float32) * 2.0) / HEAD_SIZE)
    angles = positions.astype(jnp.float32)[:, None] * freqs[None, :]
    return (jnp.cos(angles), jnp.sin(angles))

def rotate_pairs(values, cosine_table, sine_table):
    halves = values.shape[-1] // 2
    first = values[..., :halves]
    second = values[..., halves:]
    return jnp.concatenate([first * cosine_table - second * sine_table, second * cosine_table + first * sine_table], axis=-1)

def attend(query_rows, keys, values, segment_row):
    sequence_length = query_rows.shape[0]
    block = min(512, sequence_length)
    count = sequence_length // block
    key_index = jnp.arange(sequence_length, dtype=jnp.int32)

    def one_block(items):
        query_block, start = items
        scores = jnp.einsum('qhgd,khd->hgqk', query_block, keys, precision=highest_precision) * score_scale
        query_index = start + jnp.arange(block, dtype=jnp.int32)
        query_segment = lax.dynamic_slice_in_dim(segment_row, start, block)
        allowed = (key_index[None, :] <= query_index[:, None]) & (segment_row[None, :] == query_segment[:, None])
        scores = lower_backward(jnp.where(allowed[None, None], scores, masked_score))
        probs = jax.nn.softmax(scores, axis=-1)
        return jnp.einsum('hgqk,khd->qhgd', low(probs), values, precision=highest_precision)
    blocks = query_rows.reshape((count, block) + query_rows.shape[1:])
    starts = jnp.arange(count, dtype=jnp.int32) * block
    context = lax.map(jax.checkpoint(one_block), (blocks, starts))
    return context.reshape(query_rows.shape)

def experts(normed_two, routes_seq, gates, w_gate_up, w_down):
    sequence_length = normed_two.shape[0]
    flat = routes_seq.reshape(-1)
    order = jnp.argsort(flat, stable=True).astype(jnp.int32)
    counts = lax.optimization_barrier(jnp.sum((flat[:, None] == jnp.arange(EXPERTS, dtype=jnp.int32)[None, :]).astype(jnp.int32), axis=0))
    starts = jnp.cumsum(counts) - counts
    offsets = jnp.arange(N_TP * CAP, dtype=jnp.int32)
    valid = offsets[None, :] < counts[:, None]
    picks = jnp.clip(starts[:, None] + offsets[None, :], 0, sequence_length * TOP - 1)
    assign = order[picks]
    token = assign // TOP
    weight = jnp.where(valid, gates.reshape(-1)[assign], 0.0)
    inputs = lower_backward(normed_two[token]) * valid[..., None].astype(normed_two.dtype)
    hidden = lower_backward(jnp.einsum('emd,edf->emf', inputs, w_gate_up, precision=highest_precision))
    gate_part = hidden[..., :FF]
    up_part = hidden[..., FF:]
    active = low(jax.nn.silu(gate_part) * up_part)
    expert_out = low(lower_backward(jnp.einsum('emf,efd->emd', active, w_down, precision=highest_precision)))
    weighted = (expert_out * weight[..., None]).reshape(-1, normed_two.shape[1])
    return jnp.zeros_like(normed_two).at[token.reshape(-1)].add(weighted)

def layer(inputs, norm_gains, query_key_value_weight, output_weight, w_router, w_gate_up, w_down, segment_row, routes_seq):
    sequence_length = inputs.shape[0]
    head_group = QUERY_HEADS // KEY_HEADS
    scale_one = lax.rsqrt(lax.optimization_barrier(jnp.mean(inputs * inputs, axis=-1, keepdims=True)) + epsilon)
    normed_rows = low(inputs * scale_one * norm_gains[0])
    mixed_rows = lower_backward(jnp.dot(normed_rows, query_key_value_weight.reshape(MODEL_WIDTH, KEY_HEADS * PROJ_GROUP_COLS), precision=highest_precision)).reshape(sequence_length, KEY_HEADS, PROJ_GROUP_COLS)
    cosine_table, sine_table = rope_tables(positions_of(segment_row))
    query_rows = rotate_pairs(mixed_rows[:, :, :head_group * HEAD_SIZE].reshape(sequence_length, KEY_HEADS, head_group, HEAD_SIZE), cosine_table[:, None, None, :], sine_table[:, None, None, :])
    keys = rotate_pairs(mixed_rows[:, :, head_group * HEAD_SIZE:(head_group + 1) * HEAD_SIZE], cosine_table[:, None, :], sine_table[:, None, :])
    values = mixed_rows[:, :, (head_group + 1) * HEAD_SIZE:]
    context = attend(low(query_rows), low(keys), low(values), segment_row)
    context = low(lower_backward(context)).reshape(sequence_length, QUERY_HEADS * HEAD_SIZE)
    branch = lower_backward(jnp.dot(context, output_weight.reshape(QUERY_HEADS * HEAD_SIZE, MODEL_WIDTH), precision=highest_precision))
    hidden = inputs + residual_scale * branch
    scale_two = lax.rsqrt(lax.optimization_barrier(jnp.mean(hidden * hidden, axis=-1, keepdims=True)) + epsilon)
    normed_two = low(hidden * scale_two * norm_gains[1])
    logits = lower_backward(jnp.dot(normed_two, w_router, precision=highest_precision))
    onehot = (routes_seq[:, :, None] == jnp.arange(EXPERTS, dtype=jnp.int32)[None, None, :]).astype(jnp.float32)
    chosen = jnp.einsum('lke,le->lk', onehot, logits, precision=highest_precision)
    gates = jax.nn.softmax(chosen, axis=-1)
    return hidden + residual_scale * experts(normed_two, routes_seq, gates, w_gate_up, w_down)

def reference(tokens, cotangent, norm_gains, query_key_value_weight, output_weight, w_router, w_gate_up, w_down, segment_ids, routes):
    params = (norm_gains.astype(jnp.float32), query_key_value_weight.astype(jnp.float32), output_weight.astype(jnp.float32), w_router.astype(jnp.float32), w_gate_up.astype(jnp.float32), w_down.astype(jnp.float32))
    seq_routes = routes.reshape(SEQS, SEQ_LEN, TOP)

    def per_sequence(carry, items):
        seq_tokens, seq_cot, seq_segments, seq_route = items

        def forward(inputs, gains, qkv_weight, out_weight, router_weight, gate_up_weight, down_weight):
            return layer(inputs, gains, qkv_weight, out_weight, router_weight, gate_up_weight, down_weight, seq_segments, seq_route)
        result, pullback = jax.vjp(forward, seq_tokens.astype(jnp.float32), *params)
        grads = pullback(seq_cot.astype(jnp.float32))
        summed = tuple((total + part for total, part in zip(carry, grads[1:])))
        return (summed, (result.astype(jnp.bfloat16), grads[0]))
    initial = tuple((jnp.zeros(item.shape, jnp.float32) for item in params))
    totals, (outputs, input_grads) = lax.scan(per_sequence, initial, (tokens, cotangent, segment_ids, seq_routes))
    return (outputs, input_grads, totals[0], totals[1], totals[2], totals[3], totals[4], totals[5])
```

```python
import functools

import jax
import jax.numpy as jnp
from jax import lax
from jax.experimental import pallas as pl
from jax.experimental.pallas import tpu as pltpu
from jax.sharding import PartitionSpec as P

MODEL_WIDTH = 1024
HEAD_SIZE = 64
FF = 512
EXPERTS = 32
DOCS = 4
CAP = 96
LANES = 128
ROW_BLOCK = 256
GROUP_COLS = 256

epsilon = 1e-06
score_scale = 0.015625
residual_scale = 0.22
rope_base = 10000.0
masked_score = -1000000000.0

f32 = jnp.float32
bf16 = jnp.bfloat16

params = pltpu.CompilerParams(vmem_limit_bytes=58 * 1024 * 1024)
row_params = pltpu.CompilerParams(
    vmem_limit_bytes=58 * 1024 * 1024, dimension_semantics=("arbitrary",)
)


def dot(a, b):
    return jnp.dot(a, b, preferred_element_type=f32)


def dot_nt(a, b):
    return lax.dot_general(a, b, (((1,), (1,)), ((), ())), preferred_element_type=f32)


def dot_tn(a, b):
    return lax.dot_general(a, b, (((0,), (0,)), ((), ())), preferred_element_type=f32)


def lane_masks(rows):
    lane = lax.broadcasted_iota(jnp.int32, (rows, LANES), 1)
    return lane < HEAD_SIZE, (lane % HEAD_SIZE) < HEAD_SIZE // 2


def swap_halves(values, first):
    half = HEAD_SIZE // 2
    return jnp.where(first, pltpu.roll(values, LANES - half, 1), pltpu.roll(values, half, 1))


def for_blocks(count, body):
    if count <= 4:
        for index in range(count):
            body(index)
    else:

        def step(index, carry):
            body(index)
            return carry

        lax.fori_loop(0, count, step, 0)


def block_rows(index):
    if isinstance(index, int):
        return pl.ds(index * ROW_BLOCK, ROW_BLOCK)
    return pl.ds(pl.multiple_of(index * ROW_BLOCK, ROW_BLOCK), ROW_BLOCK)


def key_window(index, length):
    reach = -(-(length // 2) // ROW_BLOCK)
    if isinstance(index, int):
        start = max(0, index - reach) * ROW_BLOCK
        return start, (index + 1) * ROW_BLOCK - start
    start = jnp.maximum(index - reach, 0) * ROW_BLOCK
    return pl.multiple_of(start, ROW_BLOCK), (reach + 1) * ROW_BLOCK


def allowed_keys(index, start, width, seg_col_ref, seg_row_ref):
    query = lax.broadcasted_iota(jnp.int32, (ROW_BLOCK, width), 0) + index * ROW_BLOCK
    key = lax.broadcasted_iota(jnp.int32, (ROW_BLOCK, width), 1) + start
    same = seg_row_ref[:, pl.ds(start, width)] == seg_col_ref[block_rows(index), :]
    return (key <= query) & same


def place_rows(starts_ref, pieces, whole):
    for index, piece in enumerate(pieces):
        rows = piece.shape[0]
        begin = pl.multiple_of(starts_ref[index], ROW_BLOCK)
        whole[pl.ds(begin, rows), :] = piece[...]


def each_block(starts_ref, pieces):
    for index, piece in enumerate(pieces):
        for inner in range(0, piece.shape[0], ROW_BLOCK):
            begin = pl.multiple_of(starts_ref[index] + inner, ROW_BLOCK)
            yield pl.ds(begin, ROW_BLOCK), piece, slice(inner, inner + ROW_BLOCK)


def attention_forward_body(starts_ref, *refs, count):
    x_pieces = refs[:count]
    gain_ref, weights_ref, cos_ref, sin_ref, seg_col_ref, seg_row_ref = refs[count : count + 6]
    parts = refs[count + 6 : 2 * count + 6]
    qa_ref, qb_ref, kd_ref, vd_ref, ctx_ref, x_ref = refs[2 * count + 6 :]
    place_rows(starts_ref, x_pieces, x_ref)
    length = x_ref.shape[0]
    groups = weights_ref.shape[1] // (GROUP_COLS + LANES)
    low, first = lane_masks(ROW_BLOCK)

    def project(index):
        rows = block_rows(index)
        x = x_ref[rows, :].astype(f32)
        scale = lax.rsqrt(jnp.mean(x * x, axis=-1, keepdims=True) + epsilon)
        normed = (x * scale * gain_ref[...]).astype(bf16)
        projected = dot(normed, weights_ref[:, : groups * GROUP_COLS])
        cosine = cos_ref[rows, :]
        sine = sin_ref[rows, :]
        for group in range(groups):
            cols = slice(group * LANES, (group + 1) * LANES)
            query = projected[:, group * GROUP_COLS : group * GROUP_COLS + LANES]
            pair = projected[:, group * GROUP_COLS + LANES : (group + 1) * GROUP_COLS]
            query = (query * cosine + swap_halves(query, first) * sine) * score_scale
            qa_ref[rows, cols] = jnp.where(low, query, 0.0).astype(bf16)
            qb_ref[rows, cols] = jnp.where(low, 0.0, query).astype(bf16)
            turned = pair * cosine + swap_halves(pair, first) * sine
            kd_ref[rows, cols] = jnp.where(low, turned, pltpu.roll(turned, HEAD_SIZE, 1)).astype(
                bf16
            )
            vd_ref[rows, cols] = jnp.where(low, pltpu.roll(pair, HEAD_SIZE, 1), pair).astype(bf16)

    def attend(index):
        rows = block_rows(index)
        start, width = key_window(index, length)
        keys = pl.ds(start, width)
        allowed = allowed_keys(index, start, width, seg_col_ref, seg_row_ref)
        for group in range(groups):
            cols = slice(group * LANES, (group + 1) * LANES)
            heads = []
            for q_ref in (qa_ref, qb_ref):
                scores = dot_nt(q_ref[rows, cols], kd_ref[keys, cols])
                scores = jnp.where(allowed, scores, masked_score)
                expo = jnp.exp(scores - jnp.max(scores, axis=-1, keepdims=True))
                total = jnp.sum(expo, axis=-1, keepdims=True)
                probs = (expo * (1.0 / total)).astype(bf16)
                heads.append(dot(probs, vd_ref[keys, cols]))
            ctx_ref[rows, cols] = jnp.where(low, heads[0], heads[1]).astype(bf16)

    for_blocks(length // ROW_BLOCK, project)
    for_blocks(length // ROW_BLOCK, attend)
    for rows, part, inner in each_block(starts_ref, parts):
        part[inner, :] = dot_nt(ctx_ref[rows, :], weights_ref[:, groups * GROUP_COLS :]).astype(
            bf16
        )


def in_vmem(count):
    return [pl.BlockSpec(memory_space=pltpu.SMEM)] + [
        pl.BlockSpec(memory_space=pltpu.VMEM) for _ in range(count)
    ]


def attention_forward(starts, pieces, gain, weights, cosine, sine, seg_col, seg_row):
    length = cosine.shape[0]
    count = len(pieces)
    half = jax.ShapeDtypeStruct((length, weights.shape[1] // 3), bf16)
    results = pl.pallas_call(
        functools.partial(attention_forward_body, count=count),
        out_shape=tuple(jax.ShapeDtypeStruct(p.shape, bf16) for p in pieces) + (half,) * 5,
        in_specs=in_vmem(count + 6),
        scratch_shapes=[pltpu.VMEM((length, MODEL_WIDTH), bf16)],
        compiler_params=params,
        name="attn_fwd",
    )(starts, *pieces, gain, weights, cosine, sine, seg_col, seg_row)
    return results[:count], results[count:]


def attention_backward_body(starts_ref, *refs, count):
    x_pieces, refs = refs[:count], refs[count:]
    gain_ref, weights_ref, cos_ref, sin_ref, seg_col_ref, seg_row_ref = refs[:6]
    qa_ref, qb_ref, kd_ref, vd_ref, ctx_ref = refs[6:11]
    gb_pieces, parts, refs = refs[11 : 11 + count], refs[11 + count : 11 + 2 * count], refs[
        11 + 2 * count :
    ]
    grad_ref, gain_grad_ref, gb_ref, norm_sc, proj_sc, dk_sc, dv_sc = refs
    place_rows(starts_ref, gb_pieces, gb_ref)
    length = gb_ref.shape[0]
    groups = weights_ref.shape[1] // (GROUP_COLS + LANES)
    split = groups * GROUP_COLS
    low, first = lane_masks(ROW_BLOCK)
    dk_sc[...] = jnp.zeros_like(dk_sc)
    dv_sc[...] = jnp.zeros_like(dv_sc)

    def attend(index):
        rows = block_rows(index)
        start, width = key_window(index, length)
        keys = pl.ds(start, width)
        allowed = allowed_keys(index, start, width, seg_col_ref, seg_row_ref)
        grad_context = dot(gb_ref[rows, :], weights_ref[:, split:])
        cosine = cos_ref[rows, :]
        sine = sin_ref[rows, :]
        for group in range(groups):
            cols = slice(group * LANES, (group + 1) * LANES)
            grad_group = grad_context[:, cols]
            grad_queries = []
            for head, q_ref in enumerate((qa_ref, qb_ref)):
                if head == 0:
                    grad_head = jnp.where(low, grad_group, 0.0).astype(bf16)
                else:
                    grad_head = jnp.where(low, 0.0, grad_group).astype(bf16)
                query = q_ref[rows, cols]
                scores = dot_nt(query, kd_ref[keys, cols])
                scores = jnp.where(allowed, scores, masked_score)
                expo = jnp.exp(scores - jnp.max(scores, axis=-1, keepdims=True))
                probs = expo * (1.0 / jnp.sum(expo, axis=-1, keepdims=True))
                grad_probs = dot_nt(grad_head, vd_ref[keys, cols])
                delta = jnp.sum(probs * grad_probs, axis=-1, keepdims=True)
                grad_scores = (probs * (grad_probs - delta)).astype(bf16)
                grad_queries.append(dot(grad_scores, kd_ref[keys, cols]))
                dk_sc[keys, cols] += dot_tn(grad_scores, query)
                dv_sc[keys, cols] += dot_tn(probs.astype(bf16), grad_head)
            grad_query = jnp.where(low, grad_queries[0], grad_queries[1]) * score_scale
            grad_query = grad_query * cosine - swap_halves(grad_query, first) * sine
            proj_sc[rows, group * GROUP_COLS : group * GROUP_COLS + LANES] = grad_query.astype(bf16)

    for_blocks(length // ROW_BLOCK, attend)
    gain_grad_ref[...] = jnp.zeros_like(gain_grad_ref)

    def finish(rows, part, inner, x_piece):
        cosine = cos_ref[rows, :]
        sine = sin_ref[rows, :]
        for group in range(groups):
            cols = slice(group * LANES, (group + 1) * LANES)
            grad_key = dk_sc[rows, cols]
            grad_key = grad_key + pltpu.roll(grad_key, HEAD_SIZE, 1)
            grad_key = grad_key * cosine - swap_halves(grad_key, first) * sine
            grad_value = dv_sc[rows, cols]
            grad_value = grad_value + pltpu.roll(grad_value, HEAD_SIZE, 1)
            proj_sc[rows, group * GROUP_COLS + LANES : (group + 1) * GROUP_COLS] = jnp.where(
                low, grad_key, grad_value
            ).astype(bf16)
        grad_normed = dot_nt(proj_sc[rows, :], weights_ref[:, :split])
        x = x_piece[inner, :].astype(f32)
        unit = x * lax.rsqrt(jnp.mean(x * x, axis=-1, keepdims=True) + epsilon)
        norm_sc[rows, :] = (unit * gain_ref[...]).astype(bf16)
        gain_grad_ref[...] += jnp.sum(grad_normed * unit, axis=0, keepdims=True)
        part[inner, :] = grad_normed.astype(bf16)

    if count > 1:
        for (rows, part, inner), x_piece in zip(each_block(starts_ref, parts), x_pieces):
            finish(rows, part, inner, x_piece)
    else:

        def whole_step(index):
            finish(block_rows(index), parts[0], block_rows(index), x_pieces[0])

        for_blocks(length // ROW_BLOCK, whole_step)
    grad_ref[:, :split] = dot_tn(norm_sc[...], proj_sc[...]).astype(bf16)
    grad_ref[:, split:] = dot_tn(gb_ref[...], ctx_ref[...]).astype(bf16)


def attention_backward(
    starts, pieces, gain, weights, cosine, sine, seg_col, seg_row, kept, grad_pieces
):
    length = cosine.shape[0]
    count = len(pieces)
    heads = weights.shape[1] // 3
    results = pl.pallas_call(
        functools.partial(attention_backward_body, count=count),
        out_shape=tuple(jax.ShapeDtypeStruct(p.shape, bf16) for p in pieces)
        + (
            jax.ShapeDtypeStruct(weights.shape, bf16),
            jax.ShapeDtypeStruct((1, MODEL_WIDTH), f32),
        ),
        in_specs=in_vmem(2 * count + 11),
        scratch_shapes=[
            pltpu.VMEM((length, MODEL_WIDTH), bf16),
            pltpu.VMEM((length, MODEL_WIDTH), bf16),
            pltpu.VMEM((length, 2 * heads), bf16),
            pltpu.VMEM((length, heads), f32),
            pltpu.VMEM((length, heads), f32),
        ],
        compiler_params=params,
        name="attn_bwd",
    )(starts, *pieces, gain, weights, cosine, sine, seg_col, seg_row, *kept, *grad_pieces)
    return results[:count], results[count:]


def dispatch_body(order_ref, x_ref, router_ref, *refs, local):
    gm_pieces, (xd_ref, gd_ref, pt_ref, pgt_ref, gm_ref) = refs[:-5], refs[-5:]
    rows = x_ref.shape[0]
    for index, piece in enumerate(gm_pieces):

        @pl.when(pl.program_id(0) == index)
        def _(piece=piece):
            gm_ref[...] = piece[...]

    slots = local * CAP
    x = x_ref[...]
    mask = gm_ref[:, MODEL_WIDTH:]
    chosen = mask.astype(f32) > 0.0
    logits = jnp.where(chosen, dot(x, router_ref[...]), masked_score)
    expo = jnp.where(chosen, jnp.exp(logits - jnp.max(logits, axis=-1, keepdims=True)), 0.0)
    gates = (expo / jnp.sum(expo, axis=-1, keepdims=True)).astype(bf16)
    earlier = lax.broadcasted_iota(jnp.int32, (rows, rows), 1) < lax.broadcasted_iota(
        jnp.int32, (rows, rows), 0
    )
    place = dot(jnp.where(earlier, 1.0, 0.0).astype(bf16), mask)
    place = jnp.where(chosen, place, -1.0).astype(bf16)
    offset = order_ref[pl.num_programs(0)]

    def pick(shape, slot_axis):
        slot = lax.broadcasted_iota(jnp.int32, shape, slot_axis)
        expert = lax.broadcasted_iota(jnp.int32, shape, 1 - slot_axis)
        hit = jnp.zeros(shape, jnp.bool_)
        for own in range(local):
            hit = hit | (
                (slot >= own * CAP) & (slot < (own + 1) * CAP) & (expert == offset + own)
            )
        return jnp.where(hit, 1.0, 0.0).astype(bf16)

    def in_slot(shape, slot_axis):
        slot = lax.broadcasted_iota(jnp.int32, shape, slot_axis)
        for own in range(1, local):
            slot = jnp.where(slot >= CAP, slot - CAP, slot)
        return slot.astype(f32)

    spread = pick((slots, LANES), 0)
    hit = dot_nt(spread, place) == in_slot((slots, rows), 0)
    send = jnp.where(hit, 1.0, 0.0).astype(bf16)
    send_gated = jnp.where(hit, dot_nt(spread, gates), 0.0).astype(bf16)
    xd_ref[...] = dot(send, x).astype(bf16).reshape(xd_ref.shape)
    gd_ref[...] = (
        (dot(send_gated, gm_ref[:, :MODEL_WIDTH]) * residual_scale).astype(bf16)
    ).reshape(gd_ref.shape)
    spread = pick((LANES, slots), 1)
    hit = dot(place, spread) == in_slot((rows, slots), 1)
    pt_ref[...] = jnp.where(hit, 1.0, 0.0).astype(bf16)
    pgt_ref[...] = jnp.where(hit, dot(gates, spread), 0.0).astype(bf16)


def dispatch(order, x, gm_pieces, router, local):
    blocks = x.shape[0] // ROW_BLOCK
    slots = local * CAP
    slotted = jax.ShapeDtypeStruct((local, blocks, CAP, MODEL_WIDTH), bf16)
    slotted_spec = pl.BlockSpec((local, 1, CAP, MODEL_WIDTH), lambda s, o: (0, o[s], 0, 0))
    return pl.pallas_call(
        functools.partial(dispatch_body, local=local),
        grid_spec=pltpu.PrefetchScalarGridSpec(
            num_scalar_prefetch=1,
            grid=(blocks,),
            in_specs=[
                pl.BlockSpec((ROW_BLOCK, MODEL_WIDTH), lambda s, o: (o[s], 0)),
                pl.BlockSpec((MODEL_WIDTH, LANES), lambda s, o: (0, 0)),
            ]
            + [pl.BlockSpec((ROW_BLOCK, MODEL_WIDTH + LANES), lambda s, o: (0, 0))]
            * len(gm_pieces),
            out_specs=[
                slotted_spec,
                slotted_spec,
                pl.BlockSpec((ROW_BLOCK, slots), lambda s, o: (o[s], 0)),
                pl.BlockSpec((ROW_BLOCK, slots), lambda s, o: (o[s], 0)),
            ],
            scratch_shapes=[pltpu.VMEM((ROW_BLOCK, MODEL_WIDTH + LANES), bf16)],
        ),
        out_shape=(
            slotted,
            slotted,
            jax.ShapeDtypeStruct((x.shape[0], slots), bf16),
            jax.ShapeDtypeStruct((x.shape[0], slots), bf16),
        ),
        compiler_params=row_params,
        name="dispatch",
    )(order, x, router, *gm_pieces)


def experts_body(place_ref, *refs, count, carried):
    xd_ref, gd_ref, refs = refs[0], refs[1], refs[2:]
    tables = count + 1 if count > 1 else count
    gu_pieces, d_pieces, refs = refs[:tables], refs[tables : 2 * tables], refs[2 * tables :]
    old, refs = (refs[: 2 * count], refs[2 * count :]) if carried else ((), refs)
    out_ref, dx_ref, h_ref = refs[:3]
    dgu_refs, dd_refs = refs[3 : 3 + count], refs[3 + count : 3 + 2 * count]
    wgu_ref, wd_ref, act_sc, dh_sc = refs[3 + 2 * count :]
    expert = pl.program_id(0)
    half = pl.num_programs(0) // 2

    def starts(index, rows):
        return pl.multiple_of(place_ref[1 + index] * rows, LANES)

    def put(index, gu_piece, d_piece):
        rows = gu_piece.shape[1]
        begin = starts(index, rows)
        wgu_ref[pl.ds(begin, rows), :] = gu_piece[0]
        wd_ref[:, pl.ds(begin, rows)] = d_piece[0]

    for index in range(min(count, 3)):
        put(index, gu_pieces[index], d_pieces[index])
    if count > 1:

        @pl.when(expert < half)
        def _():
            put(3, gu_pieces[3], d_pieces[3])

        @pl.when(expert >= half)
        def _():
            put(3, gu_pieces[4], d_pieces[4])

    total = xd_ref.shape[1]
    chunk = ROW_BLOCK
    own = place_ref[0] + expert
    lane = lax.broadcasted_iota(jnp.int32, (chunk, LANES), 1)

    def chunk_step(index):
        rows = block_rows(index)
        hidden = dot(xd_ref[0, rows, :], wgu_ref[...])
        gate = hidden[:, :FF]
        up = hidden[:, FF:]
        sigmoid = jax.nn.sigmoid(gate)
        act = (gate * sigmoid * up).astype(bf16)
        act_sc[rows, :] = act
        out = dot(act, wd_ref[...]).astype(bf16)
        out_ref[0, rows, :] = out
        grad_out = gd_ref[0, rows, :]
        h = jnp.sum(grad_out.astype(f32) * out.astype(f32), axis=-1, keepdims=True)
        h_ref[0, rows, :] = jnp.where(lane == own, h, 0.0).astype(bf16)
        grad_act = dot_nt(grad_out, wd_ref[...])
        grad_gate = grad_act * up * sigmoid * (1.0 + gate * (1.0 - sigmoid))
        grad_up = grad_act * gate * sigmoid
        dh_sc[rows, :FF] = grad_gate.astype(bf16)
        dh_sc[rows, FF:] = grad_up.astype(bf16)
        dx_ref[0, rows, :] = dot_nt(dh_sc[rows, :], wgu_ref[...]).astype(bf16)

    for_blocks(total // chunk, chunk_step)
    for index in range(count):
        rows = dgu_refs[index].shape[1]
        begin = starts(index, rows)
        grad_down = dot_tn(act_sc[...], gd_ref[0, :, pl.ds(begin, rows)])
        grad_gate_up = dot_tn(xd_ref[0, :, pl.ds(begin, rows)], dh_sc[...])
        if carried:
            grad_gate_up = grad_gate_up + old[index][0].astype(f32)
            grad_down = grad_down + old[count + index][0].astype(f32)
        dgu_refs[index][0] = grad_gate_up.astype(bf16)
        dd_refs[index][0] = grad_down.astype(bf16)


def run_experts(place, xd, gd, gu_pieces, d_pieces, old):
    local, total = xd.shape[:2]
    count = place.shape[0] - 1
    rows = MODEL_WIDTH // count

    def spec(a, b):
        return pl.BlockSpec((1, a, b), lambda e, o: (e, 0, 0))

    def piece_specs(a, b):
        half = local // 2
        specs = [spec(a, b)] * min(count, 3)
        if count > 1:
            specs.append(pl.BlockSpec((1, a, b), lambda e, o: (jnp.minimum(e, half - 1), 0, 0)))
            specs.append(pl.BlockSpec((1, a, b), lambda e, o: (jnp.maximum(e - half, 0), 0, 0)))
        return specs

    row_spec = spec(total, MODEL_WIDTH)
    grad_specs = [spec(rows, 2 * FF)] * count + [spec(FF, rows)] * count
    results = pl.pallas_call(
        functools.partial(experts_body, count=count, carried=bool(old)),
        grid_spec=pltpu.PrefetchScalarGridSpec(
            num_scalar_prefetch=1,
            grid=(local,),
            in_specs=[row_spec, row_spec]
            + piece_specs(rows, 2 * FF)
            + piece_specs(FF, rows)
            + (grad_specs if old else []),
            out_specs=[row_spec, row_spec, spec(total, LANES)] + grad_specs,
            scratch_shapes=[
                pltpu.VMEM((MODEL_WIDTH, 2 * FF), bf16),
                pltpu.VMEM((FF, MODEL_WIDTH), bf16),
                pltpu.VMEM((total, FF), bf16),
                pltpu.VMEM((total, 2 * FF), bf16),
            ],
        ),
        out_shape=(
            jax.ShapeDtypeStruct((local, total, MODEL_WIDTH), bf16),
            jax.ShapeDtypeStruct((local, total, MODEL_WIDTH), bf16),
            jax.ShapeDtypeStruct((local, total, LANES), bf16),
        )
        + (jax.ShapeDtypeStruct((local, rows, 2 * FF), bf16),) * count
        + (jax.ShapeDtypeStruct((local, FF, rows), bf16),) * count,
        compiler_params=row_params,
        name="experts",
    )(place, xd, gd, *gu_pieces, *d_pieces, *old)
    return results[:3], results[3:]


def combine_body(out_ref, dx_ref, h_ref, pt_ref, pgt_ref, mix_ref, grad_ref):
    slots = pt_ref.shape[1]
    mix_ref[...] = dot(pgt_ref[...], out_ref[...].reshape(slots, MODEL_WIDTH)).astype(bf16)
    grad_ref[:, :MODEL_WIDTH] = dot(
        pt_ref[...], dx_ref[...].reshape(slots, MODEL_WIDTH)
    ).astype(bf16)
    grad_ref[:, MODEL_WIDTH:] = dot(pt_ref[...], h_ref[...].reshape(slots, LANES)).astype(bf16)


def combine(out, dx, h, pt, pgt):
    local = out.shape[0]
    blocks = pt.shape[0] // ROW_BLOCK
    slots = pt.shape[1]

    def slotted(array):
        return array.reshape(local, blocks, CAP, array.shape[-1])

    def spec(width):
        return pl.BlockSpec((local, 1, CAP, width), lambda s: (0, s, 0, 0))

    def row_spec(width):
        return pl.BlockSpec((ROW_BLOCK, width), lambda s: (s, 0))

    return pl.pallas_call(
        combine_body,
        grid=(blocks,),
        in_specs=[
            spec(MODEL_WIDTH), spec(MODEL_WIDTH), spec(LANES), row_spec(slots), row_spec(slots)
        ],
        out_specs=[row_spec(MODEL_WIDTH), row_spec(MODEL_WIDTH + LANES)],
        out_shape=(
            jax.ShapeDtypeStruct((pt.shape[0], MODEL_WIDTH), bf16),
            jax.ShapeDtypeStruct((pt.shape[0], MODEL_WIDTH + LANES), bf16),
        ),
        compiler_params=row_params,
        name="combine",
    )(slotted(out), slotted(dx), slotted(h), pt, pgt)


def flip(value, bits):
    return lax.ppermute(value, "tp", [(t, t ^ bits) for t in range(4)])


def square():
    return lax.axis_size("tp") == 4


def tp_places():
    me = lax.axis_index("tp").astype(jnp.int32)
    if square():
        return jnp.stack([me ^ bits for bits in range(4)])
    return jnp.zeros((1,), jnp.int32)


def gather_rows(value):
    if square():
        return [value] + [flip(value, bits) for bits in (1, 2, 3)]
    return [lax.all_gather(value, "tp", axis=0, tiled=True)]


def sum_rows(parts):
    if square():
        total = parts[0].astype(f32)
        for bits in (1, 2, 3):
            total = total + flip(parts[bits], bits).astype(f32)
        return total
    return lax.psum_scatter(parts[0], "tp", scatter_dimension=0, tiled=True).astype(f32)


def gather_weights(value, axis):
    if square():
        half = value.shape[0] // 2
        along_x = flip(value, 1)
        along_y = flip(value, 2)
        return [value, along_x, along_y, flip(along_y[:half], 1), flip(along_x[half:], 2)]
    return [lax.all_gather(value, "tp", axis=axis, tiled=True)]


def sum_weights(parts, axis):
    if square():
        half = parts[0].shape[0] // 2
        wide = [p.astype(f32) for p in parts]
        top = flip(parts[1][:half], 1) + wide[0][:half]
        top_far = flip(parts[3][:half], 1) + wide[2][:half]
        low = flip(parts[2][half:], 2) + wide[0][half:]
        low_far = flip(parts[3][half:], 2) + wide[1][half:]
        top = top + flip(top_far.astype(bf16), 2)
        low = low + flip(low_far.astype(bf16), 1)
        return jnp.concatenate([top, low])
    return lax.psum_scatter(parts[0], "tp", scatter_dimension=axis, tiled=True).astype(f32)


def ring_devices():
    size = lax.axis_size("ep")
    return [2 * r if 2 * r < size else 2 * (size - 1 - r) + 1 for r in range(size)]


def ring_order():
    size = lax.axis_size("ep")
    devices = ring_devices()
    table = []
    for me in range(size):
        at = devices.index(me)
        steps = [0]
        for step in range(1, size // 2 + 1):
            steps.append(-step)
            if step < size // 2:
                steps.append(step)
        table.append([devices[(at + step) % size] for step in steps])
    return jnp.asarray(table, jnp.int32)[lax.axis_index("ep")]


def ring_gather(value):
    size = lax.axis_size("ep")
    devices = ring_devices()
    ahead = [(devices[r], devices[(r + 1) % size]) for r in range(size)]
    back = [(b, a) for a, b in ahead]
    pieces = [value]
    left = right = value
    for step in range(1, size // 2 + 1):
        left = lax.ppermute(left, "ep", ahead)
        pieces.append(left)
        if step < size // 2:
            right = lax.ppermute(right, "ep", back)
            pieces.append(right)
    return pieces


def ag_ep(value, axis=0):
    return lax.all_gather(value, "ep", axis=axis, tiled=True)


def rs_ep(value, axis=0):
    return lax.psum_scatter(value, "ep", scatter_dimension=axis, tiled=True)


def rope_tables(segment_row):
    onehot = (segment_row[:, None] == jnp.arange(DOCS, dtype=jnp.int32)[None, :]).astype(jnp.int32)
    doc_len = jnp.sum(onehot, axis=0)
    starts = [jnp.sum(doc_len[:doc]) for doc in range(DOCS)]
    begin = jnp.zeros_like(segment_row)
    for doc in range(1, DOCS):
        begin = jnp.where(segment_row == doc, starts[doc], begin)
    positions = jnp.arange(segment_row.shape[0], dtype=jnp.int32) - begin
    lane = jnp.arange(LANES, dtype=jnp.int32)
    halves = HEAD_SIZE // 2
    freqs = rope_base ** (-((lane % halves).astype(f32) * 2.0) / HEAD_SIZE)
    angles = positions.astype(f32)[:, None] * freqs[None, :]
    sign = jnp.where((lane % HEAD_SIZE) < halves, -1.0, 1.0).astype(f32)
    return jnp.cos(angles), jnp.sin(angles) * sign[None, :]


def shards(
    tokens,
    cotangent,
    norm_gains,
    query_key_value_weight,
    output_weight,
    w_router,
    w_gate_up,
    w_down,
    segment_ids,
    routes,
):
    micro, rows = tokens.shape[:2]
    local_heads = query_key_value_weight.shape[1]
    local = w_gate_up.shape[0]
    ep_size = lax.axis_size("ep")
    offset = (lax.axis_index("ep") * local).astype(jnp.int32).reshape(1)
    places = tp_places()
    starts = places * ROW_BLOCK
    place = jnp.concatenate([offset, places])
    gain_one = norm_gains[0:1]
    gain_two = norm_gains[1:2]
    router = jnp.pad(w_router, ((0, 0), (0, LANES - EXPERTS)))

    order = jnp.concatenate([ring_order(), offset])

    weights = ag_ep(
        jnp.concatenate(
            [
                query_key_value_weight.reshape(query_key_value_weight.shape[0], -1),
                output_weight.reshape(-1, output_weight.shape[2]).T,
            ],
            axis=1,
        )
    )
    token_full = [gather_rows(tokens[m]) for m in range(micro)]
    lanes = jnp.arange(LANES, dtype=jnp.int32)
    masks = jnp.any(
        routes.reshape(micro, rows, -1)[..., None] == lanes, axis=2
    ).astype(bf16)
    gm_full = [ring_gather(jnp.concatenate([cotangent[m], masks[m]], axis=-1)) for m in range(micro)]
    gu_pieces = gather_weights(w_gate_up, 1)
    d_pieces = gather_weights(w_down, 2)

    tables = [rope_tables(segment_ids[m]) for m in range(micro)]
    fixed = []
    for m in range(micro):
        fixed.append(
            (
                starts, token_full[m], gain_one, weights, tables[m][0], tables[m][1],
                segment_ids[m][:, None], segment_ids[m][None, :],
            )
        )

    kept = []
    hiddens = []
    normed_twos = []
    scales = []
    gate_rows = []
    for m in range(micro):
        parts, saved = attention_forward(*fixed[m])
        kept.append(saved)
        branch = sum_rows(parts)
        hidden = tokens[m].astype(f32) + residual_scale * branch
        scale_two = lax.rsqrt(jnp.mean(hidden * hidden, axis=-1, keepdims=True) + epsilon)
        normed_two = (hidden * scale_two * gain_two).astype(bf16)
        logits = jnp.where(masks[m] > 0, dot(normed_two, router), masked_score)
        expo = jnp.where(
            masks[m] > 0, jnp.exp(logits - jnp.max(logits, axis=-1, keepdims=True)), 0.0
        )
        gate_rows.append(expo / jnp.sum(expo, axis=-1, keepdims=True))
        hiddens.append(hidden)
        normed_twos.append(normed_two)
        scales.append(scale_two)

    old = ()
    mixes = []
    outputs = []
    input_grads = []
    acc_router = 0.0
    acc_gain_one = 0.0
    acc_gain_two = 0.0
    acc_weights = 0.0
    for m in range(micro):
        x_full = ag_ep(normed_twos[m])
        xd, gd, pt, pgt = dispatch(order, x_full, gm_full[m], router, local)
        merged = (local, ep_size * CAP, MODEL_WIDTH)
        (out, dx, h), old = run_experts(
            place, xd.reshape(merged), gd.reshape(merged), gu_pieces, d_pieces, old
        )
        mix, grad = combine(out, dx, h, pt, pgt)
        grad = rs_ep(grad).astype(f32)
        mixes.append(mix)

        h_rows = grad[:, MODEL_WIDTH:]
        grad_logits = (
            h_rows - gate_rows[m] * jnp.sum(h_rows, axis=-1, keepdims=True)
        ).astype(bf16)
        acc_router = acc_router + dot_tn(normed_twos[m], grad_logits)
        grad_normed = grad[:, :MODEL_WIDTH] + dot_nt(grad_logits, router)
        scale = scales[m]
        weighted = grad_normed * gain_two
        inner = jnp.mean(weighted * hiddens[m], axis=-1, keepdims=True)
        grad_hidden = (
            cotangent[m].astype(f32)
            + scale * weighted
            - hiddens[m] * scale * scale * scale * inner
        )
        acc_gain_two = acc_gain_two + jnp.sum(grad_normed * hiddens[m] * scale, axis=0)
        grad_branch = gather_rows((residual_scale * grad_hidden).astype(bf16))
        parts, (gweights, ggain) = attention_backward(*fixed[m], kept[m], grad_branch)
        acc_weights = acc_weights + gweights.astype(f32)
        acc_gain_one = acc_gain_one + ggain[0]
        grad_normed = sum_rows(parts)
        inputs = tokens[m].astype(f32)
        scale = lax.rsqrt(jnp.mean(inputs * inputs, axis=-1, keepdims=True) + epsilon)
        weighted = grad_normed * gain_one
        inner = jnp.mean(weighted * inputs, axis=-1, keepdims=True)
        input_grads.append(
            grad_hidden + scale * weighted - inputs * scale * scale * scale * inner
        )

    for m in range(micro):
        mix, _ = lax.optimization_barrier((mixes[m], grad))
        mix = rs_ep(mix).astype(f32)
        outputs.append((hiddens[m] + residual_scale * mix).astype(bf16))

    count = places.shape[0]
    grad_gate_up = sum_weights(old[:count], 1)
    grad_down = sum_weights(old[count:], 2)

    small = jnp.concatenate(
        [
            acc_router[:, :EXPERTS],
            acc_gain_one[:, None],
            acc_gain_two[:, None],
            jnp.zeros((MODEL_WIDTH, LANES - EXPERTS - 2), f32),
        ],
        axis=-1,
    ).astype(bf16)
    rows = MODEL_WIDTH // lax.axis_size("tp")
    if square():
        small = sum_rows(
            [lax.dynamic_slice_in_dim(small, places[k] * rows, rows) for k in range(4)]
        ).astype(bf16)
    else:
        small = lax.psum_scatter(small, "tp", scatter_dimension=0, tiled=True)
    columns = acc_weights.shape[1]
    own_rows = MODEL_WIDTH // ep_size
    small_rows = rows // ep_size
    small = small.reshape(ep_size, small_rows * LANES)
    extra = -(-small.shape[1] // (8 * columns)) * 8
    small = jnp.pad(small, ((0, 0), (0, extra * columns - small.shape[1])))
    packed = jnp.concatenate(
        [
            acc_weights.astype(bf16).reshape(ep_size, own_rows, columns),
            small.reshape(ep_size, extra, columns),
        ],
        axis=1,
    )
    summed = rs_ep(packed.reshape(-1, columns)).astype(f32)
    split = local_heads * GROUP_COLS
    grad_qkv = summed[:own_rows, :split].reshape(own_rows, local_heads, GROUP_COLS)
    grad_out = summed[:own_rows, split:].T.reshape(local_heads, LANES, own_rows)
    small = summed[own_rows:].reshape(-1)[: small_rows * LANES].reshape(small_rows, LANES)
    grad_router = small[:, :EXPERTS]
    grad_gains = small[:, EXPERTS : EXPERTS + 2].T
    return (
        jnp.stack(outputs),
        jnp.stack(input_grads),
        grad_gains,
        grad_qkv,
        grad_out,
        grad_router,
        grad_gate_up,
        grad_down,
    )


def solution(mesh):
    placed = (
        P("ep", "tp", None),
        P("ep", "tp", None),
        P(),
        P("ep", "tp", None),
        P("tp", None, "ep"),
        P(),
        P("ep", "tp", None),
        P("ep", None, "tp"),
        P("ep", None),
        P("ep", "tp", None, None),
    )
    return jax.shard_map(
        shards,
        mesh=mesh,
        in_specs=placed,
        out_specs=(
            P("ep", "tp", None),
            P("ep", "tp", None),
            P(None, ("tp", "ep")),
            P("ep", "tp", None),
            P("tp", None, "ep"),
            P(("tp", "ep"), None),
            P("ep", "tp", None),
            P("ep", None, "tp"),
        ),
        check_vma=False,
    )
```

```python
import functools

import jax
import jax.numpy as jnp
from jax import lax
from jax.experimental import pallas as pl
from jax.experimental.pallas import tpu as pltpu
from jax.sharding import PartitionSpec as P

MODEL_WIDTH = 1024
HEAD_SIZE = 64
FF = 512
EXPERTS = 32
DOCS = 4
CAP = 96
LANES = 128
ROW_BLOCK = 256
GROUP_COLS = 256

epsilon = 1e-06
score_scale = 0.015625
residual_scale = 0.22
rope_base = 10000.0
masked_score = -1000000000.0

f32 = jnp.float32
bf16 = jnp.bfloat16

params = pltpu.CompilerParams(vmem_limit_bytes=58 * 1024 * 1024)
row_params = pltpu.CompilerParams(
    vmem_limit_bytes=58 * 1024 * 1024, dimension_semantics=("arbitrary",)
)


def cost(gflops, megabytes):
    return pl.CostEstimate(
        flops=int(gflops * 1e9), transcendentals=0, bytes_accessed=int(megabytes * 1e6)
    )


def after(value, *others):
    return lax.optimization_barrier((value, others))[0]


def dot(a, b):
    return jnp.dot(a, b, preferred_element_type=f32)


def dot_nt(a, b):
    return lax.dot_general(a, b, (((1,), (1,)), ((), ())), preferred_element_type=f32)


def dot_tn(a, b):
    return lax.dot_general(a, b, (((0,), (0,)), ((), ())), preferred_element_type=f32)


def lane_masks(rows):
    lane = lax.broadcasted_iota(jnp.int32, (rows, LANES), 1)
    return lane < HEAD_SIZE, (lane % HEAD_SIZE) < HEAD_SIZE // 2


def swap_halves(values, first):
    half = HEAD_SIZE // 2
    return jnp.where(first, pltpu.roll(values, LANES - half, 1), pltpu.roll(values, half, 1))


def for_blocks(count, body):
    if count <= 4:
        for index in range(count):
            body(index)
    else:

        def step(index, carry):
            body(index)
            return carry

        lax.fori_loop(0, count, step, 0)


def block_rows(index):
    if isinstance(index, int):
        return pl.ds(index * ROW_BLOCK, ROW_BLOCK)
    return pl.ds(pl.multiple_of(index * ROW_BLOCK, ROW_BLOCK), ROW_BLOCK)


def key_window(index, length):
    reach = -(-(length // 2) // ROW_BLOCK)
    if isinstance(index, int):
        start = max(0, index - reach) * ROW_BLOCK
        return start, (index + 1) * ROW_BLOCK - start
    start = jnp.maximum(index - reach, 0) * ROW_BLOCK
    return pl.multiple_of(start, ROW_BLOCK), (reach + 1) * ROW_BLOCK


def allowed_keys(index, start, width, seg_col_ref, seg_row_ref):
    query = lax.broadcasted_iota(jnp.int32, (ROW_BLOCK, width), 0) + index * ROW_BLOCK
    key = lax.broadcasted_iota(jnp.int32, (ROW_BLOCK, width), 1) + start
    same = seg_row_ref[:, pl.ds(start, width)] == seg_col_ref[block_rows(index), :]
    return (key <= query) & same


def place_rows(starts_ref, pieces, whole):
    for index, piece in enumerate(pieces):
        rows = piece.shape[0]
        begin = pl.multiple_of(starts_ref[index], ROW_BLOCK)
        whole[pl.ds(begin, rows), :] = piece[...]


def each_block(starts_ref, pieces):
    for index, piece in enumerate(pieces):
        for inner in range(0, piece.shape[0], ROW_BLOCK):
            begin = pl.multiple_of(starts_ref[index] + inner, ROW_BLOCK)
            yield pl.ds(begin, ROW_BLOCK), piece, slice(inner, inner + ROW_BLOCK)


def attention_forward_body(starts_ref, *refs, count):
    x_pieces = refs[:count]
    gain_ref, weights_ref, cos_ref, sin_ref, seg_col_ref, seg_row_ref = refs[count : count + 6]
    parts = refs[count + 6 : 2 * count + 6]
    qa_ref, qb_ref, kd_ref, vd_ref, ctx_ref, x_ref = refs[2 * count + 6 :]
    place_rows(starts_ref, x_pieces, x_ref)
    length = x_ref.shape[0]
    groups = weights_ref.shape[1] // (GROUP_COLS + LANES)
    low, first = lane_masks(ROW_BLOCK)

    def project(index):
        rows = block_rows(index)
        x = x_ref[rows, :].astype(f32)
        scale = lax.rsqrt(jnp.mean(x * x, axis=-1, keepdims=True) + epsilon)
        normed = (x * scale * gain_ref[...]).astype(bf16)
        projected = dot(normed, weights_ref[:, : groups * GROUP_COLS])
        cosine = cos_ref[rows, :]
        sine = sin_ref[rows, :]
        for group in range(groups):
            cols = slice(group * LANES, (group + 1) * LANES)
            query = projected[:, group * GROUP_COLS : group * GROUP_COLS + LANES]
            pair = projected[:, group * GROUP_COLS + LANES : (group + 1) * GROUP_COLS]
            query = (query * cosine + swap_halves(query, first) * sine) * score_scale
            qa_ref[rows, cols] = jnp.where(low, query, 0.0).astype(bf16)
            qb_ref[rows, cols] = jnp.where(low, 0.0, query).astype(bf16)
            turned = pair * cosine + swap_halves(pair, first) * sine
            kd_ref[rows, cols] = jnp.where(low, turned, pltpu.roll(turned, HEAD_SIZE, 1)).astype(
                bf16
            )
            vd_ref[rows, cols] = jnp.where(low, pltpu.roll(pair, HEAD_SIZE, 1), pair).astype(bf16)

    def attend(index):
        rows = block_rows(index)
        start, width = key_window(index, length)
        keys = pl.ds(start, width)
        allowed = allowed_keys(index, start, width, seg_col_ref, seg_row_ref)
        for group in range(groups):
            cols = slice(group * LANES, (group + 1) * LANES)
            heads = []
            for q_ref in (qa_ref, qb_ref):
                scores = dot_nt(q_ref[rows, cols], kd_ref[keys, cols])
                scores = jnp.where(allowed, scores, masked_score)
                expo = jnp.exp(scores - jnp.max(scores, axis=-1, keepdims=True))
                total = jnp.sum(expo, axis=-1, keepdims=True)
                probs = (expo * (1.0 / total)).astype(bf16)
                heads.append(dot(probs, vd_ref[keys, cols]))
            ctx_ref[rows, cols] = jnp.where(low, heads[0], heads[1]).astype(bf16)

    for_blocks(length // ROW_BLOCK, project)
    for_blocks(length // ROW_BLOCK, attend)
    for rows, part, inner in each_block(starts_ref, parts):
        part[inner, :] = dot_nt(ctx_ref[rows, :], weights_ref[:, groups * GROUP_COLS :]).astype(
            bf16
        )


def in_vmem(count):
    return [pl.BlockSpec(memory_space=pltpu.SMEM)] + [
        pl.BlockSpec(memory_space=pltpu.VMEM) for _ in range(count)
    ]


def attention_forward(starts, pieces, gain, weights, cosine, sine, seg_col, seg_row):
    length = cosine.shape[0]
    count = len(pieces)
    half = jax.ShapeDtypeStruct((length, weights.shape[1] // 3), bf16)
    results = pl.pallas_call(
        functools.partial(attention_forward_body, count=count),
        out_shape=tuple(jax.ShapeDtypeStruct(p.shape, bf16) for p in pieces) + (half,) * 5,
        in_specs=in_vmem(count + 6),
        scratch_shapes=[pltpu.VMEM((length, MODEL_WIDTH), bf16)],
        compiler_params=params,
        cost_estimate=cost(11.0, 40.0),
        name="attn_fwd",
    )(starts, *pieces, gain, weights, cosine, sine, seg_col, seg_row)
    return results[:count], results[count:]


def attention_backward_body(starts_ref, *refs, count):
    x_pieces, refs = refs[:count], refs[count:]
    gain_ref, weights_ref, cos_ref, sin_ref, seg_col_ref, seg_row_ref = refs[:6]
    qa_ref, qb_ref, kd_ref, vd_ref, ctx_ref = refs[6:11]
    gb_pieces, parts, refs = refs[11 : 11 + count], refs[11 + count : 11 + 2 * count], refs[
        11 + 2 * count :
    ]
    grad_ref, gain_grad_ref, gb_ref, norm_sc, proj_sc, dk_sc, dv_sc = refs
    place_rows(starts_ref, gb_pieces, gb_ref)
    length = gb_ref.shape[0]
    groups = weights_ref.shape[1] // (GROUP_COLS + LANES)
    split = groups * GROUP_COLS
    low, first = lane_masks(ROW_BLOCK)
    dk_sc[...] = jnp.zeros_like(dk_sc)
    dv_sc[...] = jnp.zeros_like(dv_sc)

    def attend(index):
        rows = block_rows(index)
        start, width = key_window(index, length)
        keys = pl.ds(start, width)
        allowed = allowed_keys(index, start, width, seg_col_ref, seg_row_ref)
        grad_context = dot(gb_ref[rows, :], weights_ref[:, split:])
        cosine = cos_ref[rows, :]
        sine = sin_ref[rows, :]
        for group in range(groups):
            cols = slice(group * LANES, (group + 1) * LANES)
            grad_group = grad_context[:, cols]
            grad_queries = []
            for head, q_ref in enumerate((qa_ref, qb_ref)):
                if head == 0:
                    grad_head = jnp.where(low, grad_group, 0.0).astype(bf16)
                else:
                    grad_head = jnp.where(low, 0.0, grad_group).astype(bf16)
                query = q_ref[rows, cols]
                scores = dot_nt(query, kd_ref[keys, cols])
                scores = jnp.where(allowed, scores, masked_score)
                expo = jnp.exp(scores - jnp.max(scores, axis=-1, keepdims=True))
                probs = expo * (1.0 / jnp.sum(expo, axis=-1, keepdims=True))
                grad_probs = dot_nt(grad_head, vd_ref[keys, cols])
                delta = jnp.sum(probs * grad_probs, axis=-1, keepdims=True)
                grad_scores = (probs * (grad_probs - delta)).astype(bf16)
                grad_queries.append(dot(grad_scores, kd_ref[keys, cols]))
                dk_sc[keys, cols] += dot_tn(grad_scores, query)
                dv_sc[keys, cols] += dot_tn(probs.astype(bf16), grad_head)
            grad_query = jnp.where(low, grad_queries[0], grad_queries[1]) * score_scale
            grad_query = grad_query * cosine - swap_halves(grad_query, first) * sine
            proj_sc[rows, group * GROUP_COLS : group * GROUP_COLS + LANES] = grad_query.astype(bf16)

    for_blocks(length // ROW_BLOCK, attend)
    gain_grad_ref[...] = jnp.zeros_like(gain_grad_ref)

    def finish(rows, part, inner, x_piece):
        cosine = cos_ref[rows, :]
        sine = sin_ref[rows, :]
        for group in range(groups):
            cols = slice(group * LANES, (group + 1) * LANES)
            grad_key = dk_sc[rows, cols]
            grad_key = grad_key + pltpu.roll(grad_key, HEAD_SIZE, 1)
            grad_key = grad_key * cosine - swap_halves(grad_key, first) * sine
            grad_value = dv_sc[rows, cols]
            grad_value = grad_value + pltpu.roll(grad_value, HEAD_SIZE, 1)
            proj_sc[rows, group * GROUP_COLS + LANES : (group + 1) * GROUP_COLS] = jnp.where(
                low, grad_key, grad_value
            ).astype(bf16)
        grad_normed = dot_nt(proj_sc[rows, :], weights_ref[:, :split])
        x = x_piece[inner, :].astype(f32)
        unit = x * lax.rsqrt(jnp.mean(x * x, axis=-1, keepdims=True) + epsilon)
        norm_sc[rows, :] = (unit * gain_ref[...]).astype(bf16)
        gain_grad_ref[...] += jnp.sum(grad_normed * unit, axis=0, keepdims=True)
        part[inner, :] = grad_normed.astype(bf16)

    if count > 1:
        for (rows, part, inner), x_piece in zip(each_block(starts_ref, parts), x_pieces):
            finish(rows, part, inner, x_piece)
    else:

        def whole_step(index):
            finish(block_rows(index), parts[0], block_rows(index), x_pieces[0])

        for_blocks(length // ROW_BLOCK, whole_step)
    grad_ref[:, :split] = dot_tn(norm_sc[...], proj_sc[...]).astype(bf16)
    grad_ref[:, split:] = dot_tn(gb_ref[...], ctx_ref[...]).astype(bf16)


def attention_backward(
    starts, pieces, gain, weights, cosine, sine, seg_col, seg_row, kept, grad_pieces
):
    length = cosine.shape[0]
    count = len(pieces)
    heads = weights.shape[1] // 3
    results = pl.pallas_call(
        functools.partial(attention_backward_body, count=count),
        out_shape=tuple(jax.ShapeDtypeStruct(p.shape, bf16) for p in pieces)
        + (
            jax.ShapeDtypeStruct(weights.shape, bf16),
            jax.ShapeDtypeStruct((1, MODEL_WIDTH), f32),
        ),
        in_specs=in_vmem(2 * count + 11),
        scratch_shapes=[
            pltpu.VMEM((length, MODEL_WIDTH), bf16),
            pltpu.VMEM((length, MODEL_WIDTH), bf16),
            pltpu.VMEM((length, 2 * heads), bf16),
            pltpu.VMEM((length, heads), f32),
            pltpu.VMEM((length, heads), f32),
        ],
        compiler_params=params,
        cost_estimate=cost(18.0, 65.0),
        name="attn_bwd",
    )(starts, *pieces, gain, weights, cosine, sine, seg_col, seg_row, *kept, *grad_pieces)
    return results[:count], results[count:]


def dispatch_body(
    offset_ref, x_ref, gm_ref, router_ref, xd_ref, gd_ref, pt_ref, pgt_ref, *, local
):
    rows = x_ref.shape[0]
    slots = local * CAP
    x = x_ref[...]
    mask = gm_ref[:, MODEL_WIDTH:]
    chosen = mask.astype(f32) > 0.0
    logits = jnp.where(chosen, dot(x, router_ref[...]), masked_score)
    expo = jnp.where(chosen, jnp.exp(logits - jnp.max(logits, axis=-1, keepdims=True)), 0.0)
    gates = (expo / jnp.sum(expo, axis=-1, keepdims=True)).astype(bf16)
    earlier = lax.broadcasted_iota(jnp.int32, (rows, rows), 1) < lax.broadcasted_iota(
        jnp.int32, (rows, rows), 0
    )
    place = dot(jnp.where(earlier, 1.0, 0.0).astype(bf16), mask)
    place = jnp.where(chosen, place, -1.0).astype(bf16)
    offset = offset_ref[0]

    def pick(shape, slot_axis):
        slot = lax.broadcasted_iota(jnp.int32, shape, slot_axis)
        expert = lax.broadcasted_iota(jnp.int32, shape, 1 - slot_axis)
        hit = jnp.zeros(shape, jnp.bool_)
        for own in range(local):
            hit = hit | (
                (slot >= own * CAP) & (slot < (own + 1) * CAP) & (expert == offset + own)
            )
        return jnp.where(hit, 1.0, 0.0).astype(bf16)

    def in_slot(shape, slot_axis):
        slot = lax.broadcasted_iota(jnp.int32, shape, slot_axis)
        for own in range(1, local):
            slot = jnp.where(slot >= CAP, slot - CAP, slot)
        return slot.astype(f32)

    spread = pick((slots, LANES), 0)
    hit = dot_nt(spread, place) == in_slot((slots, rows), 0)
    send = jnp.where(hit, 1.0, 0.0).astype(bf16)
    send_gated = jnp.where(hit, dot_nt(spread, gates), 0.0).astype(bf16)
    xd_ref[...] = dot(send, x).astype(bf16).reshape(xd_ref.shape)
    gd_ref[...] = (
        (dot(send_gated, gm_ref[:, :MODEL_WIDTH]) * residual_scale).astype(bf16)
    ).reshape(gd_ref.shape)
    spread = pick((LANES, slots), 1)
    hit = dot(place, spread) == in_slot((rows, slots), 1)
    pt_ref[...] = jnp.where(hit, 1.0, 0.0).astype(bf16)
    pgt_ref[...] = jnp.where(hit, dot(gates, spread), 0.0).astype(bf16)


def dispatch(offset, x, gm, router, local):
    blocks = x.shape[0] // ROW_BLOCK
    slots = local * CAP
    slotted = jax.ShapeDtypeStruct((local, blocks, CAP, MODEL_WIDTH), bf16)
    slotted_spec = pl.BlockSpec((local, 1, CAP, MODEL_WIDTH), lambda s, o: (0, s, 0, 0))
    return pl.pallas_call(
        functools.partial(dispatch_body, local=local),
        grid_spec=pltpu.PrefetchScalarGridSpec(
            num_scalar_prefetch=1,
            grid=(blocks,),
            in_specs=[
                pl.BlockSpec((ROW_BLOCK, MODEL_WIDTH), lambda s, o: (s, 0)),
                pl.BlockSpec((ROW_BLOCK, MODEL_WIDTH + LANES), lambda s, o: (s, 0)),
                pl.BlockSpec((MODEL_WIDTH, LANES), lambda s, o: (0, 0)),
            ],
            out_specs=[
                slotted_spec,
                slotted_spec,
                pl.BlockSpec((ROW_BLOCK, slots), lambda s, o: (s, 0)),
                pl.BlockSpec((ROW_BLOCK, slots), lambda s, o: (s, 0)),
            ],
        ),
        out_shape=(
            slotted,
            slotted,
            jax.ShapeDtypeStruct((x.shape[0], slots), bf16),
            jax.ShapeDtypeStruct((x.shape[0], slots), bf16),
        ),
        compiler_params=row_params,
        cost_estimate=cost(11.0, 40.0),
        name="dispatch",
    )(offset, x, gm, router)


def experts_body(place_ref, *refs, count, carried):
    xd_ref, gd_ref, refs = refs[0], refs[1], refs[2:]
    tables = count + 1 if count > 1 else count
    gu_pieces, d_pieces, refs = refs[:tables], refs[tables : 2 * tables], refs[2 * tables :]
    tables = 2 * count if count > 1 else count
    old, refs = (refs[: 2 * tables], refs[2 * tables :]) if carried else ((), refs)
    out_ref, dx_ref, h_ref = refs[:3]
    grad_refs = refs[3 : 3 + 2 * tables]
    wgu_ref, wd_ref, act_sc, dh_sc = refs[3 + 2 * tables :]
    expert = pl.program_id(0)
    half = pl.num_programs(0) // 2

    def starts(index, rows):
        return pl.multiple_of(place_ref[1 + index] * rows, LANES)

    def put(index, gu_piece, d_piece):
        rows = gu_piece.shape[1]
        begin = starts(index, rows)
        wgu_ref[pl.ds(begin, rows), :] = gu_piece[0]
        wd_ref[:, pl.ds(begin, rows)] = d_piece[0]

    for index in range(min(count, 3)):
        put(index, gu_pieces[index], d_pieces[index])
    if count > 1:

        @pl.when(expert < half)
        def _():
            put(3, gu_pieces[3], d_pieces[3])

        @pl.when(expert >= half)
        def _():
            put(3, gu_pieces[4], d_pieces[4])

    total = xd_ref.shape[1]
    chunk = ROW_BLOCK
    own = place_ref[0] + expert
    lane = lax.broadcasted_iota(jnp.int32, (chunk, LANES), 1)

    def chunk_step(index):
        rows = block_rows(index)
        hidden = dot(xd_ref[0, rows, :], wgu_ref[...])
        gate = hidden[:, :FF]
        up = hidden[:, FF:]
        sigmoid = jax.nn.sigmoid(gate)
        act = (gate * sigmoid * up).astype(bf16)
        act_sc[rows, :] = act
        out = dot(act, wd_ref[...]).astype(bf16)
        out_ref[0, rows, :] = out
        grad_out = gd_ref[0, rows, :]
        h = jnp.sum(grad_out.astype(f32) * out.astype(f32), axis=-1, keepdims=True)
        h_ref[0, rows, :] = jnp.where(lane == own, h, 0.0).astype(bf16)
        grad_act = dot_nt(grad_out, wd_ref[...])
        grad_gate = grad_act * up * sigmoid * (1.0 + gate * (1.0 - sigmoid))
        grad_up = grad_act * gate * sigmoid
        dh_sc[rows, :FF] = grad_gate.astype(bf16)
        dh_sc[rows, FF:] = grad_up.astype(bf16)
        dx_ref[0, rows, :] = dot_nt(dh_sc[rows, :], wgu_ref[...]).astype(bf16)

    for_blocks(total // chunk, chunk_step)
    def put_grad(index, value):
        if carried:
            value = value + old[index][0].astype(f32)
        grad_refs[index][0] = value.astype(bf16)

    def put_halves(index, value):
        if count == 1:
            put_grad(index, value)
            return

        @pl.when(expert < half)
        def _():
            put_grad(2 * index, value)

        @pl.when(expert >= half)
        def _():
            put_grad(2 * index + 1, value)

    for index in range(count):
        rows = grad_refs[0].shape[1]
        begin = starts(index, rows)
        put_halves(index, dot_tn(xd_ref[0, :, pl.ds(begin, rows)], dh_sc[...]))
        put_halves(count + index, dot_tn(act_sc[...], gd_ref[0, :, pl.ds(begin, rows)]))


def run_experts(place, xd, gd, gu_pieces, d_pieces, old):
    local, total = xd.shape[:2]
    count = place.shape[0] - 1
    rows = MODEL_WIDTH // count

    def spec(a, b):
        return pl.BlockSpec((1, a, b), lambda e, o: (e, 0, 0))

    half = local // 2

    def half_specs(a, b):
        return [
            pl.BlockSpec((1, a, b), lambda e, o: (jnp.minimum(e, half - 1), 0, 0)),
            pl.BlockSpec((1, a, b), lambda e, o: (jnp.maximum(e - half, 0), 0, 0)),
        ]

    def piece_specs(a, b):
        specs = [spec(a, b)] * min(count, 3)
        return specs + half_specs(a, b) if count > 1 else specs

    row_spec = spec(total, MODEL_WIDTH)
    if count > 1:
        both = half_specs(rows, 2 * FF), half_specs(FF, rows)
        grad_specs = both[0] * count + both[1] * count
        grad_rows = local // 2
    else:
        grad_specs = [spec(rows, 2 * FF), spec(FF, rows)]
        grad_rows = local
    repeats = len(grad_specs) // 2
    results = pl.pallas_call(
        functools.partial(experts_body, count=count, carried=bool(old)),
        grid_spec=pltpu.PrefetchScalarGridSpec(
            num_scalar_prefetch=1,
            grid=(local,),
            in_specs=[row_spec, row_spec]
            + piece_specs(rows, 2 * FF)
            + piece_specs(FF, rows)
            + (grad_specs if old else []),
            out_specs=[row_spec, row_spec, spec(total, LANES)] + grad_specs,
            scratch_shapes=[
                pltpu.VMEM((MODEL_WIDTH, 2 * FF), bf16),
                pltpu.VMEM((FF, MODEL_WIDTH), bf16),
                pltpu.VMEM((total, FF), bf16),
                pltpu.VMEM((total, 2 * FF), bf16),
            ],
        ),
        out_shape=(
            jax.ShapeDtypeStruct((local, total, MODEL_WIDTH), bf16),
            jax.ShapeDtypeStruct((local, total, MODEL_WIDTH), bf16),
            jax.ShapeDtypeStruct((local, total, LANES), bf16),
        )
        + (jax.ShapeDtypeStruct((grad_rows, rows, 2 * FF), bf16),) * repeats
        + (jax.ShapeDtypeStruct((grad_rows, FF, rows), bf16),) * repeats,
        compiler_params=row_params,
        cost_estimate=cost(30.0, 110.0),
        name="experts",
    )(place, xd, gd, *gu_pieces, *d_pieces, *old)
    return results[:3], results[3:]


def combine_body(out_ref, dx_ref, h_ref, pt_ref, pgt_ref, mix_ref, grad_ref):
    slots = pt_ref.shape[1]
    mix_ref[...] = dot(pgt_ref[...], out_ref[...].reshape(slots, MODEL_WIDTH)).astype(bf16)
    grad_ref[:, :MODEL_WIDTH] = dot(
        pt_ref[...], dx_ref[...].reshape(slots, MODEL_WIDTH)
    ).astype(bf16)
    grad_ref[:, MODEL_WIDTH:] = dot(pt_ref[...], h_ref[...].reshape(slots, LANES)).astype(bf16)


def combine(out, dx, h, pt, pgt):
    local = out.shape[0]
    blocks = pt.shape[0] // ROW_BLOCK
    slots = pt.shape[1]

    def slotted(array):
        return array.reshape(local, blocks, CAP, array.shape[-1])

    def spec(width):
        return pl.BlockSpec((local, 1, CAP, width), lambda s: (0, s, 0, 0))

    def row_spec(width):
        return pl.BlockSpec((ROW_BLOCK, width), lambda s: (s, 0))

    return pl.pallas_call(
        combine_body,
        grid=(blocks,),
        in_specs=[
            spec(MODEL_WIDTH), spec(MODEL_WIDTH), spec(LANES), row_spec(slots), row_spec(slots)
        ],
        out_specs=[row_spec(MODEL_WIDTH), row_spec(MODEL_WIDTH + LANES)],
        out_shape=(
            jax.ShapeDtypeStruct((pt.shape[0], MODEL_WIDTH), bf16),
            jax.ShapeDtypeStruct((pt.shape[0], MODEL_WIDTH + LANES), bf16),
        ),
        compiler_params=row_params,
        cost_estimate=cost(9.0, 33.0),
        name="combine",
    )(slotted(out), slotted(dx), slotted(h), pt, pgt)


def flip(value, bits):
    return lax.ppermute(value, "tp", [(t, t ^ bits) for t in range(4)])


def square():
    return lax.axis_size("tp") == 4


def tp_places():
    me = lax.axis_index("tp").astype(jnp.int32)
    if square():
        return jnp.stack([me ^ bits for bits in range(4)])
    return jnp.zeros((1,), jnp.int32)


def gather_rows(value):
    if square():
        return [value] + [flip(value, bits) for bits in (1, 2, 3)]
    return [lax.all_gather(value, "tp", axis=0, tiled=True)]


def send_rows(parts):
    if square():
        return [parts[0]] + [flip(parts[bits], bits) for bits in (1, 2, 3)]
    return [lax.psum_scatter(parts[0], "tp", scatter_dimension=0, tiled=True)]


def add_rows(came):
    total = came[0].astype(f32)
    for part in came[1:]:
        total = total + part.astype(f32)
    return total


def gather_weights_near(value, axis):
    if square():
        return [value, flip(value, 1), flip(value, 2)]
    return [lax.all_gather(value, "tp", axis=axis, tiled=True)]


def gather_weights_far(near):
    if square():
        half = near[0].shape[0] // 2
        return [*near, flip(near[2][:half], 1), flip(near[1][half:], 2)]
    return near


def sum_weights_near(parts, axis):
    if square():
        own, along_x, along_y, across = parts[0:2], parts[2:4], parts[4:6], parts[6:8]
        top = flip(along_x[0], 1).astype(f32) + own[0].astype(f32)
        top_far = flip(across[0], 1).astype(f32) + along_y[0].astype(f32)
        low = flip(along_y[1], 2).astype(f32) + own[1].astype(f32)
        low_far = flip(across[1], 2).astype(f32) + along_x[1].astype(f32)
        return top, low, top_far.astype(bf16), low_far.astype(bf16)
    return (lax.psum_scatter(parts[0], "tp", scatter_dimension=axis, tiled=True),)


def sum_weights_far(near):
    if square():
        top, low, top_far, low_far = near
        return top, low, flip(top_far, 2), flip(low_far, 1)
    return near


def add_far(far):
    if square():
        return jnp.concatenate([far[0] + far[2], far[1] + far[3]])
    return far[0].astype(f32)


def ag_ep(value, axis=0):
    return lax.all_gather(value, "ep", axis=axis, tiled=True)


def rs_ep(value, axis=0):
    return lax.psum_scatter(value, "ep", scatter_dimension=axis, tiled=True)


def rope_tables(segment_row):
    onehot = (segment_row[:, None] == jnp.arange(DOCS, dtype=jnp.int32)[None, :]).astype(jnp.int32)
    doc_len = jnp.sum(onehot, axis=0)
    starts = [jnp.sum(doc_len[:doc]) for doc in range(DOCS)]
    begin = jnp.zeros_like(segment_row)
    for doc in range(1, DOCS):
        begin = jnp.where(segment_row == doc, starts[doc], begin)
    positions = jnp.arange(segment_row.shape[0], dtype=jnp.int32) - begin
    lane = jnp.arange(LANES, dtype=jnp.int32)
    halves = HEAD_SIZE // 2
    freqs = rope_base ** (-((lane % halves).astype(f32) * 2.0) / HEAD_SIZE)
    angles = positions.astype(f32)[:, None] * freqs[None, :]
    sign = jnp.where((lane % HEAD_SIZE) < halves, -1.0, 1.0).astype(f32)
    return jnp.cos(angles), jnp.sin(angles) * sign[None, :]


def shards(
    tokens,
    cotangent,
    norm_gains,
    query_key_value_weight,
    output_weight,
    w_router,
    w_gate_up,
    w_down,
    segment_ids,
    routes,
):
    micro, rows = tokens.shape[:2]
    local_heads = query_key_value_weight.shape[1]
    local = w_gate_up.shape[0]
    ep_size = lax.axis_size("ep")
    offset = (lax.axis_index("ep") * local).astype(jnp.int32).reshape(1)
    places = tp_places()
    starts = places * ROW_BLOCK
    place = jnp.concatenate([offset, places])
    gain_one = norm_gains[0:1]
    gain_two = norm_gains[1:2]
    router = jnp.pad(w_router, ((0, 0), (0, LANES - EXPERTS)))

    weights = ag_ep(
        jnp.concatenate(
            [
                query_key_value_weight.reshape(query_key_value_weight.shape[0], -1),
                output_weight.reshape(-1, output_weight.shape[2]).T,
            ],
            axis=1,
        )
    )
    lanes = jnp.arange(LANES, dtype=jnp.int32)
    masks = jnp.any(
        routes.reshape(micro, rows, -1)[..., None] == lanes, axis=2
    ).astype(bf16)
    tables = [rope_tables(segment_ids[m]) for m in range(micro)]

    token_full = []
    for m in range(micro):
        own = after(tokens[m], token_full[-1]) if token_full else tokens[m]
        token_full.append(gather_rows(own))
    weights = after(weights, token_full[0])
    fixed = []
    for m in range(micro):
        fixed.append(
            (
                starts, token_full[m], gain_one, weights, tables[m][0], tables[m][1],
                segment_ids[m][:, None], segment_ids[m][None, :],
            )
        )

    gm_full = []
    kept = []
    partial = []
    for m in range(micro):
        parts, saved = attention_forward(*fixed[m])
        partial.append(parts)
        kept.append(saved)
    weights_in = after((w_gate_up, w_down), partial)
    gu_near = gather_weights_near(weights_in[0], 1)
    d_near = gather_weights_near(weights_in[1], 2)

    hiddens = []
    normed_twos = []
    scales = []
    gate_rows = []
    x_full = []
    for m in range(micro):
        came = send_rows(partial[m])
        if m == 0:
            came, token_full = lax.optimization_barrier((came, token_full))
        branch = add_rows(after(came, normed_twos))
        hidden = tokens[m].astype(f32) + residual_scale * branch
        scale_two = lax.rsqrt(jnp.mean(hidden * hidden, axis=-1, keepdims=True) + epsilon)
        normed_two = (hidden * scale_two * gain_two).astype(bf16)
        logits = jnp.where(masks[m] > 0, dot(normed_two, router), masked_score)
        expo = jnp.where(
            masks[m] > 0, jnp.exp(logits - jnp.max(logits, axis=-1, keepdims=True)), 0.0
        )
        gate_rows.append(expo / jnp.sum(expo, axis=-1, keepdims=True))
        hiddens.append(hidden)
        normed_twos.append(normed_two)
        scales.append(scale_two)
        if m == micro - 1:
            normed_two, gu_near, d_near = lax.optimization_barrier((normed_two, gu_near, d_near))
        gm = jnp.concatenate([cotangent[m], masks[m]], axis=-1)
        gm_full.append(ag_ep(after(gm, weights if m == 0 else normed_two)))
        x_full.append(ag_ep(after(normed_two, gm_full[m]) if m == 0 else normed_two))

    gu_pieces = gather_weights_far(gu_near)
    d_pieces = gather_weights_far(d_near)
    old = ()
    mixes = []
    grads = []
    ready = ()
    for m in range(micro):
        x_in = after(x_full[m], ready) if ready else x_full[m]
        xd, gd, pt, pgt = dispatch(offset, x_in, gm_full[m], router, local)
        merged = (local, ep_size * CAP, MODEL_WIDTH)
        (out, dx, h), old = run_experts(
            place, xd.reshape(merged), gd.reshape(merged), gu_pieces, d_pieces, old
        )
        mix, grad = combine(out, dx, h, pt, pgt)
        ready = (mix, grad)
        mixes.append(mix)
        grads.append(rs_ep(grad))
    near_gate_up = sum_weights_near(old[: len(old) // 2], 1)
    near_down = sum_weights_near(old[len(old) // 2 :], 2)
    input_grads = []
    acc_router = 0.0
    acc_gain_one = 0.0
    acc_gain_two = 0.0
    acc_weights = 0.0
    for m in range(micro):
        grad = grads[m]
        if m == micro - 1:
            grad, near_gate_up, near_down, _ = lax.optimization_barrier(
                (grad, near_gate_up, near_down, came)
            )
            far_down = sum_weights_far(near_down)
            mixed = []
            for n in range(micro):
                mixed.append(rs_ep(after(mixes[n], grad, mixed)))
        else:
            grad, near_down = lax.optimization_barrier((grad, near_down))
        grad = grad.astype(f32)
        h_rows = grad[:, MODEL_WIDTH:]
        grad_logits = (
            h_rows - gate_rows[m] * jnp.sum(h_rows, axis=-1, keepdims=True)
        ).astype(bf16)
        acc_router = acc_router + dot_tn(normed_twos[m], grad_logits)
        grad_normed = grad[:, :MODEL_WIDTH] + dot_nt(grad_logits, router)
        scale = scales[m]
        weighted = grad_normed * gain_two
        inner = jnp.mean(weighted * hiddens[m], axis=-1, keepdims=True)
        grad_hidden = (
            cotangent[m].astype(f32)
            + scale * weighted
            - hiddens[m] * scale * scale * scale * inner
        )
        acc_gain_two = acc_gain_two + jnp.sum(grad_normed * hiddens[m] * scale, axis=0)
        grad_branch = gather_rows((residual_scale * grad_hidden).astype(bf16))
        if m == micro - 1:
            grad_branch, far_down = lax.optimization_barrier((grad_branch, far_down))
            far_gate_up = sum_weights_far(near_gate_up)
        parts, (gweights, ggain) = attention_backward(*fixed[m], kept[m], grad_branch)
        came = send_rows(parts)
        acc_weights = acc_weights + gweights.astype(f32)
        acc_gain_one = acc_gain_one + ggain[0]
        grad_normed = add_rows(came)
        inputs = tokens[m].astype(f32)
        scale = lax.rsqrt(jnp.mean(inputs * inputs, axis=-1, keepdims=True) + epsilon)
        weighted = grad_normed * gain_one
        inner = jnp.mean(weighted * inputs, axis=-1, keepdims=True)
        input_grads.append(
            grad_hidden + scale * weighted - inputs * scale * scale * scale * inner
        )
    mixed, _ = lax.optimization_barrier((mixed, parts))
    outputs = [
        (hiddens[m] + residual_scale * mixed[m].astype(f32)).astype(bf16) for m in range(micro)
    ]
    acc_weights, far_gate_up = lax.optimization_barrier((acc_weights, far_gate_up))
    grad_gate_up = add_far(far_gate_up)
    grad_down = add_far(far_down)

    small = jnp.concatenate(
        [
            acc_router[:, :EXPERTS],
            acc_gain_one[:, None],
            acc_gain_two[:, None],
            jnp.zeros((MODEL_WIDTH, LANES - EXPERTS - 2), f32),
        ],
        axis=-1,
    ).astype(bf16)
    rows = MODEL_WIDTH // lax.axis_size("tp")
    if square():
        small = add_rows(
            send_rows(
                [lax.dynamic_slice_in_dim(small, places[k] * rows, rows) for k in range(4)]
            )
        ).astype(bf16)
    else:
        small = lax.psum_scatter(small, "tp", scatter_dimension=0, tiled=True)
    columns = acc_weights.shape[1]
    own_rows = MODEL_WIDTH // ep_size
    small_rows = rows // ep_size
    small = small.reshape(ep_size, small_rows * LANES)
    extra = -(-small.shape[1] // (8 * columns)) * 8
    small = jnp.pad(small, ((0, 0), (0, extra * columns - small.shape[1])))
    packed = jnp.concatenate(
        [
            acc_weights.astype(bf16).reshape(ep_size, own_rows, columns),
            small.reshape(ep_size, extra, columns),
        ],
        axis=1,
    )
    summed = rs_ep(packed.reshape(-1, columns)).astype(f32)
    split = local_heads * GROUP_COLS
    grad_qkv = summed[:own_rows, :split].reshape(own_rows, local_heads, GROUP_COLS)
    grad_out = summed[:own_rows, split:].T.reshape(local_heads, LANES, own_rows)
    small = summed[own_rows:].reshape(-1)[: small_rows * LANES].reshape(small_rows, LANES)
    grad_router = small[:, :EXPERTS]
    grad_gains = small[:, EXPERTS : EXPERTS + 2].T
    return (
        jnp.stack(outputs),
        jnp.stack(input_grads),
        grad_gains,
        grad_qkv,
        grad_out,
        grad_router,
        grad_gate_up,
        grad_down,
    )


def solution(mesh):
    placed = (
        P("ep", "tp", None),
        P("ep", "tp", None),
        P(),
        P("ep", "tp", None),
        P("tp", None, "ep"),
        P(),
        P("ep", "tp", None),
        P("ep", None, "tp"),
        P("ep", None),
        P("ep", "tp", None, None),
    )
    return jax.shard_map(
        shards,
        mesh=mesh,
        in_specs=placed,
        out_specs=(
            P("ep", "tp", None),
            P("ep", "tp", None),
            P(None, ("tp", "ep")),
            P("ep", "tp", None),
            P("tp", None, "ep"),
            P(("tp", "ep"), None),
            P("ep", "tp", None),
            P("ep", None, "tp"),
        ),
        check_vma=False,
    )
```

```python
import functools

import jax
import jax.numpy as jnp
from jax import lax
from jax.experimental import pallas as pl
from jax.experimental.pallas import tpu as pltpu
from jax.sharding import PartitionSpec as P

MODEL_WIDTH = 1024
HEAD_SIZE = 64
FF = 512
EXPERTS = 32
DOCS = 4
CAP = 96
LANES = 128
ROW_BLOCK = 256
GROUP_COLS = 256

epsilon = 1e-06
score_scale = 0.015625
residual_scale = 0.22
rope_base = 10000.0
masked_score = -1000000000.0

f32 = jnp.float32
bf16 = jnp.bfloat16

params = pltpu.CompilerParams(vmem_limit_bytes=58 * 1024 * 1024)
row_params = pltpu.CompilerParams(
    vmem_limit_bytes=58 * 1024 * 1024, dimension_semantics=("arbitrary",)
)


def cost(gflops, megabytes):
    return pl.CostEstimate(
        flops=int(gflops * 1e6), transcendentals=0, bytes_accessed=int(megabytes * 1e3)
    )


def after(value, *others):
    return lax.optimization_barrier((value, others))[0]


def dot(a, b):
    return jnp.dot(a, b, preferred_element_type=f32)


def dot_nt(a, b):
    return lax.dot_general(a, b, (((1,), (1,)), ((), ())), preferred_element_type=f32)


def dot_tn(a, b):
    return lax.dot_general(a, b, (((0,), (0,)), ((), ())), preferred_element_type=f32)


def lane_masks(rows):
    lane = lax.broadcasted_iota(jnp.int32, (rows, LANES), 1)
    return lane < HEAD_SIZE, (lane % HEAD_SIZE) < HEAD_SIZE // 2


def swap_halves(values, first):
    half = HEAD_SIZE // 2
    return jnp.where(first, pltpu.roll(values, LANES - half, 1), pltpu.roll(values, half, 1))


def for_blocks(count, body):
    if count <= 4:
        for index in range(count):
            body(index)
    else:

        def step(index, carry):
            body(index)
            return carry

        lax.fori_loop(0, count, step, 0)


def block_rows(index):
    if isinstance(index, int):
        return pl.ds(index * ROW_BLOCK, ROW_BLOCK)
    return pl.ds(pl.multiple_of(index * ROW_BLOCK, ROW_BLOCK), ROW_BLOCK)


def key_window(index, length):
    reach = -(-(length // 2) // ROW_BLOCK)
    if isinstance(index, int):
        start = max(0, index - reach) * ROW_BLOCK
        return start, (index + 1) * ROW_BLOCK - start
    start = jnp.maximum(index - reach, 0) * ROW_BLOCK
    return pl.multiple_of(start, ROW_BLOCK), (reach + 1) * ROW_BLOCK


def allowed_keys(index, start, width, seg_col_ref, seg_row_ref):
    query = lax.broadcasted_iota(jnp.int32, (ROW_BLOCK, width), 0) + index * ROW_BLOCK
    key = lax.broadcasted_iota(jnp.int32, (ROW_BLOCK, width), 1) + start
    same = seg_row_ref[:, pl.ds(start, width)] == seg_col_ref[block_rows(index), :]
    return (key <= query) & same


def place_rows(starts_ref, pieces, whole):
    for index, piece in enumerate(pieces):
        rows = piece.shape[0]
        begin = pl.multiple_of(starts_ref[index], ROW_BLOCK)
        whole[pl.ds(begin, rows), :] = piece[...]


def each_block(starts_ref, pieces):
    for index, piece in enumerate(pieces):
        for inner in range(0, piece.shape[0], ROW_BLOCK):
            begin = pl.multiple_of(starts_ref[index] + inner, ROW_BLOCK)
            yield pl.ds(begin, ROW_BLOCK), piece, slice(inner, inner + ROW_BLOCK)


def attention_forward_body(starts_ref, *refs, count):
    x_pieces = refs[:count]
    gain_ref, weights_ref, cos_ref, sin_ref, seg_col_ref, seg_row_ref = refs[count : count + 6]
    parts = refs[count + 6 : 2 * count + 6]
    qa_ref, qb_ref, kd_ref, vd_ref, ctx_ref, x_ref = refs[2 * count + 6 :]
    place_rows(starts_ref, x_pieces, x_ref)
    length = x_ref.shape[0]
    groups = weights_ref.shape[1] // (GROUP_COLS + LANES)
    low, first = lane_masks(ROW_BLOCK)

    def project(index):
        rows = block_rows(index)
        x = x_ref[rows, :].astype(f32)
        scale = lax.rsqrt(jnp.mean(x * x, axis=-1, keepdims=True) + epsilon)
        normed = (x * scale * gain_ref[...]).astype(bf16)
        projected = dot(normed, weights_ref[:, : groups * GROUP_COLS])
        cosine = cos_ref[rows, :]
        sine = sin_ref[rows, :]
        for group in range(groups):
            cols = slice(group * LANES, (group + 1) * LANES)
            query = projected[:, group * GROUP_COLS : group * GROUP_COLS + LANES]
            pair = projected[:, group * GROUP_COLS + LANES : (group + 1) * GROUP_COLS]
            query = (query * cosine + swap_halves(query, first) * sine) * score_scale
            qa_ref[rows, cols] = jnp.where(low, query, 0.0).astype(bf16)
            qb_ref[rows, cols] = jnp.where(low, 0.0, query).astype(bf16)
            turned = pair * cosine + swap_halves(pair, first) * sine
            kd_ref[rows, cols] = jnp.where(low, turned, pltpu.roll(turned, HEAD_SIZE, 1)).astype(
                bf16
            )
            vd_ref[rows, cols] = jnp.where(low, pltpu.roll(pair, HEAD_SIZE, 1), pair).astype(bf16)

    def attend(index):
        rows = block_rows(index)
        start, width = key_window(index, length)
        keys = pl.ds(start, width)
        allowed = allowed_keys(index, start, width, seg_col_ref, seg_row_ref)
        for group in range(groups):
            cols = slice(group * LANES, (group + 1) * LANES)
            heads = []
            for q_ref in (qa_ref, qb_ref):
                scores = dot_nt(q_ref[rows, cols], kd_ref[keys, cols])
                scores = jnp.where(allowed, scores, masked_score)
                expo = jnp.exp(scores - jnp.max(scores, axis=-1, keepdims=True))
                total = jnp.sum(expo, axis=-1, keepdims=True)
                probs = (expo * (1.0 / total)).astype(bf16)
                heads.append(dot(probs, vd_ref[keys, cols]))
            ctx_ref[rows, cols] = jnp.where(low, heads[0], heads[1]).astype(bf16)

    for_blocks(length // ROW_BLOCK, project)
    for_blocks(length // ROW_BLOCK, attend)
    for rows, part, inner in each_block(starts_ref, parts):
        part[inner, :] = dot_nt(ctx_ref[rows, :], weights_ref[:, groups * GROUP_COLS :]).astype(
            bf16
        )


def in_vmem(count):
    return [pl.BlockSpec(memory_space=pltpu.SMEM)] + [
        pl.BlockSpec(memory_space=pltpu.VMEM) for _ in range(count)
    ]


def attention_forward(starts, pieces, gain, weights, cosine, sine, seg_col, seg_row):
    length = cosine.shape[0]
    count = len(pieces)
    half = jax.ShapeDtypeStruct((length, weights.shape[1] // 3), bf16)
    results = pl.pallas_call(
        functools.partial(attention_forward_body, count=count),
        out_shape=tuple(jax.ShapeDtypeStruct(p.shape, bf16) for p in pieces) + (half,) * 5,
        in_specs=in_vmem(count + 6),
        scratch_shapes=[pltpu.VMEM((length, MODEL_WIDTH), bf16)],
        compiler_params=params,
        cost_estimate=cost(11.0, 40.0),
        name="attn_fwd",
    )(starts, *pieces, gain, weights, cosine, sine, seg_col, seg_row)
    return results[:count], results[count:]


def attention_backward_body(starts_ref, *refs, count):
    x_pieces, refs = refs[:count], refs[count:]
    gain_ref, weights_ref, cos_ref, sin_ref, seg_col_ref, seg_row_ref = refs[:6]
    qa_ref, qb_ref, kd_ref, vd_ref, ctx_ref = refs[6:11]
    gb_pieces, parts, refs = refs[11 : 11 + count], refs[11 + count : 11 + 2 * count], refs[
        11 + 2 * count :
    ]
    grad_ref, gain_grad_ref, gb_ref, norm_sc, proj_sc, dk_sc, dv_sc = refs
    place_rows(starts_ref, gb_pieces, gb_ref)
    length = gb_ref.shape[0]
    groups = weights_ref.shape[1] // (GROUP_COLS + LANES)
    split = groups * GROUP_COLS
    low, first = lane_masks(ROW_BLOCK)
    dk_sc[...] = jnp.zeros_like(dk_sc)
    dv_sc[...] = jnp.zeros_like(dv_sc)

    def attend(index):
        rows = block_rows(index)
        start, width = key_window(index, length)
        keys = pl.ds(start, width)
        allowed = allowed_keys(index, start, width, seg_col_ref, seg_row_ref)
        grad_context = dot(gb_ref[rows, :], weights_ref[:, split:])
        cosine = cos_ref[rows, :]
        sine = sin_ref[rows, :]
        for group in range(groups):
            cols = slice(group * LANES, (group + 1) * LANES)
            grad_group = grad_context[:, cols]
            grad_queries = []
            for head, q_ref in enumerate((qa_ref, qb_ref)):
                if head == 0:
                    grad_head = jnp.where(low, grad_group, 0.0).astype(bf16)
                else:
                    grad_head = jnp.where(low, 0.0, grad_group).astype(bf16)
                query = q_ref[rows, cols]
                scores = dot_nt(query, kd_ref[keys, cols])
                scores = jnp.where(allowed, scores, masked_score)
                expo = jnp.exp(scores - jnp.max(scores, axis=-1, keepdims=True))
                probs = expo * (1.0 / jnp.sum(expo, axis=-1, keepdims=True))
                grad_probs = dot_nt(grad_head, vd_ref[keys, cols])
                delta = jnp.sum(probs * grad_probs, axis=-1, keepdims=True)
                grad_scores = (probs * (grad_probs - delta)).astype(bf16)
                grad_queries.append(dot(grad_scores, kd_ref[keys, cols]))
                dk_sc[keys, cols] += dot_tn(grad_scores, query)
                dv_sc[keys, cols] += dot_tn(probs.astype(bf16), grad_head)
            grad_query = jnp.where(low, grad_queries[0], grad_queries[1]) * score_scale
            grad_query = grad_query * cosine - swap_halves(grad_query, first) * sine
            proj_sc[rows, group * GROUP_COLS : group * GROUP_COLS + LANES] = grad_query.astype(bf16)

    for_blocks(length // ROW_BLOCK, attend)
    gain_grad_ref[...] = jnp.zeros_like(gain_grad_ref)

    def finish(rows, part, inner, x_piece):
        cosine = cos_ref[rows, :]
        sine = sin_ref[rows, :]
        for group in range(groups):
            cols = slice(group * LANES, (group + 1) * LANES)
            grad_key = dk_sc[rows, cols]
            grad_key = grad_key + pltpu.roll(grad_key, HEAD_SIZE, 1)
            grad_key = grad_key * cosine - swap_halves(grad_key, first) * sine
            grad_value = dv_sc[rows, cols]
            grad_value = grad_value + pltpu.roll(grad_value, HEAD_SIZE, 1)
            proj_sc[rows, group * GROUP_COLS + LANES : (group + 1) * GROUP_COLS] = jnp.where(
                low, grad_key, grad_value
            ).astype(bf16)
        grad_normed = dot_nt(proj_sc[rows, :], weights_ref[:, :split])
        x = x_piece[inner, :].astype(f32)
        unit = x * lax.rsqrt(jnp.mean(x * x, axis=-1, keepdims=True) + epsilon)
        norm_sc[rows, :] = (unit * gain_ref[...]).astype(bf16)
        gain_grad_ref[...] += jnp.sum(grad_normed * unit, axis=0, keepdims=True)
        part[inner, :] = grad_normed.astype(bf16)

    if count > 1:
        for (rows, part, inner), x_piece in zip(each_block(starts_ref, parts), x_pieces):
            finish(rows, part, inner, x_piece)
    else:

        def whole_step(index):
            finish(block_rows(index), parts[0], block_rows(index), x_pieces[0])

        for_blocks(length // ROW_BLOCK, whole_step)
    grad_ref[:, :split] = dot_tn(norm_sc[...], proj_sc[...]).astype(bf16)
    grad_ref[:, split:] = dot_tn(gb_ref[...], ctx_ref[...]).astype(bf16)


def attention_backward(
    starts, pieces, gain, weights, cosine, sine, seg_col, seg_row, kept, grad_pieces
):
    length = cosine.shape[0]
    count = len(pieces)
    heads = weights.shape[1] // 3
    results = pl.pallas_call(
        functools.partial(attention_backward_body, count=count),
        out_shape=tuple(jax.ShapeDtypeStruct(p.shape, bf16) for p in pieces)
        + (
            jax.ShapeDtypeStruct(weights.shape, bf16),
            jax.ShapeDtypeStruct((1, MODEL_WIDTH), f32),
        ),
        in_specs=in_vmem(2 * count + 11),
        scratch_shapes=[
            pltpu.VMEM((length, MODEL_WIDTH), bf16),
            pltpu.VMEM((length, MODEL_WIDTH), bf16),
            pltpu.VMEM((length, 2 * heads), bf16),
            pltpu.VMEM((length, heads), f32),
            pltpu.VMEM((length, heads), f32),
        ],
        compiler_params=params,
        cost_estimate=cost(18.0, 65.0),
        name="attn_bwd",
    )(starts, *pieces, gain, weights, cosine, sine, seg_col, seg_row, *kept, *grad_pieces)
    return results[:count], results[count:]


def dispatch_body(offset_ref, *refs, local, count):
    ins, (router_ref, xd_ref, gd_ref, pt_ref, pgt_ref) = refs[:count], refs[count:]
    rows = ins[0].shape[0]
    slots = local * CAP
    if count == 1:
        x = ins[0][:, :MODEL_WIDTH]
        grad = ins[0][:, MODEL_WIDTH : 2 * MODEL_WIDTH]
        mask = ins[0][:, 2 * MODEL_WIDTH :]
    else:
        x = ins[0][...]
        grad = ins[1][:, :MODEL_WIDTH]
        mask = ins[1][:, MODEL_WIDTH:]
    chosen = mask.astype(f32) > 0.0
    logits = jnp.where(chosen, dot(x, router_ref[...]), masked_score)
    expo = jnp.where(chosen, jnp.exp(logits - jnp.max(logits, axis=-1, keepdims=True)), 0.0)
    gates = (expo / jnp.sum(expo, axis=-1, keepdims=True)).astype(bf16)
    earlier = lax.broadcasted_iota(jnp.int32, (rows, rows), 1) < lax.broadcasted_iota(
        jnp.int32, (rows, rows), 0
    )
    place = dot(jnp.where(earlier, 1.0, 0.0).astype(bf16), mask)
    place = jnp.where(chosen, place, -1.0).astype(bf16)
    offset = offset_ref[0]

    def pick(shape, slot_axis):
        slot = lax.broadcasted_iota(jnp.int32, shape, slot_axis)
        expert = lax.broadcasted_iota(jnp.int32, shape, 1 - slot_axis)
        hit = jnp.zeros(shape, jnp.bool_)
        for own in range(local):
            hit = hit | (
                (slot >= own * CAP) & (slot < (own + 1) * CAP) & (expert == offset + own)
            )
        return jnp.where(hit, 1.0, 0.0).astype(bf16)

    def in_slot(shape, slot_axis):
        slot = lax.broadcasted_iota(jnp.int32, shape, slot_axis)
        for own in range(1, local):
            slot = jnp.where(slot >= CAP, slot - CAP, slot)
        return slot.astype(f32)

    spread = pick((slots, LANES), 0)
    hit = dot_nt(spread, place) == in_slot((slots, rows), 0)
    send = jnp.where(hit, 1.0, 0.0).astype(bf16)
    send_gated = jnp.where(hit, dot_nt(spread, gates), 0.0).astype(bf16)
    xd_ref[...] = dot(send, x).astype(bf16).reshape(xd_ref.shape)
    gd_ref[...] = ((dot(send_gated, grad) * residual_scale).astype(bf16)).reshape(gd_ref.shape)
    spread = pick((LANES, slots), 1)
    hit = dot(place, spread) == in_slot((rows, slots), 1)
    pt_ref[...] = jnp.where(hit, 1.0, 0.0).astype(bf16)
    pgt_ref[...] = jnp.where(hit, dot(gates, spread), 0.0).astype(bf16)


def dispatch(offset, sources, router, local):
    total = sources[0].shape[0]
    blocks = total // ROW_BLOCK
    slots = local * CAP
    slotted = jax.ShapeDtypeStruct((local, blocks, CAP, MODEL_WIDTH), bf16)
    slotted_spec = pl.BlockSpec((local, 1, CAP, MODEL_WIDTH), lambda s, o: (0, s, 0, 0))
    return pl.pallas_call(
        functools.partial(dispatch_body, local=local, count=len(sources)),
        grid_spec=pltpu.PrefetchScalarGridSpec(
            num_scalar_prefetch=1,
            grid=(blocks,),
            in_specs=[
                pl.BlockSpec((ROW_BLOCK, source.shape[1]), lambda s, o: (s, 0))
                for source in sources
            ]
            + [pl.BlockSpec((MODEL_WIDTH, LANES), lambda s, o: (0, 0))],
            out_specs=[
                slotted_spec,
                slotted_spec,
                pl.BlockSpec((ROW_BLOCK, slots), lambda s, o: (s, 0)),
                pl.BlockSpec((ROW_BLOCK, slots), lambda s, o: (s, 0)),
            ],
        ),
        out_shape=(
            slotted,
            slotted,
            jax.ShapeDtypeStruct((total, slots), bf16),
            jax.ShapeDtypeStruct((total, slots), bf16),
        ),
        compiler_params=row_params,
        cost_estimate=cost(11.0, 40.0),
        name="dispatch",
    )(offset, *sources, router)


def pack_weights(gate_up, down):
    gu_rows = gate_up.shape[1]
    count = MODEL_WIDTH // gu_rows
    cut = FF // count
    side = [down[:, k * cut : (k + 1) * cut, :] for k in range(count)]
    return jnp.concatenate([gate_up, jnp.concatenate(side, axis=2)], axis=1)


def unpack_weights(packed, gu_rows):
    count = MODEL_WIDTH // gu_rows
    side = packed[:, gu_rows:]
    side = [side[:, :, k * gu_rows : (k + 1) * gu_rows] for k in range(count)]
    return packed[:, :gu_rows], jnp.concatenate(side, axis=1)


def experts_body(place_ref, xd_ref, gd_ref, *refs, base, slices, carried):
    paired = slices == 4
    kinds = 5 if paired else 1
    w_refs, refs = refs[:kinds], refs[kinds:]
    old, refs = (refs[:kinds], refs[kinds:]) if carried else ((), refs)
    out_ref, dx_ref, h_ref = refs[:3]
    grad_refs = refs[3 : 3 + kinds]
    wgu_ref, wd_ref, act_sc, dh_sc = refs[3 + kinds :]
    expert = pl.program_id(0)
    gu_rows = MODEL_WIDTH // slices
    cut = FF // slices

    def begin_of(index):
        if not paired:
            return index * gu_rows
        return pl.multiple_of(place_ref[1 + index] * gu_rows, LANES)

    def put(index, ref, *lead):
        begin = begin_of(index)
        wgu_ref[pl.ds(begin, gu_rows), :] = ref[(*lead, slice(0, gu_rows), slice(None))]
        for k in range(slices):
            wd_ref[k * cut : (k + 1) * cut, pl.ds(begin, gu_rows)] = ref[
                (*lead, slice(gu_rows, gu_rows + cut), slice(k * gu_rows, (k + 1) * gu_rows))
            ]

    if paired:
        for index in range(3):
            put(index, w_refs[index], 0)

        @pl.when(expert == 0)
        def _():
            put(3, w_refs[3], 0)

        @pl.when(expert == 1)
        def _():
            put(3, w_refs[4], 0)

    else:
        for index in range(slices):
            put(index, w_refs[0], index, 0)

    total = xd_ref.shape[1]
    chunk = ROW_BLOCK
    own = place_ref[0] + expert + base
    lane = lax.broadcasted_iota(jnp.int32, (chunk, LANES), 1)

    def chunk_step(index):
        rows = block_rows(index)
        hidden = dot(xd_ref[0, rows, :], wgu_ref[...])
        gate = hidden[:, :FF]
        up = hidden[:, FF:]
        sigmoid = jax.nn.sigmoid(gate)
        act = (gate * sigmoid * up).astype(bf16)
        act_sc[rows, :] = act
        out = dot(act, wd_ref[...]).astype(bf16)
        out_ref[0, rows, :] = out
        grad_out = gd_ref[0, rows, :]
        h = jnp.sum(grad_out.astype(f32) * out.astype(f32), axis=-1, keepdims=True)
        h_ref[0, rows, :] = jnp.where(lane == own, h, 0.0).astype(bf16)
        grad_act = dot_nt(grad_out, wd_ref[...])
        grad_gate = grad_act * up * sigmoid * (1.0 + gate * (1.0 - sigmoid))
        grad_up = grad_act * gate * sigmoid
        dh_sc[rows, :FF] = grad_gate.astype(bf16)
        dh_sc[rows, FF:] = grad_up.astype(bf16)
        dx_ref[0, rows, :] = dot_nt(dh_sc[rows, :], wgu_ref[...]).astype(bf16)

    for_blocks(total // chunk, chunk_step)

    def put_grad(kind, lead, gate_up, down):
        ref = grad_refs[kind]
        at = (*lead, slice(0, gu_rows), slice(None))
        if carried:
            gate_up = gate_up + old[kind][at].astype(f32)
        ref[at] = gate_up.astype(bf16)
        for k in range(slices):
            at = (*lead, slice(gu_rows, gu_rows + cut), slice(k * gu_rows, (k + 1) * gu_rows))
            value = down[k * cut : (k + 1) * cut, :]
            if carried:
                value = value + old[kind][at].astype(f32)
            ref[at] = value.astype(bf16)

    targets = (
        ((0, 0), (1, 0), (3, 0), (1, 1)),
        ((0, 1), (4, 0), (2, 0), (2, 1)),
    )
    for index in range(slices):
        begin = begin_of(index)
        gate_up = dot_tn(xd_ref[0, :, pl.ds(begin, gu_rows)], dh_sc[...])
        down = dot_tn(act_sc[...], gd_ref[0, :, pl.ds(begin, gu_rows)])
        if not paired:
            put_grad(0, (index, 0), gate_up, down)
            continue

        @pl.when(expert == 0)
        def _():
            kind, lead = targets[0][index]
            put_grad(kind, (lead,), gate_up, down)

        @pl.when(expert == 1)
        def _():
            kind, lead = targets[1][index]
            put_grad(kind, (lead,), gate_up, down)


def run_experts(place, xd, gd, pieces, old, base, here, slices):
    total = xd.shape[1]
    paired = slices == 4
    packed = (MODEL_WIDTH + FF) // slices

    def spec(rows, width, first=0):
        return pl.BlockSpec((1, rows, width), lambda e, o: (e + first, 0, 0))

    def fixed(count):
        return pl.BlockSpec((count, packed, MODEL_WIDTH), lambda e, o: (0, 0, 0))

    if paired:
        w_specs = [spec(packed, MODEL_WIDTH)] * 3 + [fixed(1)] * 2
        counts = (2, 2, 2, 1, 1)
        grad_specs = [fixed(count) for count in counts]
        grad_shapes = tuple(
            jax.ShapeDtypeStruct((count, packed, MODEL_WIDTH), bf16) for count in counts
        )
    else:
        w_specs = [pl.BlockSpec((slices, 1, packed, MODEL_WIDTH), lambda e, o: (0, e, 0, 0))]
        grad_specs = w_specs
        grad_shapes = (jax.ShapeDtypeStruct((slices, here, packed, MODEL_WIDTH), bf16),)
    results = pl.pallas_call(
        functools.partial(experts_body, base=base, slices=slices, carried=bool(old)),
        grid_spec=pltpu.PrefetchScalarGridSpec(
            num_scalar_prefetch=1,
            grid=(here,),
            in_specs=[spec(total, MODEL_WIDTH, base)] * 2 + w_specs + (grad_specs if old else []),
            out_specs=[spec(total, MODEL_WIDTH)] * 2 + [spec(total, LANES)] + grad_specs,
            scratch_shapes=[
                pltpu.VMEM((MODEL_WIDTH, 2 * FF), bf16),
                pltpu.VMEM((FF, MODEL_WIDTH), bf16),
                pltpu.VMEM((total, FF), bf16),
                pltpu.VMEM((total, 2 * FF), bf16),
            ],
        ),
        out_shape=(
            jax.ShapeDtypeStruct((here, total, MODEL_WIDTH), bf16),
            jax.ShapeDtypeStruct((here, total, MODEL_WIDTH), bf16),
            jax.ShapeDtypeStruct((here, total, LANES), bf16),
        )
        + grad_shapes,
        compiler_params=row_params,
        cost_estimate=cost(20.0, 60.0),
        name="experts",
    )(place, xd, gd, *pieces, *old)
    return results[:3], results[3:]


def whole_slots(refs, slots, width):
    return jnp.concatenate(
        [ref[...].reshape(slots // len(refs), width) for ref in refs], axis=0
    )


def combine_grad_body(*refs, count):
    dx_refs, h_refs, (pt_ref, grad_ref) = refs[:count], refs[count : 2 * count], refs[2 * count :]
    slots = pt_ref.shape[1]
    grad_ref[:, :MODEL_WIDTH] = dot(
        pt_ref[...], whole_slots(dx_refs, slots, MODEL_WIDTH)
    ).astype(bf16)
    grad_ref[:, MODEL_WIDTH:] = dot(pt_ref[...], whole_slots(h_refs, slots, LANES)).astype(bf16)


def combine_mix_body(*refs, count):
    out_refs, (pgt_ref, mix_ref) = refs[:count], refs[count:]
    mix_ref[...] = dot(
        pgt_ref[...], whole_slots(out_refs, pgt_ref.shape[1], MODEL_WIDTH)
    ).astype(bf16)


def combine_both_body(*refs, count):
    out_refs, dx_refs, refs = refs[:count], refs[count : 2 * count], refs[2 * count :]
    h_refs, (pgt_ref, pt_ref, both_ref) = refs[:count], refs[count:]
    slots = pt_ref.shape[1]
    both_ref[:, :MODEL_WIDTH] = dot(
        pgt_ref[...], whole_slots(out_refs, slots, MODEL_WIDTH)
    ).astype(bf16)
    both_ref[:, MODEL_WIDTH : 2 * MODEL_WIDTH] = dot(
        pt_ref[...], whole_slots(dx_refs, slots, MODEL_WIDTH)
    ).astype(bf16)
    both_ref[:, 2 * MODEL_WIDTH :] = dot(
        pt_ref[...], whole_slots(h_refs, slots, LANES)
    ).astype(bf16)


def combine(body, arrays, count, tables, width, name):
    total, slots = tables[0].shape
    blocks = total // ROW_BLOCK
    arrays = [array.reshape(array.shape[0], blocks, CAP, array.shape[-1]) for array in arrays]
    in_specs = [
        pl.BlockSpec((array.shape[0], 1, CAP, array.shape[-1]), lambda s: (0, s, 0, 0))
        for array in arrays
    ]
    return pl.pallas_call(
        functools.partial(body, count=count),
        grid=(blocks,),
        in_specs=in_specs + [pl.BlockSpec((ROW_BLOCK, slots), lambda s: (s, 0))] * len(tables),
        out_specs=pl.BlockSpec((ROW_BLOCK, width), lambda s: (s, 0)),
        out_shape=jax.ShapeDtypeStruct((total, width), bf16),
        compiler_params=row_params,
        cost_estimate=cost(5.0, 17.0),
        name=name,
    )(*arrays, *tables)


def flip(value, bits):
    return lax.ppermute(value, "tp", [(t, t ^ bits) for t in range(4)])


def square():
    return lax.axis_size("tp") == 4


def tp_places():
    me = lax.axis_index("tp").astype(jnp.int32)
    if square():
        return jnp.stack([me ^ bits for bits in range(4)])
    return jnp.zeros((1,), jnp.int32)


def gather_rows(value):
    if square():
        return [value] + [flip(value, bits) for bits in (1, 2, 3)]
    return [lax.all_gather(value, "tp", axis=0, tiled=True)]


def send_rows(parts):
    if square():
        return [parts[0]] + [flip(parts[bits], bits) for bits in (1, 2, 3)]
    return [lax.psum_scatter(parts[0], "tp", scatter_dimension=0, tiled=True)]


def add_rows(came):
    total = came[0].astype(f32)
    for part in came[1:]:
        total = total + part.astype(f32)
    return total


def gather_weights_near(packed):
    if square():
        return [packed, flip(packed, 1), flip(packed, 2)]
    return [lax.all_gather(packed, "tp")]


def gather_weights_far(near):
    if square():
        return [*near, flip(near[2][:1], 1), flip(near[1][1:], 2)]
    return near


def sum_weights_near(grads):
    if square():
        return [flip(grads[1], 1), flip(grads[2], 2), *grads]
    return [lax.psum_scatter(grads[0], "tp", scatter_dimension=0)]


def sum_weights_far(near):
    if square():
        came_x, came_y, own, _, _, kept_y, kept_x = [value.astype(f32) for value in near]
        first = came_x[:1] + own[:1]
        second = came_y[:1] + own[1:]
        far_first = flip((came_x[1:] + kept_y).astype(bf16), 2)
        far_second = flip((came_y[1:] + kept_x).astype(bf16), 1)
        return [first, second, far_first, far_second]
    return near


def add_far(far):
    if square():
        first, second, far_first, far_second = far
        return jnp.concatenate([first + far_first, second + far_second])
    return far[0].astype(f32)


def ag_ep(value, axis=0):
    return lax.all_gather(value, "ep", axis=axis, tiled=True)


def rs_ep(value, axis=0):
    return lax.psum_scatter(value, "ep", scatter_dimension=axis, tiled=True)


def rope_tables(segment_row):
    onehot = (segment_row[:, None] == jnp.arange(DOCS, dtype=jnp.int32)[None, :]).astype(jnp.int32)
    doc_len = jnp.sum(onehot, axis=0)
    starts = [jnp.sum(doc_len[:doc]) for doc in range(DOCS)]
    begin = jnp.zeros_like(segment_row)
    for doc in range(1, DOCS):
        begin = jnp.where(segment_row == doc, starts[doc], begin)
    positions = jnp.arange(segment_row.shape[0], dtype=jnp.int32) - begin
    lane = jnp.arange(LANES, dtype=jnp.int32)
    halves = HEAD_SIZE // 2
    freqs = rope_base ** (-((lane % halves).astype(f32) * 2.0) / HEAD_SIZE)
    angles = positions.astype(f32)[:, None] * freqs[None, :]
    sign = jnp.where((lane % HEAD_SIZE) < halves, -1.0, 1.0).astype(f32)
    return jnp.cos(angles), jnp.sin(angles) * sign[None, :]


def shards(
    tokens,
    cotangent,
    norm_gains,
    query_key_value_weight,
    output_weight,
    w_router,
    w_gate_up,
    w_down,
    segment_ids,
    routes,
):
    micro, rows = tokens.shape[:2]
    local_heads = query_key_value_weight.shape[1]
    local = w_gate_up.shape[0]
    ep_size = lax.axis_size("ep")
    offset = (lax.axis_index("ep") * local).astype(jnp.int32).reshape(1)
    places = tp_places()
    starts = places * ROW_BLOCK
    place = jnp.concatenate([offset, places])
    gain_one = norm_gains[0:1]
    gain_two = norm_gains[1:2]
    router = jnp.pad(w_router, ((0, 0), (0, LANES - EXPERTS)))

    slices = lax.axis_size("tp")
    weights = ag_ep(
        jnp.concatenate(
            [
                query_key_value_weight.reshape(query_key_value_weight.shape[0], -1),
                output_weight.reshape(-1, output_weight.shape[2]).T,
            ],
            axis=1,
        )
    )
    lanes = jnp.arange(LANES, dtype=jnp.int32)
    masks = jnp.any(
        routes.reshape(micro, rows, -1)[..., None] == lanes, axis=2
    ).astype(bf16)
    tables = [rope_tables(segment_ids[m]) for m in range(micro)]
    packed_weights = pack_weights(w_gate_up, w_down)
    here = local // 2
    halves = range(2)
    packed_weights = [packed_weights[h * here : (h + 1) * here] for h in halves]

    token_full = []
    for m in range(micro):
        own = after(tokens[m], token_full[-1], tables) if token_full else tokens[m]
        token_full.append(gather_rows(own))
    weights = after(weights, token_full[0], tables)
    fixed = []
    for m in range(micro):
        fixed.append(
            (
                starts, token_full[m], gain_one, weights, tables[m][0], tables[m][1],
                segment_ids[m][:, None], segment_ids[m][None, :],
            )
        )
    came = []
    kept = []
    hiddens = []
    normed_twos = []
    scales = []
    gate_rows = []
    full = []
    for m in range(micro):
        if m:
            fixed[m] = (after(starts, normed_twos), *fixed[m][1:])
        parts, saved = attention_forward(*fixed[m])
        kept.append(saved)
        came.append(send_rows(parts))
        if m == 0:
            near = [gather_weights_near(after(packed_weights[0], came[0]))]
        branch = add_rows(came[m])
        hidden = tokens[m].astype(f32) + residual_scale * branch
        scale_two = lax.rsqrt(jnp.mean(hidden * hidden, axis=-1, keepdims=True) + epsilon)
        normed_two = (hidden * scale_two * gain_two).astype(bf16)
        logits = jnp.where(masks[m] > 0, dot(normed_two, router), masked_score)
        expo = jnp.where(
            masks[m] > 0, jnp.exp(logits - jnp.max(logits, axis=-1, keepdims=True)), 0.0
        )
        gate_rows.append(expo / jnp.sum(expo, axis=-1, keepdims=True))
        hiddens.append(hidden)
        normed_twos.append(normed_two)
        scales.append(scale_two)
        if m == 0:
            gm = jnp.concatenate([cotangent[m], masks[m]], axis=-1)
            gm = ag_ep(after(gm, weights))
            full.append([ag_ep(after(normed_two, gm)), gm])
        else:
            if m == micro - 1:
                normed_two, near[0] = lax.optimization_barrier((normed_two, near[0]))
            full.append([ag_ep(jnp.concatenate([normed_two, cotangent[m], masks[m]], axis=-1))])

    pieces = [gather_weights_far(near[0])]
    near.append(gather_weights_near(after(packed_weights[1], near[0])))
    old = [(), ()]
    mixes = []
    grads = []
    ready = ()
    for m in range(micro):
        sources = after(full[m], ready) if m else full[m]
        xd, gd, pt, pgt = dispatch(offset, sources, router, local)
        if m == 0:
            xd, near[1] = lax.optimization_barrier((xd, near[1]))
            pieces.append(gather_weights_far(near[1]))
        merged = (local, ep_size * CAP, MODEL_WIDTH)
        xd = xd.reshape(merged)
        gd = gd.reshape(merged)
        done = []
        for h in halves:
            results, old[h] = run_experts(
                place, xd, gd, pieces[h], old[h], h * here, here, slices
            )
            done.append(results)
        outs, dxs, hs = zip(*done)
        if m < micro - 1:
            both = combine(
                combine_both_body, [*outs, *dxs, *hs], 2, [pgt, pt], 2 * MODEL_WIDTH + LANES,
                "combine",
            )
            ready = both
            both = rs_ep(both)
            mixes.append(both[:, :MODEL_WIDTH])
            grads.append(both[:, MODEL_WIDTH:])
        else:
            grad = combine(
                combine_grad_body, [*dxs, *hs], 2, [pt], MODEL_WIDTH + LANES, "combine_grad"
            )
            grads.append(rs_ep(grad))
            near_first = sum_weights_near(old[0])
            outs, pgt, near_first = lax.optimization_barrier((*after((outs, pgt), grad), near_first))
            mix = combine(combine_mix_body, outs, 2, [pgt], MODEL_WIDTH, "combine_mix")
            mixes.append(rs_ep(mix))
    far_first = sum_weights_far(near_first)
    input_grads = []
    acc_router = 0.0
    acc_gain_one = 0.0
    acc_gain_two = 0.0
    acc_weights = 0.0
    parts = ()
    for m in range(micro):
        grad = after(grads[m], mix, parts)
        grad = grad.astype(f32)
        h_rows = grad[:, MODEL_WIDTH:]
        grad_logits = (
            h_rows - gate_rows[m] * jnp.sum(h_rows, axis=-1, keepdims=True)
        ).astype(bf16)
        acc_router = acc_router + dot_tn(normed_twos[m], grad_logits)
        grad_normed = grad[:, :MODEL_WIDTH] + dot_nt(grad_logits, router)
        scale = scales[m]
        weighted = grad_normed * gain_two
        inner = jnp.mean(weighted * hiddens[m], axis=-1, keepdims=True)
        grad_hidden = (
            cotangent[m].astype(f32)
            + scale * weighted
            - hiddens[m] * scale * scale * scale * inner
        )
        acc_gain_two = acc_gain_two + jnp.sum(grad_normed * hiddens[m] * scale, axis=0)
        grad_branch = gather_rows((residual_scale * grad_hidden).astype(bf16))
        if m == 0:
            near_second = sum_weights_near(after(old[1], grad_branch))
            grad_branch, far_first = lax.optimization_barrier((grad_branch, far_first))
        if m == micro - 1:
            near_second, grad_branch = lax.optimization_barrier((near_second, grad_branch))
            far_second = sum_weights_far(near_second)
        parts, (gweights, ggain) = attention_backward(*fixed[m], kept[m], grad_branch)
        back = send_rows(parts)
        if m == micro - 1:
            gweights, far_second = lax.optimization_barrier((gweights, far_second))
        acc_weights = acc_weights + gweights.astype(f32)
        acc_gain_one = acc_gain_one + ggain[0]
        grad_normed = add_rows(back)
        inputs = tokens[m].astype(f32)
        scale = lax.rsqrt(jnp.mean(inputs * inputs, axis=-1, keepdims=True) + epsilon)
        weighted = grad_normed * gain_one
        inner = jnp.mean(weighted * inputs, axis=-1, keepdims=True)
        input_grads.append(
            grad_hidden + scale * weighted - inputs * scale * scale * scale * inner
        )
    hiddens, mixes, far_first = after((hiddens, mixes, far_first), parts)
    outputs = [
        (hiddens[m] + residual_scale * mixes[m].astype(f32)).astype(bf16) for m in range(micro)
    ]
    grad_gate_up, grad_down = unpack_weights(
        jnp.concatenate([add_far(far_first), add_far(far_second)]), w_gate_up.shape[1]
    )

    small = jnp.concatenate(
        [
            acc_router[:, :EXPERTS],
            acc_gain_one[:, None],
            acc_gain_two[:, None],
            jnp.zeros((MODEL_WIDTH, LANES - EXPERTS - 2), f32),
        ],
        axis=-1,
    ).astype(bf16)
    rows = MODEL_WIDTH // lax.axis_size("tp")
    if square():
        small = add_rows(
            send_rows(
                [lax.dynamic_slice_in_dim(small, places[k] * rows, rows) for k in range(4)]
            )
        ).astype(bf16)
    else:
        small = lax.psum_scatter(small, "tp", scatter_dimension=0, tiled=True)
    columns = acc_weights.shape[1]
    own_rows = MODEL_WIDTH // ep_size
    small_rows = rows // ep_size
    small = small.reshape(ep_size, small_rows * LANES)
    extra = -(-small.shape[1] // (8 * columns)) * 8
    small = jnp.pad(small, ((0, 0), (0, extra * columns - small.shape[1])))
    packed = jnp.concatenate(
        [
            acc_weights.astype(bf16).reshape(ep_size, own_rows, columns),
            small.reshape(ep_size, extra, columns),
        ],
        axis=1,
    )
    summed = rs_ep(packed.reshape(-1, columns)).astype(f32)
    split = local_heads * GROUP_COLS
    grad_qkv = summed[:own_rows, :split].reshape(own_rows, local_heads, GROUP_COLS)
    grad_out = summed[:own_rows, split:].T.reshape(local_heads, LANES, own_rows)
    small = summed[own_rows:].reshape(-1)[: small_rows * LANES].reshape(small_rows, LANES)
    grad_router = small[:, :EXPERTS]
    grad_gains = small[:, EXPERTS : EXPERTS + 2].T
    return (
        jnp.stack(outputs),
        jnp.stack(input_grads),
        grad_gains,
        grad_qkv,
        grad_out,
        grad_router,
        grad_gate_up,
        grad_down,
    )


def solution(mesh):
    placed = (
        P("ep", "tp", None),
        P("ep", "tp", None),
        P(),
        P("ep", "tp", None),
        P("tp", None, "ep"),
        P(),
        P("ep", "tp", None),
        P("ep", None, "tp"),
        P("ep", None),
        P("ep", "tp", None, None),
    )
    return jax.shard_map(
        shards,
        mesh=mesh,
        in_specs=placed,
        out_specs=(
            P("ep", "tp", None),
            P("ep", "tp", None),
            P(None, ("tp", "ep")),
            P("ep", "tp", None),
            P("tp", None, "ep"),
            P(("tp", "ep"), None),
            P("ep", "tp", None),
            P("ep", None, "tp"),
        ),
        check_vma=False,
    )
```

```python
import functools

import jax
import jax.numpy as jnp
from jax import lax
from jax.experimental import pallas as pl
from jax.experimental.pallas import tpu as pltpu
from jax.sharding import PartitionSpec as P

MODEL_WIDTH = 1024
HEAD_SIZE = 64
FF = 512
EXPERTS = 32
DOCS = 4
CAP = 96
LANES = 128
ROW_BLOCK = 256
GROUP_COLS = 256

epsilon = 1e-06
score_scale = 0.015625
residual_scale = 0.22
rope_base = 10000.0
masked_score = -1000000000.0

f32 = jnp.float32
bf16 = jnp.bfloat16

params = pltpu.CompilerParams(vmem_limit_bytes=58 * 1024 * 1024)
row_params = pltpu.CompilerParams(
    vmem_limit_bytes=58 * 1024 * 1024, dimension_semantics=("arbitrary",)
)


def cost(gflops, megabytes):
    return pl.CostEstimate(
        flops=int(gflops * 1e6), transcendentals=0, bytes_accessed=int(megabytes * 1e3)
    )


def after(value, *others):
    return lax.optimization_barrier((value, others))[0]


def dot(a, b):
    return jnp.dot(a, b, preferred_element_type=f32)


def dot_nt(a, b):
    return lax.dot_general(a, b, (((1,), (1,)), ((), ())), preferred_element_type=f32)


def dot_tn(a, b):
    return lax.dot_general(a, b, (((0,), (0,)), ((), ())), preferred_element_type=f32)


def lane_masks(rows):
    lane = lax.broadcasted_iota(jnp.int32, (rows, LANES), 1)
    return lane < HEAD_SIZE, (lane % HEAD_SIZE) < HEAD_SIZE // 2


def swap_halves(values, first):
    half = HEAD_SIZE // 2
    return jnp.where(first, pltpu.roll(values, LANES - half, 1), pltpu.roll(values, half, 1))


def for_blocks(count, body):
    if count <= 4:
        for index in range(count):
            body(index)
    else:

        def step(index, carry):
            body(index)
            return carry

        lax.fori_loop(0, count, step, 0)


def block_rows(index):
    if isinstance(index, int):
        return pl.ds(index * ROW_BLOCK, ROW_BLOCK)
    return pl.ds(pl.multiple_of(index * ROW_BLOCK, ROW_BLOCK), ROW_BLOCK)


def key_window(index, length):
    reach = -(-(length // 2) // ROW_BLOCK)
    if isinstance(index, int):
        start = max(0, index - reach) * ROW_BLOCK
        return start, (index + 1) * ROW_BLOCK - start
    start = jnp.maximum(index - reach, 0) * ROW_BLOCK
    return pl.multiple_of(start, ROW_BLOCK), (reach + 1) * ROW_BLOCK


def allowed_keys(index, start, width, seg_col_ref, seg_row_ref):
    query = lax.broadcasted_iota(jnp.int32, (ROW_BLOCK, width), 0) + index * ROW_BLOCK
    key = lax.broadcasted_iota(jnp.int32, (ROW_BLOCK, width), 1) + start
    same = seg_row_ref[:, pl.ds(start, width)] == seg_col_ref[block_rows(index), :]
    return (key <= query) & same


def place_rows(starts_ref, pieces, whole):
    for index, piece in enumerate(pieces):
        rows = piece.shape[0]
        begin = pl.multiple_of(starts_ref[index], ROW_BLOCK)
        whole[pl.ds(begin, rows), :] = piece[...]


def each_block(starts_ref, pieces):
    for index, piece in enumerate(pieces):
        for inner in range(0, piece.shape[0], ROW_BLOCK):
            begin = pl.multiple_of(starts_ref[index] + inner, ROW_BLOCK)
            yield pl.ds(begin, ROW_BLOCK), piece, slice(inner, inner + ROW_BLOCK)


def attention_forward_body(starts_ref, *refs, count):
    x_pieces = refs[:count]
    gain_ref, weights_ref, cos_ref, sin_ref, seg_col_ref, seg_row_ref = refs[count : count + 6]
    parts = refs[count + 6 : 2 * count + 6]
    qa_ref, qb_ref, kd_ref, vd_ref, ctx_ref, x_ref = refs[2 * count + 6 :]
    place_rows(starts_ref, x_pieces, x_ref)
    length = x_ref.shape[0]
    groups = weights_ref.shape[1] // (GROUP_COLS + LANES)
    low, first = lane_masks(ROW_BLOCK)

    def project(index):
        rows = block_rows(index)
        x = x_ref[rows, :].astype(f32)
        scale = lax.rsqrt(jnp.mean(x * x, axis=-1, keepdims=True) + epsilon)
        normed = (x * scale * gain_ref[...]).astype(bf16)
        projected = dot(normed, weights_ref[:, : groups * GROUP_COLS])
        cosine = cos_ref[rows, :]
        sine = sin_ref[rows, :]
        for group in range(groups):
            cols = slice(group * LANES, (group + 1) * LANES)
            query = projected[:, group * GROUP_COLS : group * GROUP_COLS + LANES]
            pair = projected[:, group * GROUP_COLS + LANES : (group + 1) * GROUP_COLS]
            query = (query * cosine + swap_halves(query, first) * sine) * score_scale
            qa_ref[rows, cols] = jnp.where(low, query, 0.0).astype(bf16)
            qb_ref[rows, cols] = jnp.where(low, 0.0, query).astype(bf16)
            turned = pair * cosine + swap_halves(pair, first) * sine
            kd_ref[rows, cols] = jnp.where(low, turned, pltpu.roll(turned, HEAD_SIZE, 1)).astype(
                bf16
            )
            vd_ref[rows, cols] = jnp.where(low, pltpu.roll(pair, HEAD_SIZE, 1), pair).astype(bf16)

    def attend(index):
        rows = block_rows(index)
        start, width = key_window(index, length)
        keys = pl.ds(start, width)
        allowed = allowed_keys(index, start, width, seg_col_ref, seg_row_ref)
        for group in range(groups):
            cols = slice(group * LANES, (group + 1) * LANES)
            heads = []
            for q_ref in (qa_ref, qb_ref):
                scores = dot_nt(q_ref[rows, cols], kd_ref[keys, cols])
                scores = jnp.where(allowed, scores, masked_score)
                expo = jnp.exp(scores - jnp.max(scores, axis=-1, keepdims=True))
                total = jnp.sum(expo, axis=-1, keepdims=True)
                probs = (expo * (1.0 / total)).astype(bf16)
                heads.append(dot(probs, vd_ref[keys, cols]))
            ctx_ref[rows, cols] = jnp.where(low, heads[0], heads[1]).astype(bf16)

    for_blocks(length // ROW_BLOCK, project)
    for_blocks(length // ROW_BLOCK, attend)
    for rows, part, inner in each_block(starts_ref, parts):
        part[inner, :] = dot_nt(ctx_ref[rows, :], weights_ref[:, groups * GROUP_COLS :]).astype(
            bf16
        )


def in_vmem(count):
    return [pl.BlockSpec(memory_space=pltpu.SMEM)] + [
        pl.BlockSpec(memory_space=pltpu.VMEM) for _ in range(count)
    ]


def attention_forward(starts, pieces, gain, weights, cosine, sine, seg_col, seg_row):
    length = cosine.shape[0]
    count = len(pieces)
    half = jax.ShapeDtypeStruct((length, weights.shape[1] // 3), bf16)
    results = pl.pallas_call(
        functools.partial(attention_forward_body, count=count),
        out_shape=tuple(jax.ShapeDtypeStruct(p.shape, bf16) for p in pieces) + (half,) * 5,
        in_specs=in_vmem(count + 6),
        scratch_shapes=[pltpu.VMEM((length, MODEL_WIDTH), bf16)],
        compiler_params=params,
        cost_estimate=cost(11.0, 40.0),
        name="attn_fwd",
    )(starts, *pieces, gain, weights, cosine, sine, seg_col, seg_row)
    return results[:count], results[count:]


def attention_backward_body(starts_ref, *refs, count):
    x_pieces, refs = refs[:count], refs[count:]
    gain_ref, weights_ref, cos_ref, sin_ref, seg_col_ref, seg_row_ref = refs[:6]
    qa_ref, qb_ref, kd_ref, vd_ref, ctx_ref = refs[6:11]
    gb_pieces, parts, refs = refs[11 : 11 + count], refs[11 + count : 11 + 2 * count], refs[
        11 + 2 * count :
    ]
    grad_ref, gain_grad_ref, gb_ref, norm_sc, proj_sc, dk_sc, dv_sc = refs
    place_rows(starts_ref, gb_pieces, gb_ref)
    length = gb_ref.shape[0]
    groups = weights_ref.shape[1] // (GROUP_COLS + LANES)
    split = groups * GROUP_COLS
    low, first = lane_masks(ROW_BLOCK)
    dk_sc[...] = jnp.zeros_like(dk_sc)
    dv_sc[...] = jnp.zeros_like(dv_sc)

    def attend(index):
        rows = block_rows(index)
        start, width = key_window(index, length)
        keys = pl.ds(start, width)
        allowed = allowed_keys(index, start, width, seg_col_ref, seg_row_ref)
        grad_context = dot(gb_ref[rows, :], weights_ref[:, split:])
        cosine = cos_ref[rows, :]
        sine = sin_ref[rows, :]
        for group in range(groups):
            cols = slice(group * LANES, (group + 1) * LANES)
            grad_group = grad_context[:, cols]
            grad_queries = []
            for head, q_ref in enumerate((qa_ref, qb_ref)):
                if head == 0:
                    grad_head = jnp.where(low, grad_group, 0.0).astype(bf16)
                else:
                    grad_head = jnp.where(low, 0.0, grad_group).astype(bf16)
                query = q_ref[rows, cols]
                scores = dot_nt(query, kd_ref[keys, cols])
                scores = jnp.where(allowed, scores, masked_score)
                expo = jnp.exp(scores - jnp.max(scores, axis=-1, keepdims=True))
                probs = expo * (1.0 / jnp.sum(expo, axis=-1, keepdims=True))
                grad_probs = dot_nt(grad_head, vd_ref[keys, cols])
                delta = jnp.sum(probs * grad_probs, axis=-1, keepdims=True)
                grad_scores = (probs * (grad_probs - delta)).astype(bf16)
                grad_queries.append(dot(grad_scores, kd_ref[keys, cols]))
                dk_sc[keys, cols] += dot_tn(grad_scores, query)
                dv_sc[keys, cols] += dot_tn(probs.astype(bf16), grad_head)
            grad_query = jnp.where(low, grad_queries[0], grad_queries[1]) * score_scale
            grad_query = grad_query * cosine - swap_halves(grad_query, first) * sine
            proj_sc[rows, group * GROUP_COLS : group * GROUP_COLS + LANES] = grad_query.astype(bf16)

    for_blocks(length // ROW_BLOCK, attend)
    gain_grad_ref[...] = jnp.zeros_like(gain_grad_ref)

    def finish(rows, part, inner, x_piece):
        cosine = cos_ref[rows, :]
        sine = sin_ref[rows, :]
        for group in range(groups):
            cols = slice(group * LANES, (group + 1) * LANES)
            grad_key = dk_sc[rows, cols]
            grad_key = grad_key + pltpu.roll(grad_key, HEAD_SIZE, 1)
            grad_key = grad_key * cosine - swap_halves(grad_key, first) * sine
            grad_value = dv_sc[rows, cols]
            grad_value = grad_value + pltpu.roll(grad_value, HEAD_SIZE, 1)
            proj_sc[rows, group * GROUP_COLS + LANES : (group + 1) * GROUP_COLS] = jnp.where(
                low, grad_key, grad_value
            ).astype(bf16)
        grad_normed = dot_nt(proj_sc[rows, :], weights_ref[:, :split])
        x = x_piece[inner, :].astype(f32)
        unit = x * lax.rsqrt(jnp.mean(x * x, axis=-1, keepdims=True) + epsilon)
        norm_sc[rows, :] = (unit * gain_ref[...]).astype(bf16)
        gain_grad_ref[...] += jnp.sum(grad_normed * unit, axis=0, keepdims=True)
        part[inner, :] = grad_normed.astype(bf16)

    if count > 1:
        for (rows, part, inner), x_piece in zip(each_block(starts_ref, parts), x_pieces):
            finish(rows, part, inner, x_piece)
    else:

        def whole_step(index):
            finish(block_rows(index), parts[0], block_rows(index), x_pieces[0])

        for_blocks(length // ROW_BLOCK, whole_step)
    grad_ref[:, :split] = dot_tn(norm_sc[...], proj_sc[...]).astype(bf16)
    grad_ref[:, split:] = dot_tn(gb_ref[...], ctx_ref[...]).astype(bf16)


def attention_backward(
    starts, pieces, gain, weights, cosine, sine, seg_col, seg_row, kept, grad_pieces
):
    length = cosine.shape[0]
    count = len(pieces)
    heads = weights.shape[1] // 3
    results = pl.pallas_call(
        functools.partial(attention_backward_body, count=count),
        out_shape=tuple(jax.ShapeDtypeStruct(p.shape, bf16) for p in pieces)
        + (
            jax.ShapeDtypeStruct(weights.shape, bf16),
            jax.ShapeDtypeStruct((1, MODEL_WIDTH), f32),
        ),
        in_specs=in_vmem(2 * count + 11),
        scratch_shapes=[
            pltpu.VMEM((length, MODEL_WIDTH), bf16),
            pltpu.VMEM((length, MODEL_WIDTH), bf16),
            pltpu.VMEM((length, 2 * heads), bf16),
            pltpu.VMEM((length, heads), f32),
            pltpu.VMEM((length, heads), f32),
        ],
        compiler_params=params,
        cost_estimate=cost(18.0, 65.0),
        name="attn_bwd",
    )(starts, *pieces, gain, weights, cosine, sine, seg_col, seg_row, *kept, *grad_pieces)
    return results[:count], results[count:]


def dispatch_body(offset_ref, *refs, local, count):
    ins, (router_ref, xd_ref, gd_ref, pt_ref, pgt_ref) = refs[:count], refs[count:]
    rows = ins[0].shape[0]
    slots = local * CAP
    if count == 1:
        x = ins[0][:, :MODEL_WIDTH]
        grad = ins[0][:, MODEL_WIDTH : 2 * MODEL_WIDTH]
        mask = ins[0][:, 2 * MODEL_WIDTH :]
    else:
        x = ins[0][...]
        grad = ins[1][:, :MODEL_WIDTH]
        mask = ins[1][:, MODEL_WIDTH:]
    chosen = mask.astype(f32) > 0.0
    logits = jnp.where(chosen, dot(x, router_ref[...]), masked_score)
    expo = jnp.where(chosen, jnp.exp(logits - jnp.max(logits, axis=-1, keepdims=True)), 0.0)
    gates = (expo / jnp.sum(expo, axis=-1, keepdims=True)).astype(bf16)
    earlier = lax.broadcasted_iota(jnp.int32, (rows, rows), 1) < lax.broadcasted_iota(
        jnp.int32, (rows, rows), 0
    )
    place = dot(jnp.where(earlier, 1.0, 0.0).astype(bf16), mask)
    place = jnp.where(chosen, place, -1.0).astype(bf16)
    offset = offset_ref[0]

    def pick(shape, slot_axis):
        slot = lax.broadcasted_iota(jnp.int32, shape, slot_axis)
        expert = lax.broadcasted_iota(jnp.int32, shape, 1 - slot_axis)
        hit = jnp.zeros(shape, jnp.bool_)
        for own in range(local):
            hit = hit | (
                (slot >= own * CAP) & (slot < (own + 1) * CAP) & (expert == offset + own)
            )
        return jnp.where(hit, 1.0, 0.0).astype(bf16)

    def in_slot(shape, slot_axis):
        slot = lax.broadcasted_iota(jnp.int32, shape, slot_axis)
        for own in range(1, local):
            slot = jnp.where(slot >= CAP, slot - CAP, slot)
        return slot.astype(f32)

    spread = pick((slots, LANES), 0)
    hit = dot_nt(spread, place) == in_slot((slots, rows), 0)
    send = jnp.where(hit, 1.0, 0.0).astype(bf16)
    send_gated = jnp.where(hit, dot_nt(spread, gates), 0.0).astype(bf16)
    xd_ref[...] = dot(send, x).astype(bf16).reshape(xd_ref.shape)
    gd_ref[...] = ((dot(send_gated, grad) * residual_scale).astype(bf16)).reshape(gd_ref.shape)
    spread = pick((LANES, slots), 1)
    hit = dot(place, spread) == in_slot((rows, slots), 1)
    pt_ref[...] = jnp.where(hit, 1.0, 0.0).astype(bf16)
    pgt_ref[...] = jnp.where(hit, dot(gates, spread), 0.0).astype(bf16)


def dispatch(offset, sources, router, local):
    total = sources[0].shape[0]
    blocks = total // ROW_BLOCK
    slots = local * CAP
    slotted = jax.ShapeDtypeStruct((local, blocks, CAP, MODEL_WIDTH), bf16)
    slotted_spec = pl.BlockSpec((local, 1, CAP, MODEL_WIDTH), lambda s, o: (0, s, 0, 0))
    return pl.pallas_call(
        functools.partial(dispatch_body, local=local, count=len(sources)),
        grid_spec=pltpu.PrefetchScalarGridSpec(
            num_scalar_prefetch=1,
            grid=(blocks,),
            in_specs=[
                pl.BlockSpec((ROW_BLOCK, source.shape[1]), lambda s, o: (s, 0))
                for source in sources
            ]
            + [pl.BlockSpec((MODEL_WIDTH, LANES), lambda s, o: (0, 0))],
            out_specs=[
                slotted_spec,
                slotted_spec,
                pl.BlockSpec((ROW_BLOCK, slots), lambda s, o: (s, 0)),
                pl.BlockSpec((ROW_BLOCK, slots), lambda s, o: (s, 0)),
            ],
        ),
        out_shape=(
            slotted,
            slotted,
            jax.ShapeDtypeStruct((total, slots), bf16),
            jax.ShapeDtypeStruct((total, slots), bf16),
        ),
        compiler_params=row_params,
        cost_estimate=cost(11.0, 40.0),
        name="dispatch",
    )(offset, *sources, router)


def pack_weights(gate_up, down):
    gu_rows = gate_up.shape[1]
    count = MODEL_WIDTH // gu_rows
    cut = FF // count
    side = [down[:, k * cut : (k + 1) * cut, :] for k in range(count)]
    return jnp.concatenate([gate_up, jnp.concatenate(side, axis=2)], axis=1)


def unpack_weights(packed, gu_rows):
    count = MODEL_WIDTH // gu_rows
    side = packed[:, gu_rows:]
    side = [side[:, :, k * gu_rows : (k + 1) * gu_rows] for k in range(count)]
    return packed[:, :gu_rows], jnp.concatenate(side, axis=1)


def experts_body(place_ref, xd_ref, gd_ref, *refs, base, slices, carried):
    paired = slices == 4
    kinds = 5 if paired else 1
    w_refs, refs = refs[:kinds], refs[kinds:]
    old, refs = (refs[:kinds], refs[kinds:]) if carried else ((), refs)
    out_ref, dx_ref, h_ref = refs[:3]
    grad_refs = refs[3 : 3 + kinds]
    wgu_ref, wd_ref, act_sc, dh_sc = refs[3 + kinds :]
    expert = pl.program_id(0)
    gu_rows = MODEL_WIDTH // slices
    cut = FF // slices

    def begin_of(index):
        if not paired:
            return index * gu_rows
        return pl.multiple_of(place_ref[1 + index] * gu_rows, LANES)

    def put(index, ref, *lead):
        begin = begin_of(index)
        wgu_ref[pl.ds(begin, gu_rows), :] = ref[(*lead, slice(0, gu_rows), slice(None))]
        for k in range(slices):
            wd_ref[k * cut : (k + 1) * cut, pl.ds(begin, gu_rows)] = ref[
                (*lead, slice(gu_rows, gu_rows + cut), slice(k * gu_rows, (k + 1) * gu_rows))
            ]

    if paired:
        for index in range(3):
            put(index, w_refs[index], 0)

        @pl.when(expert == 0)
        def _():
            put(3, w_refs[3], 0)

        @pl.when(expert == 1)
        def _():
            put(3, w_refs[4], 0)

    else:
        for index in range(slices):
            put(index, w_refs[0], index, 0)

    total = xd_ref.shape[1]
    chunk = ROW_BLOCK
    own = place_ref[0] + expert + base
    lane = lax.broadcasted_iota(jnp.int32, (chunk, LANES), 1)

    def chunk_step(index):
        rows = block_rows(index)
        hidden = dot(xd_ref[0, rows, :], wgu_ref[...])
        gate = hidden[:, :FF]
        up = hidden[:, FF:]
        sigmoid = jax.nn.sigmoid(gate)
        act = (gate * sigmoid * up).astype(bf16)
        act_sc[rows, :] = act
        out = dot(act, wd_ref[...]).astype(bf16)
        out_ref[0, rows, :] = out
        grad_out = gd_ref[0, rows, :]
        h = jnp.sum(grad_out.astype(f32) * out.astype(f32), axis=-1, keepdims=True)
        h_ref[0, rows, :] = jnp.where(lane == own, h, 0.0).astype(bf16)
        grad_act = dot_nt(grad_out, wd_ref[...])
        grad_gate = grad_act * up * sigmoid * (1.0 + gate * (1.0 - sigmoid))
        grad_up = grad_act * gate * sigmoid
        dh_sc[rows, :FF] = grad_gate.astype(bf16)
        dh_sc[rows, FF:] = grad_up.astype(bf16)
        dx_ref[0, rows, :] = dot_nt(dh_sc[rows, :], wgu_ref[...]).astype(bf16)

    for_blocks(total // chunk, chunk_step)

    def put_grad(kind, lead, gate_up, down):
        ref = grad_refs[kind]
        at = (*lead, slice(0, gu_rows), slice(None))
        if carried:
            gate_up = gate_up + old[kind][at].astype(f32)
        ref[at] = gate_up.astype(bf16)
        for k in range(slices):
            at = (*lead, slice(gu_rows, gu_rows + cut), slice(k * gu_rows, (k + 1) * gu_rows))
            value = down[k * cut : (k + 1) * cut, :]
            if carried:
                value = value + old[kind][at].astype(f32)
            ref[at] = value.astype(bf16)

    targets = (
        ((0, 0), (1, 0), (3, 0), (1, 1)),
        ((0, 1), (4, 0), (2, 0), (2, 1)),
    )
    for index in range(slices):
        begin = begin_of(index)
        gate_up = dot_tn(xd_ref[0, :, pl.ds(begin, gu_rows)], dh_sc[...])
        down = dot_tn(act_sc[...], gd_ref[0, :, pl.ds(begin, gu_rows)])
        if not paired:
            put_grad(0, (index, 0), gate_up, down)
            continue

        @pl.when(expert == 0)
        def _():
            kind, lead = targets[0][index]
            put_grad(kind, (lead,), gate_up, down)

        @pl.when(expert == 1)
        def _():
            kind, lead = targets[1][index]
            put_grad(kind, (lead,), gate_up, down)


def run_experts(place, xd, gd, pieces, old, base, here, slices):
    total = xd.shape[1]
    paired = slices == 4
    packed = (MODEL_WIDTH + FF) // slices

    def spec(rows, width, first=0):
        return pl.BlockSpec((1, rows, width), lambda e, o: (e + first, 0, 0))

    def fixed(count):
        return pl.BlockSpec((count, packed, MODEL_WIDTH), lambda e, o: (0, 0, 0))

    if paired:
        w_specs = [spec(packed, MODEL_WIDTH)] * 3 + [fixed(1)] * 2
        counts = (2, 2, 2, 1, 1)
        grad_specs = [fixed(count) for count in counts]
        grad_shapes = tuple(
            jax.ShapeDtypeStruct((count, packed, MODEL_WIDTH), bf16) for count in counts
        )
    else:
        w_specs = [pl.BlockSpec((slices, 1, packed, MODEL_WIDTH), lambda e, o: (0, e, 0, 0))]
        grad_specs = w_specs
        grad_shapes = (jax.ShapeDtypeStruct((slices, here, packed, MODEL_WIDTH), bf16),)
    results = pl.pallas_call(
        functools.partial(experts_body, base=base, slices=slices, carried=bool(old)),
        grid_spec=pltpu.PrefetchScalarGridSpec(
            num_scalar_prefetch=1,
            grid=(here,),
            in_specs=[spec(total, MODEL_WIDTH, base)] * 2 + w_specs + (grad_specs if old else []),
            out_specs=[spec(total, MODEL_WIDTH)] * 2 + [spec(total, LANES)] + grad_specs,
            scratch_shapes=[
                pltpu.VMEM((MODEL_WIDTH, 2 * FF), bf16),
                pltpu.VMEM((FF, MODEL_WIDTH), bf16),
                pltpu.VMEM((total, FF), bf16),
                pltpu.VMEM((total, 2 * FF), bf16),
            ],
        ),
        out_shape=(
            jax.ShapeDtypeStruct((here, total, MODEL_WIDTH), bf16),
            jax.ShapeDtypeStruct((here, total, MODEL_WIDTH), bf16),
            jax.ShapeDtypeStruct((here, total, LANES), bf16),
        )
        + grad_shapes,
        compiler_params=row_params,
        cost_estimate=cost(20.0, 60.0),
        name="experts",
    )(place, xd, gd, *pieces, *old)
    return results[:3], results[3:]


def whole_slots(refs, slots, width):
    return jnp.concatenate(
        [ref[...].reshape(slots // len(refs), width) for ref in refs], axis=0
    )


def combine_grad_body(*refs, count):
    dx_refs, h_refs, (pt_ref, grad_ref) = refs[:count], refs[count : 2 * count], refs[2 * count :]
    slots = pt_ref.shape[1]
    grad_ref[:, :MODEL_WIDTH] = dot(
        pt_ref[...], whole_slots(dx_refs, slots, MODEL_WIDTH)
    ).astype(bf16)
    grad_ref[:, MODEL_WIDTH:] = dot(pt_ref[...], whole_slots(h_refs, slots, LANES)).astype(bf16)


def combine_mix_body(*refs, count):
    out_refs, (pgt_ref, mix_ref) = refs[:count], refs[count:]
    mix_ref[...] = dot(
        pgt_ref[...], whole_slots(out_refs, pgt_ref.shape[1], MODEL_WIDTH)
    ).astype(bf16)


def combine_both_body(*refs, count):
    out_refs, dx_refs, refs = refs[:count], refs[count : 2 * count], refs[2 * count :]
    h_refs, (pgt_ref, pt_ref, both_ref) = refs[:count], refs[count:]
    slots = pt_ref.shape[1]
    both_ref[:, :MODEL_WIDTH] = dot(
        pgt_ref[...], whole_slots(out_refs, slots, MODEL_WIDTH)
    ).astype(bf16)
    both_ref[:, MODEL_WIDTH : 2 * MODEL_WIDTH] = dot(
        pt_ref[...], whole_slots(dx_refs, slots, MODEL_WIDTH)
    ).astype(bf16)
    both_ref[:, 2 * MODEL_WIDTH :] = dot(
        pt_ref[...], whole_slots(h_refs, slots, LANES)
    ).astype(bf16)


def combine(body, arrays, count, tables, width, name):
    total, slots = tables[0].shape
    blocks = total // ROW_BLOCK
    arrays = [array.reshape(array.shape[0], blocks, CAP, array.shape[-1]) for array in arrays]
    in_specs = [
        pl.BlockSpec((array.shape[0], 1, CAP, array.shape[-1]), lambda s: (0, s, 0, 0))
        for array in arrays
    ]
    return pl.pallas_call(
        functools.partial(body, count=count),
        grid=(blocks,),
        in_specs=in_specs + [pl.BlockSpec((ROW_BLOCK, slots), lambda s: (s, 0))] * len(tables),
        out_specs=pl.BlockSpec((ROW_BLOCK, width), lambda s: (s, 0)),
        out_shape=jax.ShapeDtypeStruct((total, width), bf16),
        compiler_params=row_params,
        cost_estimate=cost(5.0, 17.0),
        name=name,
    )(*arrays, *tables)


def flip(value, bits):
    return lax.ppermute(value, "tp", [(t, t ^ bits) for t in range(4)])


def square():
    return lax.axis_size("tp") == 4


def tp_places():
    me = lax.axis_index("tp").astype(jnp.int32)
    if square():
        return jnp.stack([me ^ bits for bits in range(4)])
    return jnp.zeros((1,), jnp.int32)


def gather_rows(value):
    if square():
        return [value] + [flip(value, bits) for bits in (1, 2, 3)]
    return [lax.all_gather(value, "tp", axis=0, tiled=True)]


def send_rows(parts):
    if square():
        return [parts[0]] + [flip(parts[bits], bits) for bits in (1, 2, 3)]
    return [lax.psum_scatter(parts[0], "tp", scatter_dimension=0, tiled=True)]


def add_rows(came):
    total = came[0].astype(f32)
    for part in came[1:]:
        total = total + part.astype(f32)
    return total


def gather_weights_near(packed):
    if square():
        return [packed, flip(packed, 1), flip(packed, 2)]
    return [lax.all_gather(packed, "tp")]


def gather_weights_far(near):
    if square():
        return [*near, flip(near[2][:1], 1), flip(near[1][1:], 2)]
    return near


def sum_weights_near(grads):
    if square():
        return [flip(grads[1], 1), flip(grads[2], 2), *grads]
    return [lax.psum_scatter(grads[0], "tp", scatter_dimension=0)]


def sum_weights_far(near):
    if square():
        came_x, came_y, own, _, _, kept_y, kept_x = [value.astype(f32) for value in near]
        first = came_x[:1] + own[:1]
        second = came_y[:1] + own[1:]
        far_first = flip((came_x[1:] + kept_y).astype(bf16), 2)
        far_second = flip((came_y[1:] + kept_x).astype(bf16), 1)
        return [first, second, far_first, far_second]
    return near


def add_far(far):
    if square():
        first, second, far_first, far_second = far
        return jnp.concatenate([first + far_first, second + far_second])
    return far[0].astype(f32)


def ag_ep(value, axis=0):
    return lax.all_gather(value, "ep", axis=axis, tiled=True)


def rs_ep(value, axis=0):
    return lax.psum_scatter(value, "ep", scatter_dimension=axis, tiled=True)


def rope_tables(segment_row):
    onehot = (segment_row[:, None] == jnp.arange(DOCS, dtype=jnp.int32)[None, :]).astype(jnp.int32)
    doc_len = jnp.sum(onehot, axis=0)
    starts = [jnp.sum(doc_len[:doc]) for doc in range(DOCS)]
    begin = jnp.zeros_like(segment_row)
    for doc in range(1, DOCS):
        begin = jnp.where(segment_row == doc, starts[doc], begin)
    positions = jnp.arange(segment_row.shape[0], dtype=jnp.int32) - begin
    lane = jnp.arange(LANES, dtype=jnp.int32)
    halves = HEAD_SIZE // 2
    freqs = rope_base ** (-((lane % halves).astype(f32) * 2.0) / HEAD_SIZE)
    angles = positions.astype(f32)[:, None] * freqs[None, :]
    sign = jnp.where((lane % HEAD_SIZE) < halves, -1.0, 1.0).astype(f32)
    return jnp.cos(angles), jnp.sin(angles) * sign[None, :]


def shards(
    tokens,
    cotangent,
    norm_gains,
    query_key_value_weight,
    output_weight,
    w_router,
    w_gate_up,
    w_down,
    segment_ids,
    routes,
):
    micro, rows = tokens.shape[:2]
    local_heads = query_key_value_weight.shape[1]
    local = w_gate_up.shape[0]
    ep_size = lax.axis_size("ep")
    offset = (lax.axis_index("ep") * local).astype(jnp.int32).reshape(1)
    places = tp_places()
    starts = places * ROW_BLOCK
    place = jnp.concatenate([offset, places])
    gain_one = norm_gains[0:1]
    gain_two = norm_gains[1:2]
    router = jnp.pad(w_router, ((0, 0), (0, LANES - EXPERTS)))

    slices = lax.axis_size("tp")
    weights = ag_ep(
        jnp.concatenate(
            [
                query_key_value_weight.reshape(query_key_value_weight.shape[0], -1),
                output_weight.reshape(-1, output_weight.shape[2]).T,
            ],
            axis=1,
        )
    )
    lanes = jnp.arange(LANES, dtype=jnp.int32)
    masks = jnp.any(
        routes.reshape(micro, rows, -1)[..., None] == lanes, axis=2
    ).astype(bf16)
    tables = [rope_tables(segment_ids[m]) for m in range(micro)]
    packed_weights = pack_weights(w_gate_up, w_down)
    here = local // 2
    halves = range(2)
    packed_weights = [packed_weights[h * here : (h + 1) * here] for h in halves]

    token_full = []
    for m in range(micro):
        own = after(tokens[m], token_full[-1], tables) if token_full else tokens[m]
        token_full.append(gather_rows(own))
    weights = after(weights, token_full[0], tables)
    fixed = []
    for m in range(micro):
        fixed.append(
            (
                starts, token_full[m], gain_one, weights, tables[m][0], tables[m][1],
                segment_ids[m][:, None], segment_ids[m][None, :],
            )
        )
    came = []
    kept = []
    hiddens = []
    normed_twos = []
    scales = []
    gate_rows = []
    full = []
    for m in range(micro):
        if m:
            fixed[m] = (after(starts, normed_twos), token_full[m], *fixed[m][2:])
        parts, saved = attention_forward(*fixed[m])
        kept.append(saved)
        if m == 0:
            parts, token_full = lax.optimization_barrier((parts, token_full))
        came.append(send_rows(parts))
        if m == 0:
            near = [gather_weights_near(after(packed_weights[0], came[0]))]
        branch = add_rows(came[m])
        hidden = tokens[m].astype(f32) + residual_scale * branch
        scale_two = lax.rsqrt(jnp.mean(hidden * hidden, axis=-1, keepdims=True) + epsilon)
        normed_two = (hidden * scale_two * gain_two).astype(bf16)
        logits = jnp.where(masks[m] > 0, dot(normed_two, router), masked_score)
        expo = jnp.where(
            masks[m] > 0, jnp.exp(logits - jnp.max(logits, axis=-1, keepdims=True)), 0.0
        )
        gate_rows.append(expo / jnp.sum(expo, axis=-1, keepdims=True))
        hiddens.append(hidden)
        normed_twos.append(normed_two)
        scales.append(scale_two)
        if m == 0:
            gm = jnp.concatenate([cotangent[m], masks[m]], axis=-1)
            gm = ag_ep(after(gm, weights))
            full.append([ag_ep(after(normed_two, gm)), gm])
        else:
            if m == micro - 1:
                normed_two, near[0] = lax.optimization_barrier((normed_two, near[0]))
            full.append([ag_ep(jnp.concatenate([normed_two, cotangent[m], masks[m]], axis=-1))])

    pieces = [gather_weights_far(near[0])]
    near.append(gather_weights_near(after(packed_weights[1], pieces[0])))
    old = [(), ()]
    mixes = []
    grads = []
    ready = ()
    for m in range(micro):
        sources = after(full[m], ready) if m else full[m]
        xd, gd, pt, pgt = dispatch(offset, sources, router, local)
        merged = (local, ep_size * CAP, MODEL_WIDTH)
        xd = xd.reshape(merged)
        gd = gd.reshape(merged)
        done = []
        for h in halves:
            results, old[h] = run_experts(
                place, xd, gd, pieces[h], old[h], h * here, here, slices
            )
            done.append(results)
            if m == 0 and h == 0:
                near[1] = after(near[1], results)
                pieces.append(gather_weights_far(near[1]))
        outs, dxs, hs = zip(*done)
        if m < micro - 1:
            both = combine(
                combine_both_body, [*outs, *dxs, *hs], 2, [pgt, pt], 2 * MODEL_WIDTH + LANES,
                "combine",
            )
            ready = both
            both = rs_ep(both)
            mixes.append(both[:, :MODEL_WIDTH])
            grads.append(both[:, MODEL_WIDTH:])
        else:
            near_first = sum_weights_near(old[0])
            dxs, near_first = lax.optimization_barrier((dxs, near_first))
            near_second = sum_weights_near(old[1])
            grad = combine(
                combine_grad_body, [*dxs, *hs], 2, [pt], MODEL_WIDTH + LANES, "combine_grad"
            )
            grads.append(rs_ep(grad))
    input_grads = []
    acc_router = 0.0
    acc_gain_one = 0.0
    acc_gain_two = 0.0
    acc_weights = 0.0
    parts = ()
    backs = []
    grad_hiddens = []
    for m in range(micro):
        grad = grads[m]
        if m:
            grad, far_first = after((grad, far_first), parts)
        grad = grad.astype(f32)
        h_rows = grad[:, MODEL_WIDTH:]
        grad_logits = (
            h_rows - gate_rows[m] * jnp.sum(h_rows, axis=-1, keepdims=True)
        ).astype(bf16)
        acc_router = acc_router + dot_tn(normed_twos[m], grad_logits)
        grad_normed = grad[:, :MODEL_WIDTH] + dot_nt(grad_logits, router)
        scale = scales[m]
        weighted = grad_normed * gain_two
        inner = jnp.mean(weighted * hiddens[m], axis=-1, keepdims=True)
        grad_hidden = (
            cotangent[m].astype(f32)
            + scale * weighted
            - hiddens[m] * scale * scale * scale * inner
        )
        acc_gain_two = acc_gain_two + jnp.sum(grad_normed * hiddens[m] * scale, axis=0)
        grad_branch = (residual_scale * grad_hidden).astype(bf16)
        if m == 0:
            outs, pgt, grad_branch, near_second = lax.optimization_barrier(
                (outs, pgt, grad_branch, near_second)
            )
            mix = combine(combine_mix_body, outs, 2, [pgt], MODEL_WIDTH, "combine_mix")
            mixes.append(rs_ep(mix))
        grad_branch = gather_rows(grad_branch)
        if m == 0:
            grad_branch = after(grad_branch, mix)
            far_first = sum_weights_far(after(near_first, grad_branch))
        if m == micro - 1:
            far_second = sum_weights_far(after(near_second, grad_branch))
        parts, (gweights, ggain) = attention_backward(*fixed[m], kept[m], grad_branch)
        backs.append(parts)
        grad_hiddens.append(grad_hidden)
        if m == micro - 1:
            parts, gweights, ggain, far_second, mixes = lax.optimization_barrier(
                (parts, gweights, ggain, far_second, mixes)
            )
            backs[-1] = parts
        acc_weights = acc_weights + gweights.astype(f32)
        acc_gain_one = acc_gain_one + ggain[0]
    small = jnp.concatenate(
        [
            acc_router[:, :EXPERTS],
            acc_gain_one[:, None],
            acc_gain_two[:, None],
            jnp.zeros((MODEL_WIDTH, LANES - EXPERTS - 2), f32),
        ],
        axis=-1,
    ).astype(bf16)
    rows = MODEL_WIDTH // lax.axis_size("tp")
    if square():
        small = add_rows(
            send_rows(
                [lax.dynamic_slice_in_dim(small, places[k] * rows, rows) for k in range(4)]
            )
        ).astype(bf16)
    else:
        small = lax.psum_scatter(small, "tp", scatter_dimension=0, tiled=True)
    backs = [send_rows(after(parts, small)) for parts in backs]
    for m in range(micro):
        grad_normed = add_rows(backs[m])
        inputs = tokens[m].astype(f32)
        scale = lax.rsqrt(jnp.mean(inputs * inputs, axis=-1, keepdims=True) + epsilon)
        weighted = grad_normed * gain_one
        inner = jnp.mean(weighted * inputs, axis=-1, keepdims=True)
        input_grads.append(
            grad_hiddens[m] + scale * weighted - inputs * scale * scale * scale * inner
        )
    hiddens, mixes, far_first = after((hiddens, mixes, far_first), parts)
    outputs = [
        (hiddens[m] + residual_scale * mixes[m].astype(f32)).astype(bf16) for m in range(micro)
    ]
    grad_gate_up, grad_down = unpack_weights(
        jnp.concatenate([add_far(far_first), add_far(far_second)]), w_gate_up.shape[1]
    )

    columns = acc_weights.shape[1]
    own_rows = MODEL_WIDTH // ep_size
    small_rows = rows // ep_size
    small = small.reshape(ep_size, small_rows * LANES)
    extra = -(-small.shape[1] // (8 * columns)) * 8
    small = jnp.pad(small, ((0, 0), (0, extra * columns - small.shape[1])))
    packed = jnp.concatenate(
        [
            acc_weights.astype(bf16).reshape(ep_size, own_rows, columns),
            small.reshape(ep_size, extra, columns),
        ],
        axis=1,
    )
    summed = rs_ep(packed.reshape(-1, columns)).astype(f32)
    split = local_heads * GROUP_COLS
    grad_qkv = summed[:own_rows, :split].reshape(own_rows, local_heads, GROUP_COLS)
    grad_out = summed[:own_rows, split:].T.reshape(local_heads, LANES, own_rows)
    small = summed[own_rows:].reshape(-1)[: small_rows * LANES].reshape(small_rows, LANES)
    grad_router = small[:, :EXPERTS]
    grad_gains = small[:, EXPERTS : EXPERTS + 2].T
    return (
        jnp.stack(outputs),
        jnp.stack(input_grads),
        grad_gains,
        grad_qkv,
        grad_out,
        grad_router,
        grad_gate_up,
        grad_down,
    )


def solution(mesh):
    placed = (
        P("ep", "tp", None),
        P("ep", "tp", None),
        P(),
        P("ep", "tp", None),
        P("tp", None, "ep"),
        P(),
        P("ep", "tp", None),
        P("ep", None, "tp"),
        P("ep", None),
        P("ep", "tp", None, None),
    )
    return jax.shard_map(
        shards,
        mesh=mesh,
        in_specs=placed,
        out_specs=(
            P("ep", "tp", None),
            P("ep", "tp", None),
            P(None, ("tp", "ep")),
            P("ep", "tp", None),
            P("tp", None, "ep"),
            P(("tp", "ep"), None),
            P("ep", "tp", None),
            P("ep", None, "tp"),
        ),
        check_vma=False,
    )
```

```python
import functools

import jax
import jax.numpy as jnp
from jax import lax
from jax.experimental import pallas as pl
from jax.experimental.pallas import tpu as pltpu
from jax.sharding import PartitionSpec as P

MODEL_WIDTH = 1024
HEAD_SIZE = 64
FF = 512
EXPERTS = 32
DOCS = 4
CAP = 96
LANES = 128
ROW_BLOCK = 256
GROUP_COLS = 256

epsilon = 1e-06
score_scale = 0.015625
residual_scale = 0.22
rope_base = 10000.0
masked_score = -1000000000.0

f32 = jnp.float32
bf16 = jnp.bfloat16

params = pltpu.CompilerParams(vmem_limit_bytes=58 * 1024 * 1024)
row_params = pltpu.CompilerParams(
    vmem_limit_bytes=58 * 1024 * 1024, dimension_semantics=("arbitrary",)
)


def cost(gflops, megabytes):
    return pl.CostEstimate(
        flops=int(gflops * 1e6), transcendentals=0, bytes_accessed=int(megabytes * 1e3)
    )


def after(value, *others):
    return lax.optimization_barrier((value, others))[0]


def dot(a, b):
    return jnp.dot(a, b, preferred_element_type=f32)


def dot_nt(a, b):
    return lax.dot_general(a, b, (((1,), (1,)), ((), ())), preferred_element_type=f32)


def dot_tn(a, b):
    return lax.dot_general(a, b, (((0,), (0,)), ((), ())), preferred_element_type=f32)


def lane_masks(rows):
    lane = lax.broadcasted_iota(jnp.int32, (rows, LANES), 1)
    return lane < HEAD_SIZE, (lane % HEAD_SIZE) < HEAD_SIZE // 2


def swap_halves(values, first):
    half = HEAD_SIZE // 2
    return jnp.where(first, pltpu.roll(values, LANES - half, 1), pltpu.roll(values, half, 1))


def for_blocks(count, body):
    if count <= 4:
        for index in range(count):
            body(index)
    else:

        def step(index, carry):
            body(index)
            return carry

        lax.fori_loop(0, count, step, 0)


def block_rows(index):
    if isinstance(index, int):
        return pl.ds(index * ROW_BLOCK, ROW_BLOCK)
    return pl.ds(pl.multiple_of(index * ROW_BLOCK, ROW_BLOCK), ROW_BLOCK)


def key_window(index, length):
    reach = -(-(length // 2) // ROW_BLOCK)
    if isinstance(index, int):
        start = max(0, index - reach) * ROW_BLOCK
        return start, (index + 1) * ROW_BLOCK - start
    start = jnp.maximum(index - reach, 0) * ROW_BLOCK
    return pl.multiple_of(start, ROW_BLOCK), (reach + 1) * ROW_BLOCK


def allowed_keys(index, start, width, seg_col_ref, seg_row_ref):
    query = lax.broadcasted_iota(jnp.int32, (ROW_BLOCK, width), 0) + index * ROW_BLOCK
    key = lax.broadcasted_iota(jnp.int32, (ROW_BLOCK, width), 1) + start
    same = seg_row_ref[:, pl.ds(start, width)] == seg_col_ref[block_rows(index), :]
    return (key <= query) & same


def place_rows(starts_ref, pieces, whole):
    for index, piece in enumerate(pieces):
        rows = piece.shape[0]
        begin = pl.multiple_of(starts_ref[index], ROW_BLOCK)
        whole[pl.ds(begin, rows), :] = piece[...]


def each_block(starts_ref, pieces):
    for index, piece in enumerate(pieces):
        for inner in range(0, piece.shape[0], ROW_BLOCK):
            begin = pl.multiple_of(starts_ref[index] + inner, ROW_BLOCK)
            yield pl.ds(begin, ROW_BLOCK), piece, slice(inner, inner + ROW_BLOCK)


def attention_forward_body(starts_ref, *refs, count):
    x_pieces = refs[:count]
    gain_ref, weights_ref, cos_ref, sin_ref, seg_col_ref, seg_row_ref = refs[count : count + 6]
    parts = refs[count + 6 : 2 * count + 6]
    qa_ref, qb_ref, kd_ref, vd_ref, ctx_ref, x_ref = refs[2 * count + 6 :]
    place_rows(starts_ref, x_pieces, x_ref)
    length = x_ref.shape[0]
    groups = weights_ref.shape[1] // (GROUP_COLS + LANES)
    low, first = lane_masks(ROW_BLOCK)

    def project(index):
        rows = block_rows(index)
        x = x_ref[rows, :].astype(f32)
        scale = lax.rsqrt(jnp.mean(x * x, axis=-1, keepdims=True) + epsilon)
        normed = (x * scale * gain_ref[...]).astype(bf16)
        projected = dot(normed, weights_ref[:, : groups * GROUP_COLS])
        cosine = cos_ref[rows, :]
        sine = sin_ref[rows, :]
        for group in range(groups):
            cols = slice(group * LANES, (group + 1) * LANES)
            query = projected[:, group * GROUP_COLS : group * GROUP_COLS + LANES]
            pair = projected[:, group * GROUP_COLS + LANES : (group + 1) * GROUP_COLS]
            query = (query * cosine + swap_halves(query, first) * sine) * score_scale
            qa_ref[rows, cols] = jnp.where(low, query, 0.0).astype(bf16)
            qb_ref[rows, cols] = jnp.where(low, 0.0, query).astype(bf16)
            turned = pair * cosine + swap_halves(pair, first) * sine
            kd_ref[rows, cols] = jnp.where(low, turned, pltpu.roll(turned, HEAD_SIZE, 1)).astype(
                bf16
            )
            vd_ref[rows, cols] = jnp.where(low, pltpu.roll(pair, HEAD_SIZE, 1), pair).astype(bf16)

    def attend(index):
        rows = block_rows(index)
        start, width = key_window(index, length)
        keys = pl.ds(start, width)
        allowed = allowed_keys(index, start, width, seg_col_ref, seg_row_ref)
        for group in range(groups):
            cols = slice(group * LANES, (group + 1) * LANES)
            heads = []
            for q_ref in (qa_ref, qb_ref):
                scores = dot_nt(q_ref[rows, cols], kd_ref[keys, cols])
                scores = jnp.where(allowed, scores, masked_score)
                expo = jnp.exp(scores - jnp.max(scores, axis=-1, keepdims=True))
                total = jnp.sum(expo, axis=-1, keepdims=True)
                probs = (expo * (1.0 / total)).astype(bf16)
                heads.append(dot(probs, vd_ref[keys, cols]))
            ctx_ref[rows, cols] = jnp.where(low, heads[0], heads[1]).astype(bf16)

    for_blocks(length // ROW_BLOCK, project)
    for_blocks(length // ROW_BLOCK, attend)
    for rows, part, inner in each_block(starts_ref, parts):
        part[inner, :] = dot_nt(ctx_ref[rows, :], weights_ref[:, groups * GROUP_COLS :]).astype(
            bf16
        )


def in_vmem(count):
    return [pl.BlockSpec(memory_space=pltpu.SMEM)] + [
        pl.BlockSpec(memory_space=pltpu.VMEM) for _ in range(count)
    ]


def attention_forward(starts, pieces, gain, weights, cosine, sine, seg_col, seg_row):
    length = cosine.shape[0]
    count = len(pieces)
    half = jax.ShapeDtypeStruct((length, weights.shape[1] // 3), bf16)
    results = pl.pallas_call(
        functools.partial(attention_forward_body, count=count),
        out_shape=tuple(jax.ShapeDtypeStruct(p.shape, bf16) for p in pieces) + (half,) * 5,
        in_specs=in_vmem(count + 6),
        scratch_shapes=[pltpu.VMEM((length, MODEL_WIDTH), bf16)],
        compiler_params=params,
        cost_estimate=cost(11.0, 40.0),
        name="attn_fwd",
    )(starts, *pieces, gain, weights, cosine, sine, seg_col, seg_row)
    return results[:count], results[count:]


def attention_backward_body(starts_ref, *refs, count):
    x_pieces, refs = refs[:count], refs[count:]
    gain_ref, weights_ref, cos_ref, sin_ref, seg_col_ref, seg_row_ref = refs[:6]
    qa_ref, qb_ref, kd_ref, vd_ref, ctx_ref = refs[6:11]
    gb_pieces, parts, refs = refs[11 : 11 + count], refs[11 + count : 11 + 2 * count], refs[
        11 + 2 * count :
    ]
    grad_ref, gain_grad_ref, gb_ref, norm_sc, proj_sc, dk_sc, dv_sc = refs
    place_rows(starts_ref, gb_pieces, gb_ref)
    length = gb_ref.shape[0]
    groups = weights_ref.shape[1] // (GROUP_COLS + LANES)
    split = groups * GROUP_COLS
    low, first = lane_masks(ROW_BLOCK)
    dk_sc[...] = jnp.zeros_like(dk_sc)
    dv_sc[...] = jnp.zeros_like(dv_sc)

    def attend(index):
        rows = block_rows(index)
        start, width = key_window(index, length)
        keys = pl.ds(start, width)
        allowed = allowed_keys(index, start, width, seg_col_ref, seg_row_ref)
        grad_context = dot(gb_ref[rows, :], weights_ref[:, split:])
        cosine = cos_ref[rows, :]
        sine = sin_ref[rows, :]
        for group in range(groups):
            cols = slice(group * LANES, (group + 1) * LANES)
            grad_group = grad_context[:, cols]
            grad_queries = []
            for head, q_ref in enumerate((qa_ref, qb_ref)):
                if head == 0:
                    grad_head = jnp.where(low, grad_group, 0.0).astype(bf16)
                else:
                    grad_head = jnp.where(low, 0.0, grad_group).astype(bf16)
                query = q_ref[rows, cols]
                scores = dot_nt(query, kd_ref[keys, cols])
                scores = jnp.where(allowed, scores, masked_score)
                expo = jnp.exp(scores - jnp.max(scores, axis=-1, keepdims=True))
                probs = expo * (1.0 / jnp.sum(expo, axis=-1, keepdims=True))
                grad_probs = dot_nt(grad_head, vd_ref[keys, cols])
                delta = jnp.sum(probs * grad_probs, axis=-1, keepdims=True)
                grad_scores = (probs * (grad_probs - delta)).astype(bf16)
                grad_queries.append(dot(grad_scores, kd_ref[keys, cols]))
                dk_sc[keys, cols] += dot_tn(grad_scores, query)
                dv_sc[keys, cols] += dot_tn(probs.astype(bf16), grad_head)
            grad_query = jnp.where(low, grad_queries[0], grad_queries[1]) * score_scale
            grad_query = grad_query * cosine - swap_halves(grad_query, first) * sine
            proj_sc[rows, group * GROUP_COLS : group * GROUP_COLS + LANES] = grad_query.astype(bf16)

    for_blocks(length // ROW_BLOCK, attend)
    gain_grad_ref[...] = jnp.zeros_like(gain_grad_ref)

    def finish(rows, part, inner, x_piece):
        cosine = cos_ref[rows, :]
        sine = sin_ref[rows, :]
        for group in range(groups):
            cols = slice(group * LANES, (group + 1) * LANES)
            grad_key = dk_sc[rows, cols]
            grad_key = grad_key + pltpu.roll(grad_key, HEAD_SIZE, 1)
            grad_key = grad_key * cosine - swap_halves(grad_key, first) * sine
            grad_value = dv_sc[rows, cols]
            grad_value = grad_value + pltpu.roll(grad_value, HEAD_SIZE, 1)
            proj_sc[rows, group * GROUP_COLS + LANES : (group + 1) * GROUP_COLS] = jnp.where(
                low, grad_key, grad_value
            ).astype(bf16)
        grad_normed = dot_nt(proj_sc[rows, :], weights_ref[:, :split])
        x = x_piece[inner, :].astype(f32)
        unit = x * lax.rsqrt(jnp.mean(x * x, axis=-1, keepdims=True) + epsilon)
        norm_sc[rows, :] = (unit * gain_ref[...]).astype(bf16)
        gain_grad_ref[...] += jnp.sum(grad_normed * unit, axis=0, keepdims=True)
        part[inner, :] = grad_normed.astype(bf16)

    if count > 1:
        for (rows, part, inner), x_piece in zip(each_block(starts_ref, parts), x_pieces):
            finish(rows, part, inner, x_piece)
    else:

        def whole_step(index):
            finish(block_rows(index), parts[0], block_rows(index), x_pieces[0])

        for_blocks(length // ROW_BLOCK, whole_step)
    grad_ref[:, :split] = dot_tn(norm_sc[...], proj_sc[...]).astype(bf16)
    grad_ref[:, split:] = dot_tn(gb_ref[...], ctx_ref[...]).astype(bf16)


def attention_backward(
    starts, pieces, gain, weights, cosine, sine, seg_col, seg_row, kept, grad_pieces
):
    length = cosine.shape[0]
    count = len(pieces)
    heads = weights.shape[1] // 3
    results = pl.pallas_call(
        functools.partial(attention_backward_body, count=count),
        out_shape=tuple(jax.ShapeDtypeStruct(p.shape, bf16) for p in pieces)
        + (
            jax.ShapeDtypeStruct(weights.shape, bf16),
            jax.ShapeDtypeStruct((1, MODEL_WIDTH), f32),
        ),
        in_specs=in_vmem(2 * count + 11),
        scratch_shapes=[
            pltpu.VMEM((length, MODEL_WIDTH), bf16),
            pltpu.VMEM((length, MODEL_WIDTH), bf16),
            pltpu.VMEM((length, 2 * heads), bf16),
            pltpu.VMEM((length, heads), f32),
            pltpu.VMEM((length, heads), f32),
        ],
        compiler_params=params,
        cost_estimate=cost(18.0, 65.0),
        name="attn_bwd",
    )(starts, *pieces, gain, weights, cosine, sine, seg_col, seg_row, *kept, *grad_pieces)
    return results[:count], results[count:]


def dispatch_body(offset_ref, *refs, local, count):
    ins, (router_ref, xd_ref, gd_ref, pt_ref, pgt_ref) = refs[:count], refs[count:]
    rows = ins[0].shape[0]
    slots = local * CAP
    if count == 1:
        x = ins[0][:, :MODEL_WIDTH]
        grad = ins[0][:, MODEL_WIDTH : 2 * MODEL_WIDTH]
        mask = ins[0][:, 2 * MODEL_WIDTH :]
    else:
        x = ins[0][...]
        grad = ins[1][:, :MODEL_WIDTH]
        mask = ins[1][:, MODEL_WIDTH:]
    chosen = mask.astype(f32) > 0.0
    logits = jnp.where(chosen, dot(x, router_ref[...]), masked_score)
    expo = jnp.where(chosen, jnp.exp(logits - jnp.max(logits, axis=-1, keepdims=True)), 0.0)
    gates = (expo / jnp.sum(expo, axis=-1, keepdims=True)).astype(bf16)
    earlier = lax.broadcasted_iota(jnp.int32, (rows, rows), 1) < lax.broadcasted_iota(
        jnp.int32, (rows, rows), 0
    )
    place = dot(jnp.where(earlier, 1.0, 0.0).astype(bf16), mask)
    place = jnp.where(chosen, place, -1.0).astype(bf16)
    offset = offset_ref[0]

    def pick(shape, slot_axis):
        slot = lax.broadcasted_iota(jnp.int32, shape, slot_axis)
        expert = lax.broadcasted_iota(jnp.int32, shape, 1 - slot_axis)
        hit = jnp.zeros(shape, jnp.bool_)
        for own in range(local):
            hit = hit | (
                (slot >= own * CAP) & (slot < (own + 1) * CAP) & (expert == offset + own)
            )
        return jnp.where(hit, 1.0, 0.0).astype(bf16)

    def in_slot(shape, slot_axis):
        slot = lax.broadcasted_iota(jnp.int32, shape, slot_axis)
        for own in range(1, local):
            slot = jnp.where(slot >= CAP, slot - CAP, slot)
        return slot.astype(f32)

    spread = pick((slots, LANES), 0)
    hit = dot_nt(spread, place) == in_slot((slots, rows), 0)
    send = jnp.where(hit, 1.0, 0.0).astype(bf16)
    send_gated = jnp.where(hit, dot_nt(spread, gates), 0.0).astype(bf16)
    xd_ref[...] = dot(send, x).astype(bf16).reshape(xd_ref.shape)
    gd_ref[...] = ((dot(send_gated, grad) * residual_scale).astype(bf16)).reshape(gd_ref.shape)
    spread = pick((LANES, slots), 1)
    hit = dot(place, spread) == in_slot((rows, slots), 1)
    pt_ref[...] = jnp.where(hit, 1.0, 0.0).astype(bf16)
    pgt_ref[...] = jnp.where(hit, dot(gates, spread), 0.0).astype(bf16)


def dispatch(offset, sources, router, local):
    total = sources[0].shape[0]
    blocks = total // ROW_BLOCK
    slots = local * CAP
    slotted = jax.ShapeDtypeStruct((local, blocks, CAP, MODEL_WIDTH), bf16)
    slotted_spec = pl.BlockSpec((local, 1, CAP, MODEL_WIDTH), lambda s, o: (0, s, 0, 0))
    return pl.pallas_call(
        functools.partial(dispatch_body, local=local, count=len(sources)),
        grid_spec=pltpu.PrefetchScalarGridSpec(
            num_scalar_prefetch=1,
            grid=(blocks,),
            in_specs=[
                pl.BlockSpec((ROW_BLOCK, source.shape[1]), lambda s, o: (s, 0))
                for source in sources
            ]
            + [pl.BlockSpec((MODEL_WIDTH, LANES), lambda s, o: (0, 0))],
            out_specs=[
                slotted_spec,
                slotted_spec,
                pl.BlockSpec((ROW_BLOCK, slots), lambda s, o: (s, 0)),
                pl.BlockSpec((ROW_BLOCK, slots), lambda s, o: (s, 0)),
            ],
        ),
        out_shape=(
            slotted,
            slotted,
            jax.ShapeDtypeStruct((total, slots), bf16),
            jax.ShapeDtypeStruct((total, slots), bf16),
        ),
        compiler_params=row_params,
        cost_estimate=cost(11.0, 40.0),
        name="dispatch",
    )(offset, *sources, router)


def pack_weights(gate_up, down):
    gu_rows = gate_up.shape[1]
    count = MODEL_WIDTH // gu_rows
    cut = FF // count
    side = [down[:, k * cut : (k + 1) * cut, :] for k in range(count)]
    return jnp.concatenate([gate_up, jnp.concatenate(side, axis=2)], axis=1)


def unpack_weights(packed, gu_rows):
    count = MODEL_WIDTH // gu_rows
    side = packed[:, gu_rows:]
    side = [side[:, :, k * gu_rows : (k + 1) * gu_rows] for k in range(count)]
    return packed[:, :gu_rows], jnp.concatenate(side, axis=1)


def experts_body(place_ref, xd_ref, gd_ref, *refs, base, slices, carried):
    paired = slices == 4
    kinds = 5 if paired else 1
    w_refs, refs = refs[:kinds], refs[kinds:]
    old, refs = (refs[:kinds], refs[kinds:]) if carried else ((), refs)
    out_ref, dx_ref, h_ref = refs[:3]
    grad_refs = refs[3 : 3 + kinds]
    wgu_ref, wd_ref, act_sc, dh_sc = refs[3 + kinds :]
    expert = pl.program_id(0)
    gu_rows = MODEL_WIDTH // slices
    cut = FF // slices

    def begin_of(index):
        if not paired:
            return index * gu_rows
        return pl.multiple_of(place_ref[1 + index] * gu_rows, LANES)

    def put(index, ref, *lead):
        begin = begin_of(index)
        wgu_ref[pl.ds(begin, gu_rows), :] = ref[(*lead, slice(0, gu_rows), slice(None))]
        for k in range(slices):
            wd_ref[k * cut : (k + 1) * cut, pl.ds(begin, gu_rows)] = ref[
                (*lead, slice(gu_rows, gu_rows + cut), slice(k * gu_rows, (k + 1) * gu_rows))
            ]

    if paired:
        for index in range(3):
            put(index, w_refs[index], 0)

        @pl.when(expert == 0)
        def _():
            put(3, w_refs[3], 0)

        @pl.when(expert == 1)
        def _():
            put(3, w_refs[4], 0)

    else:
        for index in range(slices):
            put(index, w_refs[0], index, 0)

    total = xd_ref.shape[1]
    chunk = ROW_BLOCK
    own = place_ref[0] + expert + base
    lane = lax.broadcasted_iota(jnp.int32, (chunk, LANES), 1)

    def chunk_step(index):
        rows = block_rows(index)
        hidden = dot(xd_ref[0, rows, :], wgu_ref[...])
        gate = hidden[:, :FF]
        up = hidden[:, FF:]
        sigmoid = jax.nn.sigmoid(gate)
        act = (gate * sigmoid * up).astype(bf16)
        act_sc[rows, :] = act
        out = dot(act, wd_ref[...]).astype(bf16)
        out_ref[0, rows, :] = out
        grad_out = gd_ref[0, rows, :]
        h = jnp.sum(grad_out.astype(f32) * out.astype(f32), axis=-1, keepdims=True)
        h_ref[0, rows, :] = jnp.where(lane == own, h, 0.0).astype(bf16)
        grad_act = dot_nt(grad_out, wd_ref[...])
        grad_gate = grad_act * up * sigmoid * (1.0 + gate * (1.0 - sigmoid))
        grad_up = grad_act * gate * sigmoid
        dh_sc[rows, :FF] = grad_gate.astype(bf16)
        dh_sc[rows, FF:] = grad_up.astype(bf16)
        dx_ref[0, rows, :] = dot_nt(dh_sc[rows, :], wgu_ref[...]).astype(bf16)

    for_blocks(total // chunk, chunk_step)

    def put_grad(kind, lead, gate_up, down):
        ref = grad_refs[kind]
        at = (*lead, slice(0, gu_rows), slice(None))
        if carried:
            gate_up = gate_up + old[kind][at].astype(f32)
        ref[at] = gate_up.astype(bf16)
        for k in range(slices):
            at = (*lead, slice(gu_rows, gu_rows + cut), slice(k * gu_rows, (k + 1) * gu_rows))
            value = down[k * cut : (k + 1) * cut, :]
            if carried:
                value = value + old[kind][at].astype(f32)
            ref[at] = value.astype(bf16)

    targets = (
        ((0, 0), (1, 0), (3, 0), (1, 1)),
        ((0, 1), (4, 0), (2, 0), (2, 1)),
    )
    for index in range(slices):
        begin = begin_of(index)
        gate_up = dot_tn(xd_ref[0, :, pl.ds(begin, gu_rows)], dh_sc[...])
        down = dot_tn(act_sc[...], gd_ref[0, :, pl.ds(begin, gu_rows)])
        if not paired:
            put_grad(0, (index, 0), gate_up, down)
            continue

        @pl.when(expert == 0)
        def _():
            kind, lead = targets[0][index]
            put_grad(kind, (lead,), gate_up, down)

        @pl.when(expert == 1)
        def _():
            kind, lead = targets[1][index]
            put_grad(kind, (lead,), gate_up, down)


def run_experts(place, xd, gd, pieces, old, base, here, slices):
    total = xd.shape[1]
    paired = slices == 4
    packed = (MODEL_WIDTH + FF) // slices

    def spec(rows, width, first=0):
        return pl.BlockSpec((1, rows, width), lambda e, o: (e + first, 0, 0))

    def fixed(count):
        return pl.BlockSpec((count, packed, MODEL_WIDTH), lambda e, o: (0, 0, 0))

    if paired:
        w_specs = [spec(packed, MODEL_WIDTH)] * 3 + [fixed(1)] * 2
        counts = (2, 2, 2, 1, 1)
        grad_specs = [fixed(count) for count in counts]
        grad_shapes = tuple(
            jax.ShapeDtypeStruct((count, packed, MODEL_WIDTH), bf16) for count in counts
        )
    else:
        w_specs = [pl.BlockSpec((slices, 1, packed, MODEL_WIDTH), lambda e, o: (0, e, 0, 0))]
        grad_specs = w_specs
        grad_shapes = (jax.ShapeDtypeStruct((slices, here, packed, MODEL_WIDTH), bf16),)
    results = pl.pallas_call(
        functools.partial(experts_body, base=base, slices=slices, carried=bool(old)),
        grid_spec=pltpu.PrefetchScalarGridSpec(
            num_scalar_prefetch=1,
            grid=(here,),
            in_specs=[spec(total, MODEL_WIDTH, base)] * 2 + w_specs + (grad_specs if old else []),
            out_specs=[spec(total, MODEL_WIDTH)] * 2 + [spec(total, LANES)] + grad_specs,
            scratch_shapes=[
                pltpu.VMEM((MODEL_WIDTH, 2 * FF), bf16),
                pltpu.VMEM((FF, MODEL_WIDTH), bf16),
                pltpu.VMEM((total, FF), bf16),
                pltpu.VMEM((total, 2 * FF), bf16),
            ],
        ),
        out_shape=(
            jax.ShapeDtypeStruct((here, total, MODEL_WIDTH), bf16),
            jax.ShapeDtypeStruct((here, total, MODEL_WIDTH), bf16),
            jax.ShapeDtypeStruct((here, total, LANES), bf16),
        )
        + grad_shapes,
        compiler_params=row_params,
        cost_estimate=cost(20.0, 60.0),
        name="experts",
    )(place, xd, gd, *pieces, *old)
    return results[:3], results[3:]


def whole_slots(refs, slots, width):
    return jnp.concatenate(
        [ref[...].reshape(slots // len(refs), width) for ref in refs], axis=0
    )


def combine_grad_body(*refs, count):
    dx_refs, h_refs, (pt_ref, grad_ref) = refs[:count], refs[count : 2 * count], refs[2 * count :]
    slots = pt_ref.shape[1]
    grad_ref[:, :MODEL_WIDTH] = dot(
        pt_ref[...], whole_slots(dx_refs, slots, MODEL_WIDTH)
    ).astype(bf16)
    grad_ref[:, MODEL_WIDTH:] = dot(pt_ref[...], whole_slots(h_refs, slots, LANES)).astype(bf16)


def combine_mix_body(*refs, count):
    out_refs, (pgt_ref, mix_ref) = refs[:count], refs[count:]
    mix_ref[...] = dot(
        pgt_ref[...], whole_slots(out_refs, pgt_ref.shape[1], MODEL_WIDTH)
    ).astype(bf16)


def combine_both_body(*refs, count):
    out_refs, dx_refs, refs = refs[:count], refs[count : 2 * count], refs[2 * count :]
    h_refs, (pgt_ref, pt_ref, both_ref) = refs[:count], refs[count:]
    slots = pt_ref.shape[1]
    both_ref[:, :MODEL_WIDTH] = dot(
        pgt_ref[...], whole_slots(out_refs, slots, MODEL_WIDTH)
    ).astype(bf16)
    both_ref[:, MODEL_WIDTH : 2 * MODEL_WIDTH] = dot(
        pt_ref[...], whole_slots(dx_refs, slots, MODEL_WIDTH)
    ).astype(bf16)
    both_ref[:, 2 * MODEL_WIDTH :] = dot(
        pt_ref[...], whole_slots(h_refs, slots, LANES)
    ).astype(bf16)


def combine(body, arrays, count, tables, width, name):
    total, slots = tables[0].shape
    blocks = total // ROW_BLOCK
    arrays = [array.reshape(array.shape[0], blocks, CAP, array.shape[-1]) for array in arrays]
    in_specs = [
        pl.BlockSpec((array.shape[0], 1, CAP, array.shape[-1]), lambda s: (0, s, 0, 0))
        for array in arrays
    ]
    return pl.pallas_call(
        functools.partial(body, count=count),
        grid=(blocks,),
        in_specs=in_specs + [pl.BlockSpec((ROW_BLOCK, slots), lambda s: (s, 0))] * len(tables),
        out_specs=pl.BlockSpec((ROW_BLOCK, width), lambda s: (s, 0)),
        out_shape=jax.ShapeDtypeStruct((total, width), bf16),
        compiler_params=row_params,
        cost_estimate=cost(5.0, 17.0),
        name=name,
    )(*arrays, *tables)


def flip(value, bits):
    return lax.ppermute(value, "tp", [(t, t ^ bits) for t in range(4)])


def square():
    return lax.axis_size("tp") == 4


def tp_places():
    me = lax.axis_index("tp").astype(jnp.int32)
    if square():
        return jnp.stack([me ^ bits for bits in range(4)])
    return jnp.zeros((1,), jnp.int32)


def gather_rows(value):
    if square():
        return [value] + [flip(value, bits) for bits in (1, 2, 3)]
    return [lax.all_gather(value, "tp", axis=0, tiled=True)]


def send_rows(parts):
    if square():
        return [parts[0]] + [flip(parts[bits], bits) for bits in (1, 2, 3)]
    return [lax.psum_scatter(parts[0], "tp", scatter_dimension=0, tiled=True)]


def add_rows(came):
    total = came[0].astype(f32)
    for part in came[1:]:
        total = total + part.astype(f32)
    return total


def gather_weights_near(packed):
    if square():
        return [packed, flip(packed, 1), flip(packed, 2)]
    return [lax.all_gather(packed, "tp")]


def gather_weights_far(near):
    if square():
        return [*near, flip(near[2][:1], 1), flip(near[1][1:], 2)]
    return near


def sum_weights_near(grads):
    if square():
        return [flip(grads[1], 1), flip(grads[2], 2), *grads]
    return [lax.psum_scatter(grads[0], "tp", scatter_dimension=0)]


def far_sums(near):
    if square():
        came_x, came_y, _, _, _, kept_y, kept_x = near
        first = came_x[1:].astype(f32) + kept_y.astype(f32)
        second = came_y[1:].astype(f32) + kept_x.astype(f32)
        return [first.astype(bf16), second.astype(bf16)]
    return []


def send_far(sums):
    if square():
        return [flip(sums[0], 2), flip(sums[1], 1)]
    return []


def add_far(near, far):
    if square():
        came_x, came_y, own = [value.astype(f32) for value in near[:3]]
        return jnp.concatenate(
            [
                came_x[:1] + own[:1] + far[0].astype(f32),
                came_y[:1] + own[1:] + far[1].astype(f32),
            ]
        )
    return near[0].astype(f32)


def ag_ep(value, axis=0):
    return lax.all_gather(value, "ep", axis=axis, tiled=True)


def rs_ep(value, axis=0):
    return lax.psum_scatter(value, "ep", scatter_dimension=axis, tiled=True)


def rope_tables(segment_row):
    onehot = (segment_row[:, None] == jnp.arange(DOCS, dtype=jnp.int32)[None, :]).astype(jnp.int32)
    doc_len = jnp.sum(onehot, axis=0)
    starts = [jnp.sum(doc_len[:doc]) for doc in range(DOCS)]
    begin = jnp.zeros_like(segment_row)
    for doc in range(1, DOCS):
        begin = jnp.where(segment_row == doc, starts[doc], begin)
    positions = jnp.arange(segment_row.shape[0], dtype=jnp.int32) - begin
    lane = jnp.arange(LANES, dtype=jnp.int32)
    halves = HEAD_SIZE // 2
    freqs = rope_base ** (-((lane % halves).astype(f32) * 2.0) / HEAD_SIZE)
    angles = positions.astype(f32)[:, None] * freqs[None, :]
    sign = jnp.where((lane % HEAD_SIZE) < halves, -1.0, 1.0).astype(f32)
    return jnp.cos(angles), jnp.sin(angles) * sign[None, :]


def shards(
    tokens,
    cotangent,
    norm_gains,
    query_key_value_weight,
    output_weight,
    w_router,
    w_gate_up,
    w_down,
    segment_ids,
    routes,
):
    micro, rows = tokens.shape[:2]
    local_heads = query_key_value_weight.shape[1]
    local = w_gate_up.shape[0]
    ep_size = lax.axis_size("ep")
    offset = (lax.axis_index("ep") * local).astype(jnp.int32).reshape(1)
    places = tp_places()
    starts = places * ROW_BLOCK
    place = jnp.concatenate([offset, places])
    gain_one = norm_gains[0:1]
    gain_two = norm_gains[1:2]
    router = jnp.pad(w_router, ((0, 0), (0, LANES - EXPERTS)))

    slices = lax.axis_size("tp")
    weights = ag_ep(
        jnp.concatenate(
            [
                query_key_value_weight.reshape(query_key_value_weight.shape[0], -1),
                output_weight.reshape(-1, output_weight.shape[2]).T,
            ],
            axis=1,
        )
    )
    lanes = jnp.arange(LANES, dtype=jnp.int32)
    masks = jnp.any(
        routes.reshape(micro, rows, -1)[..., None] == lanes, axis=2
    ).astype(bf16)
    tables = [rope_tables(segment_ids[m]) for m in range(micro)]
    packed_weights = pack_weights(w_gate_up, w_down)
    here = local // 2
    halves = range(2)
    packed_weights = [packed_weights[h * here : (h + 1) * here] for h in halves]

    token_full = []
    for m in range(micro):
        own = after(tokens[m], token_full[-1], tables) if token_full else tokens[m]
        token_full.append(gather_rows(own))
    weights = after(weights, token_full[0], tables)
    fixed = []
    for m in range(micro):
        fixed.append(
            (
                starts, token_full[m], gain_one, weights, tables[m][0], tables[m][1],
                segment_ids[m][:, None], segment_ids[m][None, :],
            )
        )
    came = []
    kept = []
    for m in range(micro):
        if m:
            fixed[m] = (after(starts, parts), token_full[m], *fixed[m][2:])
        parts, saved = attention_forward(*fixed[m])
        kept.append(saved)
        if m == 0:
            parts, token_full = lax.optimization_barrier((parts, token_full))
        if m == micro - 1:
            came[0] = after(came[0], parts)
        came.append(send_rows(parts))

    hiddens = []
    normed_twos = []
    scales = []
    gate_rows = []
    full = []
    for m in range(micro):
        if m == 0:
            near = [gather_weights_near(after(packed_weights[0], came[0]))]
        branch = add_rows(came[m])
        hidden = tokens[m].astype(f32) + residual_scale * branch
        scale_two = lax.rsqrt(jnp.mean(hidden * hidden, axis=-1, keepdims=True) + epsilon)
        normed_two = (hidden * scale_two * gain_two).astype(bf16)
        logits = jnp.where(masks[m] > 0, dot(normed_two, router), masked_score)
        expo = jnp.where(
            masks[m] > 0, jnp.exp(logits - jnp.max(logits, axis=-1, keepdims=True)), 0.0
        )
        gate_rows.append(expo / jnp.sum(expo, axis=-1, keepdims=True))
        hiddens.append(hidden)
        normed_twos.append(normed_two)
        scales.append(scale_two)
        if m == 0:
            gm = jnp.concatenate([cotangent[m], masks[m]], axis=-1)
            gm = ag_ep(after(gm, weights))
            full.append([ag_ep(after(normed_two, gm)), gm])
        else:
            if m == micro - 1:
                normed_two, near[0] = lax.optimization_barrier((normed_two, near[0]))
            full.append([ag_ep(jnp.concatenate([normed_two, cotangent[m], masks[m]], axis=-1))])

    pieces = [gather_weights_far(near[0])]
    near.append(gather_weights_near(after(packed_weights[1], near[0])))
    old = [(), ()]
    mixes = []
    grads = []
    ready = ()
    for m in range(micro):
        sources = after(full[m], ready) if m else full[m]
        xd, gd, pt, pgt = dispatch(offset, sources, router, local)
        merged = (local, ep_size * CAP, MODEL_WIDTH)
        xd = xd.reshape(merged)
        gd = gd.reshape(merged)
        done = []
        for h in halves:
            results, old[h] = run_experts(
                place, xd, gd, pieces[h], old[h], h * here, here, slices
            )
            done.append(results)
            if m == 0 and h == 0:
                near[1] = after(near[1], results)
                pieces.append(gather_weights_far(near[1]))
        outs, dxs, hs = zip(*done)
        if m < micro - 1:
            both = combine(
                combine_both_body, [*outs, *dxs, *hs], 2, [pgt, pt], 2 * MODEL_WIDTH + LANES,
                "combine",
            )
            ready = both
            both = rs_ep(both)
            mixes.append(both[:, :MODEL_WIDTH])
            grads.append(both[:, MODEL_WIDTH:])
        else:
            near_first = sum_weights_near(old[0])
            dxs, near_first = lax.optimization_barrier((dxs, near_first))
            grad = combine(
                combine_grad_body, [*dxs, *hs], 2, [pt], MODEL_WIDTH + LANES, "combine_grad"
            )
            grads.append(rs_ep(grad))
            outs, pgt = after((outs, pgt), grad)
            mix = combine(combine_mix_body, outs, 2, [pgt], MODEL_WIDTH, "combine_mix")
            mixes.append(rs_ep(mix))
            grads[0] = after(grads[0], mix)
    input_grads = []
    acc_router = 0.0
    acc_gain_one = 0.0
    acc_gain_two = 0.0
    acc_weights = 0.0
    parts = ()
    backs = []
    grad_hiddens = []
    for m in range(micro):
        grad = grads[m]
        if m:
            grad, near_second = after((grad, near_second), parts)
        grad = grad.astype(f32)
        h_rows = grad[:, MODEL_WIDTH:]
        grad_logits = (
            h_rows - gate_rows[m] * jnp.sum(h_rows, axis=-1, keepdims=True)
        ).astype(bf16)
        acc_router = acc_router + dot_tn(normed_twos[m], grad_logits)
        grad_normed = grad[:, :MODEL_WIDTH] + dot_nt(grad_logits, router)
        scale = scales[m]
        weighted = grad_normed * gain_two
        inner = jnp.mean(weighted * hiddens[m], axis=-1, keepdims=True)
        grad_hidden = (
            cotangent[m].astype(f32)
            + scale * weighted
            - hiddens[m] * scale * scale * scale * inner
        )
        acc_gain_two = acc_gain_two + jnp.sum(grad_normed * hiddens[m] * scale, axis=0)
        grad_branch = (residual_scale * grad_hidden).astype(bf16)
        grad_branch = gather_rows(grad_branch)
        if m == 0:
            near_second = sum_weights_near(after(old[1], grad_branch))
        if m == micro - 1:
            far_first = send_far(after(far_sums(near_first), grad_branch))
            far_second = send_far(after(far_sums(near_second), grad_branch))
        parts, (gweights, ggain) = attention_backward(*fixed[m], kept[m], grad_branch)
        backs.append(parts)
        grad_hiddens.append(grad_hidden)
        if m == micro - 1:
            parts, gweights, ggain, far_first, mixes = lax.optimization_barrier(
                (parts, gweights, ggain, far_first, mixes)
            )
            backs[-1] = parts
        acc_weights = acc_weights + gweights.astype(f32)
        acc_gain_one = acc_gain_one + ggain[0]
    small = jnp.concatenate(
        [
            acc_router[:, :EXPERTS],
            acc_gain_one[:, None],
            acc_gain_two[:, None],
            jnp.zeros((MODEL_WIDTH, LANES - EXPERTS - 2), f32),
        ],
        axis=-1,
    ).astype(bf16)
    rows = MODEL_WIDTH // lax.axis_size("tp")
    if square():
        small = add_rows(
            send_rows(
                [lax.dynamic_slice_in_dim(small, places[k] * rows, rows) for k in range(4)]
            )
        ).astype(bf16)
    else:
        small = lax.psum_scatter(small, "tp", scatter_dimension=0, tiled=True)
    columns = acc_weights.shape[1]
    own_rows = MODEL_WIDTH // ep_size
    small_rows = rows // ep_size
    small = small.reshape(ep_size, small_rows * LANES)
    extra = -(-small.shape[1] // (8 * columns)) * 8
    small = jnp.pad(small, ((0, 0), (0, extra * columns - small.shape[1])))
    packed = jnp.concatenate(
        [
            acc_weights.astype(bf16).reshape(ep_size, own_rows, columns),
            small.reshape(ep_size, extra, columns),
        ],
        axis=1,
    )
    packed = packed.reshape(-1, columns)
    summed = rs_ep(packed).astype(f32)
    hiddens, mixes, far_first, far_second = after((hiddens, mixes, far_first, far_second), packed)
    backs = [send_rows(after(parts, packed)) for parts in backs]
    for m in range(micro):
        grad_normed = add_rows(backs[m])
        inputs = tokens[m].astype(f32)
        scale = lax.rsqrt(jnp.mean(inputs * inputs, axis=-1, keepdims=True) + epsilon)
        weighted = grad_normed * gain_one
        inner = jnp.mean(weighted * inputs, axis=-1, keepdims=True)
        input_grads.append(
            grad_hiddens[m] + scale * weighted - inputs * scale * scale * scale * inner
        )
    outputs = [
        (hiddens[m] + residual_scale * mixes[m].astype(f32)).astype(bf16) for m in range(micro)
    ]
    grad_gate_up, grad_down = unpack_weights(
        jnp.concatenate([add_far(near_first, far_first), add_far(near_second, far_second)]), w_gate_up.shape[1]
    )
    split = local_heads * GROUP_COLS
    grad_qkv = summed[:own_rows, :split].reshape(own_rows, local_heads, GROUP_COLS)
    grad_out = summed[:own_rows, split:].T.reshape(local_heads, LANES, own_rows)
    small = summed[own_rows:].reshape(-1)[: small_rows * LANES].reshape(small_rows, LANES)
    grad_router = small[:, :EXPERTS]
    grad_gains = small[:, EXPERTS : EXPERTS + 2].T
    return (
        jnp.stack(outputs),
        jnp.stack(input_grads),
        grad_gains,
        grad_qkv,
        grad_out,
        grad_router,
        grad_gate_up,
        grad_down,
    )


def solution(mesh):
    placed = (
        P("ep", "tp", None),
        P("ep", "tp", None),
        P(),
        P("ep", "tp", None),
        P("tp", None, "ep"),
        P(),
        P("ep", "tp", None),
        P("ep", None, "tp"),
        P("ep", None),
        P("ep", "tp", None, None),
    )
    return jax.shard_map(
        shards,
        mesh=mesh,
        in_specs=placed,
        out_specs=(
            P("ep", "tp", None),
            P("ep", "tp", None),
            P(None, ("tp", "ep")),
            P("ep", "tp", None),
            P("tp", None, "ep"),
            P(("tp", "ep"), None),
            P("ep", "tp", None),
            P("ep", None, "tp"),
        ),
        check_vma=False,
    )
```

```python
import functools

import jax
import jax.numpy as jnp
from jax import lax
from jax.experimental import pallas as pl
from jax.experimental.pallas import tpu as pltpu
from jax.sharding import PartitionSpec as P

MODEL_WIDTH = 1024
HEAD_SIZE = 64
FF = 512
EXPERTS = 32
DOCS = 4
CAP = 96
LANES = 128
ROW_BLOCK = 256
GROUP_COLS = 256

epsilon = 1e-06
score_scale = 0.015625
residual_scale = 0.22
rope_base = 10000.0
masked_score = -1000000000.0

f32 = jnp.float32
bf16 = jnp.bfloat16

params = pltpu.CompilerParams(vmem_limit_bytes=58 * 1024 * 1024)
row_params = pltpu.CompilerParams(
    vmem_limit_bytes=58 * 1024 * 1024, dimension_semantics=("arbitrary",)
)


def cost(gflops, megabytes):
    return pl.CostEstimate(
        flops=int(gflops * 1e6), transcendentals=0, bytes_accessed=int(megabytes * 1e3)
    )


def after(value, *others):
    return lax.optimization_barrier((value, others))[0]


def dot(a, b):
    return jnp.dot(a, b, preferred_element_type=f32)


def dot_nt(a, b):
    return lax.dot_general(a, b, (((1,), (1,)), ((), ())), preferred_element_type=f32)


def dot_tn(a, b):
    return lax.dot_general(a, b, (((0,), (0,)), ((), ())), preferred_element_type=f32)


def lane_masks(rows):
    lane = lax.broadcasted_iota(jnp.int32, (rows, LANES), 1)
    return lane < HEAD_SIZE, (lane % HEAD_SIZE) < HEAD_SIZE // 2


def swap_halves(values, first):
    half = HEAD_SIZE // 2
    return jnp.where(first, pltpu.roll(values, LANES - half, 1), pltpu.roll(values, half, 1))


def for_blocks(count, body):
    if count <= 4:
        for index in range(count):
            body(index)
    else:

        def step(index, carry):
            body(index)
            return carry

        lax.fori_loop(0, count, step, 0)


def block_rows(index):
    if isinstance(index, int):
        return pl.ds(index * ROW_BLOCK, ROW_BLOCK)
    return pl.ds(pl.multiple_of(index * ROW_BLOCK, ROW_BLOCK), ROW_BLOCK)


def key_window(index, length):
    reach = -(-(length // 2) // ROW_BLOCK)
    if isinstance(index, int):
        start = max(0, index - reach) * ROW_BLOCK
        return start, (index + 1) * ROW_BLOCK - start
    start = jnp.maximum(index - reach, 0) * ROW_BLOCK
    return pl.multiple_of(start, ROW_BLOCK), (reach + 1) * ROW_BLOCK


def allowed_keys(index, start, width, seg_col_ref, seg_row_ref):
    query = lax.broadcasted_iota(jnp.int32, (ROW_BLOCK, width), 0) + index * ROW_BLOCK
    key = lax.broadcasted_iota(jnp.int32, (ROW_BLOCK, width), 1) + start
    same = seg_row_ref[:, pl.ds(start, width)] == seg_col_ref[block_rows(index), :]
    return (key <= query) & same


def place_rows(starts_ref, pieces, whole):
    for index, piece in enumerate(pieces):
        rows = piece.shape[0]
        begin = pl.multiple_of(starts_ref[index], ROW_BLOCK)
        whole[pl.ds(begin, rows), :] = piece[...]


def each_block(starts_ref, pieces):
    for index, piece in enumerate(pieces):
        for inner in range(0, piece.shape[0], ROW_BLOCK):
            begin = pl.multiple_of(starts_ref[index] + inner, ROW_BLOCK)
            yield pl.ds(begin, ROW_BLOCK), piece, slice(inner, inner + ROW_BLOCK)


def attention_forward_body(starts_ref, *refs, count):
    x_pieces = refs[:count]
    gain_ref, weights_ref, cos_ref, sin_ref, seg_col_ref, seg_row_ref = refs[count : count + 6]
    parts = refs[count + 6 : 2 * count + 6]
    qa_ref, qb_ref, kd_ref, vd_ref, ctx_ref, x_ref = refs[2 * count + 6 :]
    place_rows(starts_ref, x_pieces, x_ref)
    length = x_ref.shape[0]
    groups = weights_ref.shape[1] // (GROUP_COLS + LANES)
    low, first = lane_masks(ROW_BLOCK)

    def project(index):
        rows = block_rows(index)
        x = x_ref[rows, :].astype(f32)
        scale = lax.rsqrt(jnp.mean(x * x, axis=-1, keepdims=True) + epsilon)
        normed = (x * scale * gain_ref[...]).astype(bf16)
        projected = dot(normed, weights_ref[:, : groups * GROUP_COLS])
        cosine = cos_ref[rows, :]
        sine = sin_ref[rows, :]
        for group in range(groups):
            cols = slice(group * LANES, (group + 1) * LANES)
            query = projected[:, group * GROUP_COLS : group * GROUP_COLS + LANES]
            pair = projected[:, group * GROUP_COLS + LANES : (group + 1) * GROUP_COLS]
            query = (query * cosine + swap_halves(query, first) * sine) * score_scale
            qa_ref[rows, cols] = jnp.where(low, query, 0.0).astype(bf16)
            qb_ref[rows, cols] = jnp.where(low, 0.0, query).astype(bf16)
            turned = pair * cosine + swap_halves(pair, first) * sine
            kd_ref[rows, cols] = jnp.where(low, turned, pltpu.roll(turned, HEAD_SIZE, 1)).astype(
                bf16
            )
            vd_ref[rows, cols] = jnp.where(low, pltpu.roll(pair, HEAD_SIZE, 1), pair).astype(bf16)

    def attend(index):
        rows = block_rows(index)
        start, width = key_window(index, length)
        keys = pl.ds(start, width)
        allowed = allowed_keys(index, start, width, seg_col_ref, seg_row_ref)
        for group in range(groups):
            cols = slice(group * LANES, (group + 1) * LANES)
            heads = []
            for q_ref in (qa_ref, qb_ref):
                scores = dot_nt(q_ref[rows, cols], kd_ref[keys, cols])
                scores = jnp.where(allowed, scores, masked_score)
                expo = jnp.exp(scores - jnp.max(scores, axis=-1, keepdims=True))
                total = jnp.sum(expo, axis=-1, keepdims=True)
                probs = (expo * (1.0 / total)).astype(bf16)
                heads.append(dot(probs, vd_ref[keys, cols]))
            ctx_ref[rows, cols] = jnp.where(low, heads[0], heads[1]).astype(bf16)

    for_blocks(length // ROW_BLOCK, project)
    for_blocks(length // ROW_BLOCK, attend)
    for rows, part, inner in each_block(starts_ref, parts):
        part[inner, :] = dot_nt(ctx_ref[rows, :], weights_ref[:, groups * GROUP_COLS :]).astype(
            bf16
        )


def in_vmem(count):
    return [pl.BlockSpec(memory_space=pltpu.SMEM)] + [
        pl.BlockSpec(memory_space=pltpu.VMEM) for _ in range(count)
    ]


def attention_forward(starts, pieces, gain, weights, cosine, sine, seg_col, seg_row):
    length = cosine.shape[0]
    count = len(pieces)
    half = jax.ShapeDtypeStruct((length, weights.shape[1] // 3), bf16)
    results = pl.pallas_call(
        functools.partial(attention_forward_body, count=count),
        out_shape=tuple(jax.ShapeDtypeStruct(p.shape, bf16) for p in pieces) + (half,) * 5,
        in_specs=in_vmem(count + 6),
        scratch_shapes=[pltpu.VMEM((length, MODEL_WIDTH), bf16)],
        compiler_params=params,
        cost_estimate=cost(11.0, 40.0),
        name="attn_fwd",
    )(starts, *pieces, gain, weights, cosine, sine, seg_col, seg_row)
    return results[:count], results[count:]


def attention_backward_body(starts_ref, *refs, count):
    x_pieces, refs = refs[:count], refs[count:]
    gain_ref, weights_ref, cos_ref, sin_ref, seg_col_ref, seg_row_ref = refs[:6]
    qa_ref, qb_ref, kd_ref, vd_ref, ctx_ref = refs[6:11]
    gb_pieces, parts, refs = refs[11 : 11 + count], refs[11 + count : 11 + 2 * count], refs[
        11 + 2 * count :
    ]
    grad_ref, gain_grad_ref, gb_ref, norm_sc, proj_sc, dk_sc, dv_sc = refs
    place_rows(starts_ref, gb_pieces, gb_ref)
    length = gb_ref.shape[0]
    groups = weights_ref.shape[1] // (GROUP_COLS + LANES)
    split = groups * GROUP_COLS
    low, first = lane_masks(ROW_BLOCK)
    dk_sc[...] = jnp.zeros_like(dk_sc)
    dv_sc[...] = jnp.zeros_like(dv_sc)

    def attend(index):
        rows = block_rows(index)
        start, width = key_window(index, length)
        keys = pl.ds(start, width)
        allowed = allowed_keys(index, start, width, seg_col_ref, seg_row_ref)
        grad_context = dot(gb_ref[rows, :], weights_ref[:, split:])
        cosine = cos_ref[rows, :]
        sine = sin_ref[rows, :]
        for group in range(groups):
            cols = slice(group * LANES, (group + 1) * LANES)
            grad_group = grad_context[:, cols]
            grad_queries = []
            for head, q_ref in enumerate((qa_ref, qb_ref)):
                if head == 0:
                    grad_head = jnp.where(low, grad_group, 0.0).astype(bf16)
                else:
                    grad_head = jnp.where(low, 0.0, grad_group).astype(bf16)
                query = q_ref[rows, cols]
                scores = dot_nt(query, kd_ref[keys, cols])
                scores = jnp.where(allowed, scores, masked_score)
                expo = jnp.exp(scores - jnp.max(scores, axis=-1, keepdims=True))
                probs = expo * (1.0 / jnp.sum(expo, axis=-1, keepdims=True))
                grad_probs = dot_nt(grad_head, vd_ref[keys, cols])
                delta = jnp.sum(probs * grad_probs, axis=-1, keepdims=True)
                grad_scores = (probs * (grad_probs - delta)).astype(bf16)
                grad_queries.append(dot(grad_scores, kd_ref[keys, cols]))
                dk_sc[keys, cols] += dot_tn(grad_scores, query)
                dv_sc[keys, cols] += dot_tn(probs.astype(bf16), grad_head)
            grad_query = jnp.where(low, grad_queries[0], grad_queries[1]) * score_scale
            grad_query = grad_query * cosine - swap_halves(grad_query, first) * sine
            proj_sc[rows, group * GROUP_COLS : group * GROUP_COLS + LANES] = grad_query.astype(bf16)

    for_blocks(length // ROW_BLOCK, attend)
    gain_grad_ref[...] = jnp.zeros_like(gain_grad_ref)

    def finish(rows, part, inner, x_piece):
        cosine = cos_ref[rows, :]
        sine = sin_ref[rows, :]
        for group in range(groups):
            cols = slice(group * LANES, (group + 1) * LANES)
            grad_key = dk_sc[rows, cols]
            grad_key = grad_key + pltpu.roll(grad_key, HEAD_SIZE, 1)
            grad_key = grad_key * cosine - swap_halves(grad_key, first) * sine
            grad_value = dv_sc[rows, cols]
            grad_value = grad_value + pltpu.roll(grad_value, HEAD_SIZE, 1)
            proj_sc[rows, group * GROUP_COLS + LANES : (group + 1) * GROUP_COLS] = jnp.where(
                low, grad_key, grad_value
            ).astype(bf16)
        grad_normed = dot_nt(proj_sc[rows, :], weights_ref[:, :split])
        x = x_piece[inner, :].astype(f32)
        unit = x * lax.rsqrt(jnp.mean(x * x, axis=-1, keepdims=True) + epsilon)
        norm_sc[rows, :] = (unit * gain_ref[...]).astype(bf16)
        gain_grad_ref[...] += jnp.sum(grad_normed * unit, axis=0, keepdims=True)
        part[inner, :] = grad_normed.astype(bf16)

    if count > 1:
        for (rows, part, inner), x_piece in zip(each_block(starts_ref, parts), x_pieces):
            finish(rows, part, inner, x_piece)
    else:

        def whole_step(index):
            finish(block_rows(index), parts[0], block_rows(index), x_pieces[0])

        for_blocks(length // ROW_BLOCK, whole_step)
    grad_ref[:, :split] = dot_tn(norm_sc[...], proj_sc[...]).astype(bf16)
    grad_ref[:, split:] = dot_tn(gb_ref[...], ctx_ref[...]).astype(bf16)


def attention_backward(
    starts, pieces, gain, weights, cosine, sine, seg_col, seg_row, kept, grad_pieces
):
    length = cosine.shape[0]
    count = len(pieces)
    heads = weights.shape[1] // 3
    results = pl.pallas_call(
        functools.partial(attention_backward_body, count=count),
        out_shape=tuple(jax.ShapeDtypeStruct(p.shape, bf16) for p in pieces)
        + (
            jax.ShapeDtypeStruct(weights.shape, bf16),
            jax.ShapeDtypeStruct((1, MODEL_WIDTH), f32),
        ),
        in_specs=in_vmem(2 * count + 11),
        scratch_shapes=[
            pltpu.VMEM((length, MODEL_WIDTH), bf16),
            pltpu.VMEM((length, MODEL_WIDTH), bf16),
            pltpu.VMEM((length, 2 * heads), bf16),
            pltpu.VMEM((length, heads), f32),
            pltpu.VMEM((length, heads), f32),
        ],
        compiler_params=params,
        cost_estimate=cost(18.0, 65.0),
        name="attn_bwd",
    )(starts, *pieces, gain, weights, cosine, sine, seg_col, seg_row, *kept, *grad_pieces)
    return results[:count], results[count:]


def dispatch_body(offset_ref, *refs, local, count):
    ins, (router_ref, xd_ref, gd_ref, pt_ref, pgt_ref) = refs[:count], refs[count:]
    rows = ins[0].shape[0]
    slots = local * CAP
    if count == 1:
        x = ins[0][:, :MODEL_WIDTH]
        grad = ins[0][:, MODEL_WIDTH : 2 * MODEL_WIDTH]
        mask = ins[0][:, 2 * MODEL_WIDTH :]
    else:
        x = ins[0][...]
        grad = ins[1][:, :MODEL_WIDTH]
        mask = ins[1][:, MODEL_WIDTH:]
    chosen = mask.astype(f32) > 0.0
    logits = jnp.where(chosen, dot(x, router_ref[...]), masked_score)
    expo = jnp.where(chosen, jnp.exp(logits - jnp.max(logits, axis=-1, keepdims=True)), 0.0)
    gates = (expo / jnp.sum(expo, axis=-1, keepdims=True)).astype(bf16)
    earlier = lax.broadcasted_iota(jnp.int32, (rows, rows), 1) < lax.broadcasted_iota(
        jnp.int32, (rows, rows), 0
    )
    place = dot(jnp.where(earlier, 1.0, 0.0).astype(bf16), mask)
    place = jnp.where(chosen, place, -1.0).astype(bf16)
    offset = offset_ref[0]

    def pick(shape, slot_axis):
        slot = lax.broadcasted_iota(jnp.int32, shape, slot_axis)
        expert = lax.broadcasted_iota(jnp.int32, shape, 1 - slot_axis)
        hit = jnp.zeros(shape, jnp.bool_)
        for own in range(local):
            hit = hit | (
                (slot >= own * CAP) & (slot < (own + 1) * CAP) & (expert == offset + own)
            )
        return jnp.where(hit, 1.0, 0.0).astype(bf16)

    def in_slot(shape, slot_axis):
        slot = lax.broadcasted_iota(jnp.int32, shape, slot_axis)
        for own in range(1, local):
            slot = jnp.where(slot >= CAP, slot - CAP, slot)
        return slot.astype(f32)

    spread = pick((slots, LANES), 0)
    hit = dot_nt(spread, place) == in_slot((slots, rows), 0)
    send = jnp.where(hit, 1.0, 0.0).astype(bf16)
    send_gated = jnp.where(hit, dot_nt(spread, gates), 0.0).astype(bf16)
    xd_ref[...] = dot(send, x).astype(bf16).reshape(xd_ref.shape)
    gd_ref[...] = ((dot(send_gated, grad) * residual_scale).astype(bf16)).reshape(gd_ref.shape)
    spread = pick((LANES, slots), 1)
    hit = dot(place, spread) == in_slot((rows, slots), 1)
    pt_ref[...] = jnp.where(hit, 1.0, 0.0).astype(bf16)
    pgt_ref[...] = jnp.where(hit, dot(gates, spread), 0.0).astype(bf16)


def dispatch(offset, sources, router, local):
    total = sources[0].shape[0]
    blocks = total // ROW_BLOCK
    slots = local * CAP
    slotted = jax.ShapeDtypeStruct((local, blocks, CAP, MODEL_WIDTH), bf16)
    slotted_spec = pl.BlockSpec((local, 1, CAP, MODEL_WIDTH), lambda s, o: (0, s, 0, 0))
    return pl.pallas_call(
        functools.partial(dispatch_body, local=local, count=len(sources)),
        grid_spec=pltpu.PrefetchScalarGridSpec(
            num_scalar_prefetch=1,
            grid=(blocks,),
            in_specs=[
                pl.BlockSpec((ROW_BLOCK, source.shape[1]), lambda s, o: (s, 0))
                for source in sources
            ]
            + [pl.BlockSpec((MODEL_WIDTH, LANES), lambda s, o: (0, 0))],
            out_specs=[
                slotted_spec,
                slotted_spec,
                pl.BlockSpec((ROW_BLOCK, slots), lambda s, o: (s, 0)),
                pl.BlockSpec((ROW_BLOCK, slots), lambda s, o: (s, 0)),
            ],
        ),
        out_shape=(
            slotted,
            slotted,
            jax.ShapeDtypeStruct((total, slots), bf16),
            jax.ShapeDtypeStruct((total, slots), bf16),
        ),
        compiler_params=row_params,
        cost_estimate=cost(11.0, 40.0),
        name="dispatch",
    )(offset, *sources, router)


def pack_weights(gate_up, down):
    gu_rows = gate_up.shape[1]
    count = MODEL_WIDTH // gu_rows
    cut = FF // count
    side = [down[:, k * cut : (k + 1) * cut, :] for k in range(count)]
    return jnp.concatenate([gate_up, jnp.concatenate(side, axis=2)], axis=1)


def unpack_weights(packed, gu_rows):
    count = MODEL_WIDTH // gu_rows
    side = packed[:, gu_rows:]
    side = [side[:, :, k * gu_rows : (k + 1) * gu_rows] for k in range(count)]
    return packed[:, :gu_rows], jnp.concatenate(side, axis=1)


def experts_body(place_ref, xd_ref, gd_ref, *refs, base, slices, carried):
    paired = slices == 4
    kinds = 5 if paired else 1
    w_refs, refs = refs[:kinds], refs[kinds:]
    old, refs = (refs[:kinds], refs[kinds:]) if carried else ((), refs)
    out_ref, dx_ref, h_ref = refs[:3]
    grad_refs = refs[3 : 3 + kinds]
    wgu_ref, wd_ref, act_sc, dh_sc = refs[3 + kinds :]
    expert = pl.program_id(0)
    gu_rows = MODEL_WIDTH // slices
    cut = FF // slices

    def begin_of(index):
        if not paired:
            return index * gu_rows
        return pl.multiple_of(place_ref[1 + index] * gu_rows, LANES)

    def put(index, ref, *lead):
        begin = begin_of(index)
        wgu_ref[pl.ds(begin, gu_rows), :] = ref[(*lead, slice(0, gu_rows), slice(None))]
        for k in range(slices):
            wd_ref[k * cut : (k + 1) * cut, pl.ds(begin, gu_rows)] = ref[
                (*lead, slice(gu_rows, gu_rows + cut), slice(k * gu_rows, (k + 1) * gu_rows))
            ]

    if paired:
        for index in range(3):
            put(index, w_refs[index], 0)

        @pl.when(expert == 0)
        def _():
            put(3, w_refs[3], 0)

        @pl.when(expert == 1)
        def _():
            put(3, w_refs[4], 0)

    else:
        for index in range(slices):
            put(index, w_refs[0], index, 0)

    total = xd_ref.shape[1]
    chunk = ROW_BLOCK
    own = place_ref[0] + expert + base
    lane = lax.broadcasted_iota(jnp.int32, (chunk, LANES), 1)

    def chunk_step(index):
        rows = block_rows(index)
        hidden = dot(xd_ref[0, rows, :], wgu_ref[...])
        gate = hidden[:, :FF]
        up = hidden[:, FF:]
        sigmoid = jax.nn.sigmoid(gate)
        act = (gate * sigmoid * up).astype(bf16)
        act_sc[rows, :] = act
        out = dot(act, wd_ref[...]).astype(bf16)
        out_ref[0, rows, :] = out
        grad_out = gd_ref[0, rows, :]
        h = jnp.sum(grad_out.astype(f32) * out.astype(f32), axis=-1, keepdims=True)
        h_ref[0, rows, :] = jnp.where(lane == own, h, 0.0).astype(bf16)
        grad_act = dot_nt(grad_out, wd_ref[...])
        grad_gate = grad_act * up * sigmoid * (1.0 + gate * (1.0 - sigmoid))
        grad_up = grad_act * gate * sigmoid
        dh_sc[rows, :FF] = grad_gate.astype(bf16)
        dh_sc[rows, FF:] = grad_up.astype(bf16)
        dx_ref[0, rows, :] = dot_nt(dh_sc[rows, :], wgu_ref[...]).astype(bf16)

    def loop_step(index, carry):
        chunk_step(index)
        return carry

    lax.fori_loop(0, total // chunk, loop_step, 0)

    def put_grad(kind, lead, gate_up, down):
        ref = grad_refs[kind]
        at = (*lead, slice(0, gu_rows), slice(None))
        if carried:
            gate_up = gate_up + old[kind][at].astype(f32)
        ref[at] = gate_up.astype(bf16)
        for k in range(slices):
            at = (*lead, slice(gu_rows, gu_rows + cut), slice(k * gu_rows, (k + 1) * gu_rows))
            value = down[k * cut : (k + 1) * cut, :]
            if carried:
                value = value + old[kind][at].astype(f32)
            ref[at] = value.astype(bf16)

    targets = (
        ((0, 0), (1, 0), (3, 0), (1, 1)),
        ((0, 1), (4, 0), (2, 0), (2, 1)),
    )
    for index in range(slices):
        begin = begin_of(index)
        gate_up = dot_tn(xd_ref[0, :, pl.ds(begin, gu_rows)], dh_sc[...])
        down = dot_tn(act_sc[...], gd_ref[0, :, pl.ds(begin, gu_rows)])
        if not paired:
            put_grad(0, (index, 0), gate_up, down)
            continue

        @pl.when(expert == 0)
        def _():
            kind, lead = targets[0][index]
            put_grad(kind, (lead,), gate_up, down)

        @pl.when(expert == 1)
        def _():
            kind, lead = targets[1][index]
            put_grad(kind, (lead,), gate_up, down)


def run_experts(place, xd, gd, pieces, old, base, here, slices):
    total = xd.shape[1]
    paired = slices == 4
    packed = (MODEL_WIDTH + FF) // slices

    def spec(rows, width, first=0):
        return pl.BlockSpec((1, rows, width), lambda e, o: (e + first, 0, 0))

    def fixed(count):
        return pl.BlockSpec((count, packed, MODEL_WIDTH), lambda e, o: (0, 0, 0))

    if paired:
        w_specs = [spec(packed, MODEL_WIDTH)] * 3 + [fixed(1)] * 2
        counts = (2, 2, 2, 1, 1)
        grad_specs = [fixed(count) for count in counts]
        grad_shapes = tuple(
            jax.ShapeDtypeStruct((count, packed, MODEL_WIDTH), bf16) for count in counts
        )
    else:
        w_specs = [pl.BlockSpec((slices, 1, packed, MODEL_WIDTH), lambda e, o: (0, e, 0, 0))]
        grad_specs = w_specs
        grad_shapes = (jax.ShapeDtypeStruct((slices, here, packed, MODEL_WIDTH), bf16),)
    results = pl.pallas_call(
        functools.partial(experts_body, base=base, slices=slices, carried=bool(old)),
        grid_spec=pltpu.PrefetchScalarGridSpec(
            num_scalar_prefetch=1,
            grid=(here,),
            in_specs=[spec(total, MODEL_WIDTH, base)] * 2 + w_specs + (grad_specs if old else []),
            out_specs=[spec(total, MODEL_WIDTH)] * 2 + [spec(total, LANES)] + grad_specs,
            scratch_shapes=[
                pltpu.VMEM((MODEL_WIDTH, 2 * FF), bf16),
                pltpu.VMEM((FF, MODEL_WIDTH), bf16),
                pltpu.VMEM((total, FF), bf16),
                pltpu.VMEM((total, 2 * FF), bf16),
            ],
        ),
        out_shape=(
            jax.ShapeDtypeStruct((here, total, MODEL_WIDTH), bf16),
            jax.ShapeDtypeStruct((here, total, MODEL_WIDTH), bf16),
            jax.ShapeDtypeStruct((here, total, LANES), bf16),
        )
        + grad_shapes,
        compiler_params=row_params,
        cost_estimate=cost(20.0, 60.0),
        name="experts",
    )(place, xd, gd, *pieces, *old)
    return results[:3], results[3:]


def whole_slots(refs, slots, width):
    return jnp.concatenate(
        [ref[...].reshape(slots // len(refs), width) for ref in refs], axis=0
    )


def combine_grad_body(*refs, count):
    dx_refs, h_refs, (pt_ref, grad_ref) = refs[:count], refs[count : 2 * count], refs[2 * count :]
    slots = pt_ref.shape[1]
    grad_ref[:, :MODEL_WIDTH] = dot(
        pt_ref[...], whole_slots(dx_refs, slots, MODEL_WIDTH)
    ).astype(bf16)
    grad_ref[:, MODEL_WIDTH:] = dot(pt_ref[...], whole_slots(h_refs, slots, LANES)).astype(bf16)


def combine_mix_body(*refs, count):
    out_refs, (pgt_ref, mix_ref) = refs[:count], refs[count:]
    mix_ref[...] = dot(
        pgt_ref[...], whole_slots(out_refs, pgt_ref.shape[1], MODEL_WIDTH)
    ).astype(bf16)


def combine_both_body(*refs, count):
    out_refs, dx_refs, refs = refs[:count], refs[count : 2 * count], refs[2 * count :]
    h_refs, (pgt_ref, pt_ref, both_ref) = refs[:count], refs[count:]
    slots = pt_ref.shape[1]
    both_ref[:, :MODEL_WIDTH] = dot(
        pgt_ref[...], whole_slots(out_refs, slots, MODEL_WIDTH)
    ).astype(bf16)
    both_ref[:, MODEL_WIDTH : 2 * MODEL_WIDTH] = dot(
        pt_ref[...], whole_slots(dx_refs, slots, MODEL_WIDTH)
    ).astype(bf16)
    both_ref[:, 2 * MODEL_WIDTH :] = dot(
        pt_ref[...], whole_slots(h_refs, slots, LANES)
    ).astype(bf16)


def combine(body, arrays, count, tables, width, name):
    total, slots = tables[0].shape
    blocks = total // ROW_BLOCK
    arrays = [array.reshape(array.shape[0], blocks, CAP, array.shape[-1]) for array in arrays]
    in_specs = [
        pl.BlockSpec((array.shape[0], 1, CAP, array.shape[-1]), lambda s: (0, s, 0, 0))
        for array in arrays
    ]
    return pl.pallas_call(
        functools.partial(body, count=count),
        grid=(blocks,),
        in_specs=in_specs + [pl.BlockSpec((ROW_BLOCK, slots), lambda s: (s, 0))] * len(tables),
        out_specs=pl.BlockSpec((ROW_BLOCK, width), lambda s: (s, 0)),
        out_shape=jax.ShapeDtypeStruct((total, width), bf16),
        compiler_params=row_params,
        cost_estimate=cost(5.0, 17.0),
        name=name,
    )(*arrays, *tables)


def flip(value, bits):
    return lax.ppermute(value, "tp", [(t, t ^ bits) for t in range(4)])


def square():
    return lax.axis_size("tp") == 4


def tp_places():
    me = lax.axis_index("tp").astype(jnp.int32)
    if square():
        return jnp.stack([me ^ bits for bits in range(4)])
    return jnp.zeros((1,), jnp.int32)


def gather_rows(value):
    if square():
        return [value] + [flip(value, bits) for bits in (1, 2, 3)]
    return [lax.all_gather(value, "tp", axis=0, tiled=True)]


def send_rows(parts):
    if square():
        return [parts[0]] + [flip(parts[bits], bits) for bits in (1, 2, 3)]
    return [lax.psum_scatter(parts[0], "tp", scatter_dimension=0, tiled=True)]


def add_rows(came):
    total = came[0].astype(f32)
    for part in came[1:]:
        total = total + part.astype(f32)
    return total


def gather_weights_near(packed):
    if square():
        return [packed, flip(packed, 1), flip(packed, 2)]
    return [lax.all_gather(packed, "tp")]


def gather_weights_far(near):
    if square():
        return [*near, flip(near[2][:1], 1), flip(near[1][1:], 2)]
    return near


def sum_weights_near(grads):
    if square():
        return [flip(grads[1], 1), flip(grads[2], 2), *grads]
    return [lax.psum_scatter(grads[0], "tp", scatter_dimension=0)]


def far_sums_body(came_x, kept_y, came_y, kept_x, first, second):
    first[...] = (came_x[...].astype(f32) + kept_y[...].astype(f32)).astype(bf16)
    second[...] = (came_y[...].astype(f32) + kept_x[...].astype(f32)).astype(bf16)


def far_sums(near):
    if square():
        came_x, came_y, _, _, _, kept_y, kept_x = near
        block = (1, LANES, MODEL_WIDTH)
        second = pl.BlockSpec(block, lambda s: (1, s, 0))
        only = pl.BlockSpec(block, lambda s: (0, s, 0))
        return pl.pallas_call(
            far_sums_body,
            grid=(kept_y.shape[1] // LANES,),
            in_specs=[second, only, second, only],
            out_specs=[only, only],
            out_shape=(jax.ShapeDtypeStruct(kept_y.shape, bf16),) * 2,
            compiler_params=row_params,
            cost_estimate=cost(0.1, 5.0),
            name="far_sums",
        )(came_x, kept_y, came_y, kept_x)
    return []


def send_far(sums):
    if square():
        return [flip(sums[0], 2), flip(sums[1], 1)]
    return []


def weight_sums_body(*refs, gu_rows):
    halves, (gate_up_ref, down_ref) = refs[:-2], refs[-2:]
    cut = FF * gu_rows // MODEL_WIDTH
    expert = 0
    for at in range(0, len(halves), 5):
        came_x, came_y, own, far_first, far_second = halves[at : at + 5]
        for near, mine, far in ((came_x, 0, far_first), (came_y, 1, far_second)):
            total = near[0].astype(f32) + own[mine].astype(f32) + far[0].astype(f32)
            gate_up_ref[expert] = total[:gu_rows]
            for k in range(MODEL_WIDTH // gu_rows):
                down_ref[expert, k * cut : (k + 1) * cut, :] = total[
                    gu_rows:, k * gu_rows : (k + 1) * gu_rows
                ]
            expert += 1


def weight_sums(halves, gu_rows):
    if square():
        arrays = [array for near, far in halves for array in (*near[:3], *far)]
        experts = 2 * len(halves)
        return pl.pallas_call(
            functools.partial(weight_sums_body, gu_rows=gu_rows),
            out_shape=(
                jax.ShapeDtypeStruct((experts, gu_rows, 2 * FF), f32),
                jax.ShapeDtypeStruct((experts, FF, gu_rows), f32),
            ),
            compiler_params=params,
            cost_estimate=cost(0.1, 5.0),
            name="weight_sums",
        )(*arrays)
    return unpack_weights(
        jnp.concatenate([near[0].astype(f32) for near, _ in halves]), gu_rows
    )


def ag_ep(value, axis=0):
    return lax.all_gather(value, "ep", axis=axis, tiled=True)


def rs_ep(value, axis=0):
    return lax.psum_scatter(value, "ep", scatter_dimension=axis, tiled=True)


def rope_tables(segment_row):
    onehot = (segment_row[:, None] == jnp.arange(DOCS, dtype=jnp.int32)[None, :]).astype(jnp.int32)
    doc_len = jnp.sum(onehot, axis=0)
    starts = [jnp.sum(doc_len[:doc]) for doc in range(DOCS)]
    begin = jnp.zeros_like(segment_row)
    for doc in range(1, DOCS):
        begin = jnp.where(segment_row == doc, starts[doc], begin)
    positions = jnp.arange(segment_row.shape[0], dtype=jnp.int32) - begin
    lane = jnp.arange(LANES, dtype=jnp.int32)
    halves = HEAD_SIZE // 2
    freqs = rope_base ** (-((lane % halves).astype(f32) * 2.0) / HEAD_SIZE)
    angles = positions.astype(f32)[:, None] * freqs[None, :]
    sign = jnp.where((lane % HEAD_SIZE) < halves, -1.0, 1.0).astype(f32)
    return jnp.cos(angles), jnp.sin(angles) * sign[None, :]


def shards(
    tokens,
    cotangent,
    norm_gains,
    query_key_value_weight,
    output_weight,
    w_router,
    w_gate_up,
    w_down,
    segment_ids,
    routes,
):
    micro, rows = tokens.shape[:2]
    local_heads = query_key_value_weight.shape[1]
    local = w_gate_up.shape[0]
    ep_size = lax.axis_size("ep")
    offset = (lax.axis_index("ep") * local).astype(jnp.int32).reshape(1)
    places = tp_places()
    starts = places * ROW_BLOCK
    place = jnp.concatenate([offset, places])
    gain_one = norm_gains[0:1]
    gain_two = norm_gains[1:2]
    router = jnp.pad(w_router, ((0, 0), (0, LANES - EXPERTS)))

    slices = lax.axis_size("tp")
    weights = ag_ep(
        jnp.concatenate(
            [
                query_key_value_weight.reshape(query_key_value_weight.shape[0], -1),
                output_weight.reshape(-1, output_weight.shape[2]).T,
            ],
            axis=1,
        )
    )
    lanes = jnp.arange(LANES, dtype=jnp.int32)
    masks = jnp.any(
        routes.reshape(micro, rows, -1)[..., None] == lanes, axis=2
    ).astype(bf16)
    tables = [rope_tables(segment_ids[m]) for m in range(micro)]
    packed_weights = pack_weights(w_gate_up, w_down)
    here = local // 2
    halves = range(2)
    packed_weights = [packed_weights[h * here : (h + 1) * here] for h in halves]

    token_full = []
    for m in range(micro):
        own = after(tokens[m], token_full[-1], tables) if token_full else tokens[m]
        token_full.append(gather_rows(own))
    weights = after(weights, token_full[0], tables)
    fixed = []
    for m in range(micro):
        fixed.append(
            (
                starts, token_full[m], gain_one, weights, tables[m][0], tables[m][1],
                segment_ids[m][:, None], segment_ids[m][None, :],
            )
        )
    came = []
    kept = []
    for m in range(micro):
        if m:
            fixed[m] = (after(starts, parts), token_full[m], *fixed[m][2:])
        parts, saved = attention_forward(*fixed[m])
        kept.append(saved)
        if m == 0:
            parts, token_full = lax.optimization_barrier((parts, token_full))
        if m == micro - 1:
            came[0] = after(came[0], parts)
        came.append(send_rows(parts))

    hiddens = []
    normed_twos = []
    scales = []
    gate_rows = []
    full = []
    for m in range(micro):
        if m == 0:
            near = [gather_weights_near(after(packed_weights[0], came[0]))]
        branch = add_rows(came[m])
        hidden = tokens[m].astype(f32) + residual_scale * branch
        scale_two = lax.rsqrt(jnp.mean(hidden * hidden, axis=-1, keepdims=True) + epsilon)
        normed_two = (hidden * scale_two * gain_two).astype(bf16)
        logits = jnp.where(masks[m] > 0, dot(normed_two, router), masked_score)
        expo = jnp.where(
            masks[m] > 0, jnp.exp(logits - jnp.max(logits, axis=-1, keepdims=True)), 0.0
        )
        gate_rows.append(expo / jnp.sum(expo, axis=-1, keepdims=True))
        hiddens.append(hidden)
        normed_twos.append(normed_two)
        scales.append(scale_two)
        if m == 0:
            gm = jnp.concatenate([cotangent[m], masks[m]], axis=-1)
            gm = ag_ep(after(gm, weights))
            full.append([ag_ep(after(normed_two, gm)), gm])
        else:
            if m == micro - 1:
                normed_two, near[0] = lax.optimization_barrier((normed_two, near[0]))
            full.append([ag_ep(jnp.concatenate([normed_two, cotangent[m], masks[m]], axis=-1))])

    pieces = [gather_weights_far(near[0])]
    old = [(), ()]
    mixes = []
    grads = []
    ready = ()
    for m in range(micro):
        sources = after(full[m], ready) if m else full[m]
        xd, gd, pt, pgt = dispatch(offset, sources, router, local)
        if m == 0:
            near.append(gather_weights_near(after(packed_weights[1], pieces[0], xd)))
        merged = (local, ep_size * CAP, MODEL_WIDTH)
        xd = xd.reshape(merged)
        gd = gd.reshape(merged)
        done = []
        for h in halves:
            results, old[h] = run_experts(
                place, xd, gd, pieces[h], old[h], h * here, here, slices
            )
            done.append(results)
            if m == 0 and h == 0:
                near[1] = after(near[1], results)
                pieces.append(gather_weights_far(near[1]))
        outs, dxs, hs = zip(*done)
        if m < micro - 1:
            both = combine(
                combine_both_body, [*outs, *dxs, *hs], 2, [pgt, pt], 2 * MODEL_WIDTH + LANES,
                "combine",
            )
            ready = both
            both = rs_ep(both)
            mixes.append(both[:, :MODEL_WIDTH])
            grads.append(both[:, MODEL_WIDTH:])
        else:
            near_first = sum_weights_near(old[0])
            dxs, near_first = lax.optimization_barrier((dxs, near_first))
            grad = combine(
                combine_grad_body, [*dxs, *hs], 2, [pt], MODEL_WIDTH + LANES, "combine_grad"
            )
            grads.append(rs_ep(grad))
            outs, pgt = after((outs, pgt), grad)
            mix = combine(combine_mix_body, outs, 2, [pgt], MODEL_WIDTH, "combine_mix")
            mixes.append(rs_ep(mix))
            grads[0] = after(grads[0], mix)
    input_grads = []
    acc_router = 0.0
    acc_gain_one = 0.0
    acc_gain_two = 0.0
    acc_weights = 0.0
    parts = ()
    backs = []
    grad_hiddens = []
    for m in range(micro):
        grad = grads[m]
        if m:
            grad, near_second = after((grad, near_second), parts)
        grad = grad.astype(f32)
        h_rows = grad[:, MODEL_WIDTH:]
        grad_logits = (
            h_rows - gate_rows[m] * jnp.sum(h_rows, axis=-1, keepdims=True)
        ).astype(bf16)
        acc_router = acc_router + dot_tn(normed_twos[m], grad_logits)
        grad_normed = grad[:, :MODEL_WIDTH] + dot_nt(grad_logits, router)
        scale = scales[m]
        weighted = grad_normed * gain_two
        inner = jnp.mean(weighted * hiddens[m], axis=-1, keepdims=True)
        grad_hidden = (
            cotangent[m].astype(f32)
            + scale * weighted
            - hiddens[m] * scale * scale * scale * inner
        )
        acc_gain_two = acc_gain_two + jnp.sum(grad_normed * hiddens[m] * scale, axis=0)
        grad_branch = (residual_scale * grad_hidden).astype(bf16)
        grad_branch = gather_rows(grad_branch)
        if m == 0:
            near_second = sum_weights_near(after(old[1], grad_branch))
        if m == micro - 1:
            far_first = send_far(after(far_sums(near_first), grad_branch))
            far_second = send_far(after(far_sums(near_second), grad_branch))
        parts, (gweights, ggain) = attention_backward(*fixed[m], kept[m], grad_branch)
        backs.append(parts)
        grad_hiddens.append(grad_hidden)
        if m == micro - 1:
            parts, gweights, ggain, far_first, mixes = lax.optimization_barrier(
                (parts, gweights, ggain, far_first, mixes)
            )
            backs[-1] = parts
        acc_weights = acc_weights + gweights.astype(f32)
        acc_gain_one = acc_gain_one + ggain[0]
    small = jnp.concatenate(
        [
            acc_router[:, :EXPERTS],
            acc_gain_one[:, None],
            acc_gain_two[:, None],
            jnp.zeros((MODEL_WIDTH, LANES - EXPERTS - 2), f32),
        ],
        axis=-1,
    ).astype(bf16)
    rows = MODEL_WIDTH // lax.axis_size("tp")
    if square():
        small = add_rows(
            send_rows(
                [lax.dynamic_slice_in_dim(small, places[k] * rows, rows) for k in range(4)]
            )
        ).astype(bf16)
    else:
        small = lax.psum_scatter(small, "tp", scatter_dimension=0, tiled=True)
    columns = acc_weights.shape[1]
    own_rows = MODEL_WIDTH // ep_size
    small_rows = rows // ep_size
    small = small.reshape(ep_size, small_rows * LANES)
    extra = -(-small.shape[1] // (8 * columns)) * 8
    small = jnp.pad(small, ((0, 0), (0, extra * columns - small.shape[1])))
    packed = jnp.concatenate(
        [
            acc_weights.astype(bf16).reshape(ep_size, own_rows, columns),
            small.reshape(ep_size, extra, columns),
        ],
        axis=1,
    )
    packed = packed.reshape(-1, columns)
    summed = rs_ep(packed).astype(f32)
    hiddens, mixes, far_first, far_second = after((hiddens, mixes, far_first, far_second), packed)
    backs = [send_rows(after(parts, packed)) for parts in backs]
    for m in range(micro):
        grad_normed = add_rows(backs[m])
        inputs = tokens[m].astype(f32)
        scale = lax.rsqrt(jnp.mean(inputs * inputs, axis=-1, keepdims=True) + epsilon)
        weighted = grad_normed * gain_one
        inner = jnp.mean(weighted * inputs, axis=-1, keepdims=True)
        input_grads.append(
            grad_hiddens[m] + scale * weighted - inputs * scale * scale * scale * inner
        )
    outputs = [
        (hiddens[m] + residual_scale * mixes[m].astype(f32)).astype(bf16) for m in range(micro)
    ]
    grad_gate_up, grad_down = weight_sums(
        [(near_first, far_first), (near_second, far_second)], w_gate_up.shape[1]
    )
    split = local_heads * GROUP_COLS
    grad_qkv = summed[:own_rows, :split].reshape(own_rows, local_heads, GROUP_COLS)
    grad_out = summed[:own_rows, split:].T.reshape(local_heads, LANES, own_rows)
    small = summed[own_rows:].reshape(-1)[: small_rows * LANES].reshape(small_rows, LANES)
    grad_router = small[:, :EXPERTS]
    grad_gains = small[:, EXPERTS : EXPERTS + 2].T
    return (
        jnp.stack(outputs),
        jnp.stack(input_grads),
        grad_gains,
        grad_qkv,
        grad_out,
        grad_router,
        grad_gate_up,
        grad_down,
    )


def solution(mesh):
    placed = (
        P("ep", "tp", None),
        P("ep", "tp", None),
        P(),
        P("ep", "tp", None),
        P("tp", None, "ep"),
        P(),
        P("ep", "tp", None),
        P("ep", None, "tp"),
        P("ep", None),
        P("ep", "tp", None, None),
    )
    return jax.shard_map(
        shards,
        mesh=mesh,
        in_specs=placed,
        out_specs=(
            P("ep", "tp", None),
            P("ep", "tp", None),
            P(None, ("tp", "ep")),
            P("ep", "tp", None),
            P("tp", None, "ep"),
            P(("tp", "ep"), None),
            P("ep", "tp", None),
            P("ep", None, "tp"),
        ),
        check_vma=False,
    )
```
